256 devices in a mesh: row: 32 (over z_hi, x, core), col: 8 (over y, z_lo).
Axes of the slice: x: 4, y: 4, z: 8 (z_hi: 4, z_lo: 2; z = z_hi * 2 + z_lo), core: 2. Of those that a mesh axis runs over, the one named last changes fastest.
Arguments:
- ocean_field: bfloat16 [32, 2048, 2048], P(None, 'row', 'col'), may hold values from -6 to 6
- cotangent: bfloat16 [2048, 2048], P('row', 'col'), may hold values from -6 to 6
- conv_weight: bfloat16 [3, 3, 32, 32], replicated, may hold values from -0.375 to 0.375
- conv_bias: float32 [32], replicated, may hold values from -3 to 3
- projection: float32 [32], replicated, may hold values from -4 to 4
- mode_weight: bfloat16 [128, 2, 32, 32, 256], P('row', None, None, None, 'col'), may hold values from -4.5 to 4.5
Outputs:
- grad_input: float32 [32, 2048, 2048], P(None, 'row', 'col')
- grad_spec: float32 [128, 2, 32, 32, 256], P('row', None, None, None, 'col')
- grad_conv: float32 [3, 3, 32, 32], replicated
- grad_bias: float32 [32], replicated
- grad_proj: float32 [32], replicated
The draws below stay inside these ranges and needn't reach their ends.
All inputs are finite; a program needn't handle non-finite values.
Results may differ from the reference program's by a relative error of at most 0.0062.
Values may be sent and summed in bfloat16 or wider, within the bound.
A program may use at most 128 MiB of HBM per device.

```python
import math
import jax
import jax.numpy as jnp
from jax import lax

C = 32
M = 128
RX = 64
KX = 256
NX = 2048
NY = 2048
N_ROW = 32


def shard_levels(own_key, extent, pieces, smallest, top_value):
    def one(dim, blocks):
        heights = jax.random.uniform(jax.random.fold_in(jax.random.fold_in(own_key, 6), dim), (blocks,), jnp.float32, smallest / len(pieces), top_value / len(pieces))
        return jnp.repeat(jnp.exp(heights), extent[dim] // blocks).reshape((-1,) + (1,) * (len(extent) - dim - 1))

    level = one(*pieces[0])
    for cut in pieces[1:]:
        level = level * one(*cut)
    return level


def centred(stream_key, extent, deviation, most, split=(), kind=jnp.bfloat16):
    factor_of = shard_levels(stream_key, extent, split, -0.22, 0.18) if split else 1.0
    values = jax.random.normal(stream_key, extent, jnp.float32) * deviation * factor_of
    return jnp.minimum(jnp.maximum(values, -most), most).astype(kind)


def setup_inputs(seed: int = 0) -> dict:
    seeds = jax.random.split(jax.random.key(seed), 7)
    ocean_field = centred(seeds[0], (C, NX, NY), 1.0, 6.0, ((1, 32), (2, 8)))
    cotangent = centred(seeds[1], (NX, NY), 1.0, 6.0, ((0, 32), (1, 8)))
    conv_weight = centred(seeds[2], (3, 3, C, C), (9 * C) ** -0.5, 0.375)
    conv_bias = centred(seeds[3], (C,), 0.5, 3.0, (), jnp.float32)
    projection = centred(seeds[4], (C,), 1.0, 4.0, (), jnp.float32)
    mode_weight = centred(seeds[5], (M, 2, C, C, KX), 0.75, 4.5, ((0, 32), (4, 8)))
    return {"ocean_field": ocean_field, "cotangent": cotangent, "conv_weight": conv_weight, "conv_bias": conv_bias, "projection": projection, "mode_weight": mode_weight}


TWO_PI = 2.0 * math.pi
HIGH = lax.Precision.HIGHEST

def angle_pair(products, period):
    angles = (products % period).astype(jnp.float32) * (TWO_PI / period)
    return (jnp.cos(angles).astype(jnp.bfloat16), jnp.sin(angles).astype(jnp.bfloat16))

def column_table(col_ids, modes, period):
    freqs = jnp.arange(modes, dtype=jnp.int32)
    cosine, sine = angle_pair(freqs[:, None] * col_ids[None, :], period)
    return jnp.stack([cosine, -sine], axis=1)

def row_tables(row_ids, kx_ids, modes, period):
    freqs = jnp.where(kx_ids < modes, kx_ids, kx_ids - 2 * modes) % period
    return angle_pair(row_ids[:, None] * freqs[None, :], period)

def row_section(partial_value, row_ids, kx_ids, modes, period):
    cosine, sine = row_tables(row_ids, kx_ids, modes, period)
    with_cos = jnp.einsum('kpcx,xj->kpcj', partial_value, cosine.astype(jnp.float32), precision=HIGH)
    with_sin = jnp.einsum('kpcx,xj->kpcj', partial_value, sine.astype(jnp.float32), precision=HIGH)
    return jnp.stack([with_cos[:, 0] + with_sin[:, 1], with_cos[:, 1] - with_sin[:, 0]], axis=1)

def forward_transform(field):
    table = column_table(jnp.arange(NY, dtype=jnp.int32), M, NY).astype(jnp.float32)

    def per_channel(plane):
        return jnp.einsum('xy,kpy->kpx', plane.astype(jnp.float32), table, precision=HIGH)
    partial_value = jnp.transpose(lax.map(per_channel, field), (1, 2, 0, 3))
    return row_section(partial_value, jnp.arange(NX, dtype=jnp.int32), jnp.arange(KX, dtype=jnp.int32), M, NX)

def inverse_rows(spectral, weights_ky, row_ids, scale):
    cosine, sine = row_tables(row_ids, jnp.arange(KX, dtype=jnp.int32), M, NX)
    spec_f = spectral.astype(jnp.float32)
    with_cos = jnp.einsum('kpcj,xj->kpcx', spec_f, cosine.astype(jnp.float32), precision=HIGH)
    with_sin = jnp.einsum('kpcj,xj->kpcx', spec_f, sine.astype(jnp.float32), precision=HIGH)
    summed = jnp.stack([with_cos[:, 0] - with_sin[:, 1], with_cos[:, 1] + with_sin[:, 0]], axis=1)
    table = column_table(jnp.arange(NY, dtype=jnp.int32), M, NY).astype(jnp.float32)
    weighted = summed * weights_ky[:, None, None, None]
    return scale * jnp.einsum('kpcx,kpy->cxy', weighted, table, precision=HIGH)

def mix_modes(spectrum, weight):
    wf = weight.astype(jnp.float32)
    real_part = jnp.einsum('kij,kioj->koj', spectrum[:, 0], wf[:, 0], precision=HIGH) - jnp.einsum('kij,kioj->koj', spectrum[:, 1], wf[:, 1], precision=HIGH)
    imag_part = jnp.einsum('kij,kioj->koj', spectrum[:, 1], wf[:, 0], precision=HIGH) + jnp.einsum('kij,kioj->koj', spectrum[:, 0], wf[:, 1], precision=HIGH)
    return jnp.stack([real_part, imag_part], axis=1)

def mix_back(spectrum, weight, grad_mixed):
    wf = weight.astype(jnp.float32)
    spec_re, spec_im = (spectrum[:, 0], spectrum[:, 1])
    grad_re, grad_im = (grad_mixed[:, 0], grad_mixed[:, 1])
    weight_re = grad_re[:, None, :, :] * spec_re[:, :, None, :] + grad_im[:, None, :, :] * spec_im[:, :, None, :]
    weight_im = grad_im[:, None, :, :] * spec_re[:, :, None, :] - grad_re[:, None, :, :] * spec_im[:, :, None, :]
    back_re = jnp.einsum('kioj,koj->kij', wf[:, 0], grad_re, precision=HIGH) + jnp.einsum('kioj,koj->kij', wf[:, 1], grad_im, precision=HIGH)
    back_im = jnp.einsum('kioj,koj->kij', wf[:, 0], grad_im, precision=HIGH) - jnp.einsum('kioj,koj->kij', wf[:, 1], grad_re, precision=HIGH)
    return (jnp.stack([weight_re, weight_im], axis=1), jnp.stack([back_re, back_im], axis=1).astype(jnp.bfloat16))

def gelu_parts(pre):
    cdf = 0.5 * (1.0 + jax.scipy.special.erf(pre / math.sqrt(2.0)))
    pdf = jnp.exp(-0.5 * pre * pre) / math.sqrt(TWO_PI)
    return (pre * cdf, cdf + pre * pdf)

def conv_cells(window, kernel):
    n_rows = window.shape[1] - 2
    n_cols = window.shape[2] - 2
    kernel_f = kernel.astype(jnp.float32)
    result = jnp.zeros((window.shape[0], n_rows, n_cols), jnp.float32)
    for tap_row in range(3):
        for tap_col in range(3):
            shifted = window[:, tap_row:tap_row + n_rows, tap_col:tap_col + n_cols].astype(jnp.float32)
            result = result + jnp.einsum('io,ixy->oxy', kernel_f[tap_row, tap_col], shifted, precision=HIGH)
    return result

def conv_transpose(window, kernel):
    n_rows = window.shape[1] - 2
    n_cols = window.shape[2] - 2
    kernel_f = kernel.astype(jnp.float32)
    result = jnp.zeros((window.shape[0], n_rows, n_cols), jnp.float32)
    for tap_row in range(3):
        for tap_col in range(3):
            shifted = window[:, 2 - tap_row:2 - tap_row + n_rows, 2 - tap_col:2 - tap_col + n_cols].astype(jnp.float32)
            result = result + jnp.einsum('io,oxy->ixy', kernel_f[tap_row, tap_col], shifted, precision=HIGH)
    return result

def kernel_grad(window, grad_round):
    n_rows = grad_round.shape[1]
    n_cols = grad_round.shape[2]
    grad_f = grad_round.astype(jnp.float32)
    taps = []
    for tap_row in range(3):
        for tap_col in range(3):
            shifted = window[:, tap_row:tap_row + n_rows, tap_col:tap_col + n_cols].astype(jnp.float32)
            taps.append(jnp.einsum('ixy,oxy->io', shifted, grad_f, precision=HIGH))
    return jnp.stack(taps).reshape(3, 3, window.shape[0], grad_round.shape[0])

def reference(ocean_field, cotangent, conv_weight, conv_bias, projection, mode_weight):
    scale = 1.0 / math.sqrt(NX * NY)
    ky_weight = jnp.where(jnp.arange(M) == 0, 1.0, 2.0).astype(jnp.float32)
    spectrum = forward_transform(ocean_field) * scale
    mixed = mix_modes(spectrum, mode_weight).astype(jnp.bfloat16)
    padded_in = jnp.pad(ocean_field, ((0, 0), (1, 1), (1, 1)))
    zero_idx = jnp.zeros((), jnp.int32)

    def forward_block(block_id):
        first = (block_id * RX).astype(jnp.int32)
        window_in = lax.dynamic_slice(padded_in, (zero_idx, first, zero_idx), (C, RX + 2, NY + 2))
        row_ids = first + jnp.arange(RX, dtype=jnp.int32)
        pre_act = conv_cells(window_in, conv_weight) + inverse_rows(mixed, ky_weight, row_ids, scale) + conv_bias[:, None, None]
        activ, slope = gelu_parts(pre_act)
        cot_rows = lax.dynamic_slice(cotangent, (first, zero_idx), (RX, NY)).astype(jnp.float32)
        grad_pre = projection[:, None, None] * cot_rows[None] * slope
        grad_round = grad_pre.astype(jnp.bfloat16)
        return (grad_round, kernel_grad(window_in, grad_round), lax.optimization_barrier(jnp.sum(grad_pre, axis=(1, 2))), lax.optimization_barrier(jnp.sum(activ * cot_rows[None], axis=(1, 2))))
    grad_blocks, kernel_parts, bias_parts, proj_parts = lax.map(forward_block, jnp.arange(N_ROW, dtype=jnp.int32))
    grad_round = jnp.transpose(grad_blocks, (1, 0, 2, 3)).reshape(C, NX, NY)
    grad_conv = lax.optimization_barrier(jnp.sum(kernel_parts, axis=0)) * scale
    grad_bias = lax.optimization_barrier(jnp.sum(bias_parts, axis=0)) * scale
    grad_proj = lax.optimization_barrier(jnp.sum(proj_parts, axis=0)) * scale
    grad_modes = forward_transform(grad_round) * (scale * ky_weight)[:, None, None, None]
    grad_spec, grad_spectrum = mix_back(spectrum, mode_weight, grad_modes)
    padded_grad = jnp.pad(grad_round, ((0, 0), (1, 1), (1, 1)))
    all_ones = jnp.ones((M,), jnp.float32)

    def backward_block(block_id):
        first = (block_id * RX).astype(jnp.int32)
        window_grad = lax.dynamic_slice(padded_grad, (zero_idx, first, zero_idx), (C, RX + 2, NY + 2))
        row_ids = first + jnp.arange(RX, dtype=jnp.int32)
        return conv_transpose(window_grad, conv_weight) + inverse_rows(grad_spectrum, all_ones, row_ids, scale)
    input_blocks = lax.map(backward_block, jnp.arange(N_ROW, dtype=jnp.int32))
    grad_input = jnp.transpose(input_blocks, (1, 0, 2, 3)).reshape(C, NX, NY)
    return (grad_input, grad_spec, grad_conv, grad_bias, grad_proj)
```

```python
import functools
import math

import jax
import jax.numpy as jnp
import ml_dtypes
import numpy as np
from jax import lax
from jax.experimental import pallas as pl
from jax.experimental.pallas import tpu as pltpu
from jax.sharding import PartitionSpec as P

TWO_PI = 2.0 * math.pi
VMEM_BYTES = 56 * 1024 * 1024


def with_halo(array, sides, width):
    for axis, dim in sides:
        devices, length = (lax.axis_size(axis), array.shape[dim])
        up = [(i, (i + 1) % devices) for i in range(devices - 1)]
        down = [(j, i) for i, j in up]
        last = lax.slice_in_dim(array, length - width, length, axis=dim)
        first = lax.slice_in_dim(array, 0, width, axis=dim)
        before = lax.ppermute(last, axis, up)
        after = lax.ppermute(first, axis, down)
        array = jnp.concatenate([before, array, after], axis=dim)
    return array


def angle_pair(products, period):
    angles = (products % period).astype(np.float32) * np.float32(TWO_PI / period)
    return (np.cos(angles).astype(ml_dtypes.bfloat16), np.sin(angles).astype(ml_dtypes.bfloat16))


def tables(n_row, n_col, ky_dev, rows_dev, cols_dev, kx_all):
    modes, nx, ny = (ky_dev * n_row, rows_dev * n_row, cols_dev * n_col)
    cosine, sine = angle_pair(np.arange(modes)[:, None] * np.arange(ny)[None, :], ny)
    ty = np.stack([cosine.reshape(n_row, ky_dev, ny), -sine.reshape(n_row, ky_dev, ny)], axis=1)
    ty = ty.reshape(2 * modes, n_col, cols_dev).transpose(1, 0, 2)
    ids = np.arange(kx_all)
    freqs = np.where(ids < modes, ids, ids - 2 * modes) % nx
    cosine, sine = angle_pair(freqs[:, None] * np.arange(nx)[None, :], nx)
    return np.ascontiguousarray(ty), np.concatenate([cosine, sine], axis=0)


NT = (((1,), (1,)), ((), ()))
NN = (((1,), (0,)), ((), ()))


def dot(a, b, dims):
    return lax.dot_general(a, b, dims, preferred_element_type=jnp.float32)


def exchange(axis, me, size, source, target, send_sem, recv_sem):
    def copy(step, peer, slot):
        return pltpu.make_async_remote_copy(
            src_ref=source(peer),
            dst_ref=target(slot),
            send_sem=send_sem.at[step],
            recv_sem=recv_sem.at[step],
            device_id={axis: peer},
            device_id_type=pl.DeviceIdType.MESH,
        )

    def start(step):
        copy(step, lax.rem(me + step, size), me).start()

    def wait_send(step):
        copy(step, lax.rem(me + step, size), me).wait_send()

    def wait_recv(step):
        origin = lax.rem(me + size - step, size)
        copy(step, lax.rem(me + step, size), origin).wait_recv()
        return origin

    return start, wait_send, wait_recv


def each(size, body):
    def step(index, carry):
        body(index)
        return carry

    lax.fori_loop(1, size, step, 0)


def part_swap(value, sign):
    rows = value.shape[0]
    is_real = (lax.broadcasted_iota(jnp.int32, value.shape, 0) & 4) == 0
    after = pltpu.roll(value, rows - 4, 0)
    before = pltpu.roll(value, 4, 0)
    return jnp.where(is_real, sign * after, -sign * before)


def chain_kernel(forward, n_row, n_col, *refs):
    if forward:
        (v_ref, w_ref, ty_ref, tx_ref, cells_ref, spec_ref, *scratch) = refs
    else:
        (v_ref, w_ref, ty_ref, tx_ref, spec_ref, cells_ref, gspec_ref, *scratch) = refs
    (buf1, acc, snd3, rcv3, rows_x, snd5, rcv5, modes_ref, mix_ref, snd7, rcv7, snd9, rcv9, snd10, rcv10,
     local_sem, s1, r1, s3, r3, s5, r5, s7, r7, s9, r9, s10, r10) = scratch
    row_at = lax.axis_index("row")
    col_at = lax.axis_index("col")
    pairs = n_row // 2
    scale = 1.0 / math.sqrt((64 * n_row) * (256 * n_col))

    own = pltpu.make_async_copy(v_ref.at[col_at], buf1.at[col_at], local_sem)
    own.start()
    barrier = pltpu.get_barrier_semaphore()
    each(n_col, lambda d: pl.semaphore_signal(
        barrier, inc=1, device_id={"col": lax.rem(col_at + d, n_col)}, device_id_type=pl.DeviceIdType.MESH))
    each(n_row, lambda d: pl.semaphore_signal(
        barrier, inc=1, device_id={"row": lax.rem(row_at + d, n_row)}, device_id_type=pl.DeviceIdType.MESH))
    pl.semaphore_wait(barrier, n_col - 1 + n_row - 1)

    start1, sent1, got1 = exchange("col", col_at, n_col, lambda i: v_ref.at[i], lambda i: buf1.at[i], s1, r1)
    each(n_col, start1)
    own.wait()
    acc[...] = dot(ty_ref[col_at], buf1[col_at], NT)

    def add_block(d):
        origin = got1(d)
        acc[...] += dot(ty_ref[origin], buf1[origin], NT)

    each(n_col, add_block)

    whole = acc[...]
    left = whole[:, :128].reshape(n_row, 8, 128)
    right = whole[:, 128:].reshape(n_row, 8, 128)
    snd3[...] = jnp.concatenate([left, right], axis=1).astype(jnp.bfloat16)
    start3, sent3, got3 = exchange("row", row_at, n_row, lambda i: snd3.at[i], lambda i: rcv3.at[i], s3, r3)
    each(n_row, start3)
    rcv3[row_at] = snd3[row_at]
    each(n_row, got3)

    low = lax.broadcasted_iota(jnp.int32, (16, 128), 1) < 64
    for s in range(pairs):
        first = rcv3[2 * s].astype(jnp.float32)
        second = rcv3[2 * s + 1].astype(jnp.float32)
        even = jnp.where(low, first, pltpu.roll(second, 64, 1))
        odd = jnp.where(low, pltpu.roll(first, 64, 1), second)
        rows_x[0:16, 128 * s : 128 * s + 128] = even.astype(jnp.bfloat16)
        rows_x[16:32, 128 * s : 128 * s + 128] = odd.astype(jnp.bfloat16)
    both = dot(rows_x[...], tx_ref[...], NT)
    coeffs = (both[:, :256] + part_swap(both[:, 256:], 1.0)) * scale
    coeffs = jnp.concatenate([coeffs[0:8], coeffs[16:24], coeffs[8:16], coeffs[24:32]], axis=0)
    snd5[0] = coeffs[:, :128].astype(jnp.bfloat16)
    snd5[1] = coeffs[:, 128:].astype(jnp.bfloat16)
    start5, sent5, got5 = exchange("col", col_at, n_col, lambda i: snd5.at[i // 4], lambda i: rcv5.at[i], s5, r5)
    each(n_col, start5)
    rcv5[col_at] = snd5[col_at // 4]
    each(n_col, got5)
    quarter = lax.rem(col_at, 4) * 32
    back_shift = lax.rem(128 - quarter, 128)
    for i in range(n_col):
        modes_ref[32 * i : 32 * i + 32] = pltpu.roll(rcv5[i].astype(jnp.float32), back_shift, 1)

    mix_ref[...] = jnp.zeros_like(mix_ref)
    if forward:
        spec_ref[...] = modes_ref[...]
        for kl in range(4):

            def add_channel(i, sums):
                real, imag = sums
                s_re = modes_ref[pl.ds(8 * i + kl, 1), :][:, :32]
                s_im = modes_ref[pl.ds(8 * i + 4 + kl, 1), :][:, :32]
                w_re = w_ref[kl, 0, i].astype(jnp.float32)
                w_im = w_ref[kl, 1, i].astype(jnp.float32)
                return (real + (w_re * s_re - w_im * s_im), imag + (w_re * s_im + w_im * s_re))

            zero = jnp.zeros((32, 32), jnp.float32)
            real, imag = lax.fori_loop(0, 32, add_channel, (zero, zero))
            factor = jnp.where(row_at * 4 + kl == 0, 1.0, 2.0).astype(jnp.float32) * scale
            mix_ref[32 * kl : 32 * kl + 32, 0:32] = real.astype(jnp.bfloat16).astype(jnp.float32) * factor
            mix_ref[128 + 32 * kl : 160 + 32 * kl, 0:32] = imag.astype(jnp.bfloat16).astype(jnp.float32) * factor
    else:
        for kl in range(4):
            factor = jnp.where(row_at * 4 + kl == 0, 1.0, 2.0).astype(jnp.float32)
            g_re = modes_ref[pl.ds(kl, 32, stride=8), :][:, :32] * factor
            g_im = modes_ref[pl.ds(4 + kl, 32, stride=8), :][:, :32] * factor

            def one_channel(i, carry):
                s_re = spec_ref[pl.ds(8 * i + kl, 1), :][:, :32]
                s_im = spec_ref[pl.ds(8 * i + 4 + kl, 1), :][:, :32]
                w_re = w_ref[kl, 0, i].astype(jnp.float32)
                w_im = w_ref[kl, 1, i].astype(jnp.float32)
                gspec_ref[kl, 0, i] = g_re * s_re + g_im * s_im
                gspec_ref[kl, 1, i] = g_im * s_re - g_re * s_im
                b_re = jnp.sum(w_re * g_re + w_im * g_im, axis=0, keepdims=True)
                b_im = jnp.sum(w_re * g_im - w_im * g_re, axis=0, keepdims=True)
                mix_ref[pl.ds(32 * kl + i, 1), 0:32] = b_re.astype(jnp.bfloat16).astype(jnp.float32) * scale
                mix_ref[pl.ds(128 + 32 * kl + i, 1), 0:32] = b_im.astype(jnp.bfloat16).astype(jnp.float32) * scale
                return carry

            lax.fori_loop(0, 32, one_channel, 0)

    mix_ref[...] = pltpu.roll(mix_ref[...], quarter, 1)
    for i in range(n_col):
        for odd_channel in range(2):
            upper = mix_ref[pl.ds(4 * i + odd_channel, 8, stride=32), :]
            lower = mix_ref[pl.ds(4 * i + 2 + odd_channel, 8, stride=32), :]
            snd7[i, 16 * odd_channel : 16 * odd_channel + 16] = jnp.concatenate([upper, lower], axis=0).astype(
                jnp.bfloat16
            )
    start7, sent7, got7 = exchange("col", col_at, n_col, lambda i: snd7.at[i], lambda i: rcv7.at[i], s7, r7)
    each(n_col, start7)
    rcv7[col_at] = snd7[col_at]
    each(n_col, got7)
    halves = [sum(rcv7[4 * h + q].astype(jnp.float32) for q in range(4)) for h in range(2)]
    mixed = jnp.concatenate(halves, axis=1)
    swapped = part_swap(mixed, -1.0)
    operand = jnp.concatenate([mixed, swapped], axis=1).astype(jnp.bfloat16)
    by_rows = dot(operand, tx_ref[...], NN)
    for s in range(pairs):
        even = by_rows[0:16, 128 * s : 128 * s + 128]
        odd = by_rows[16:32, 128 * s : 128 * s + 128]
        snd9[2 * s] = jnp.where(low, even, pltpu.roll(odd, 64, 1)).astype(jnp.bfloat16)
        snd9[2 * s + 1] = jnp.where(low, pltpu.roll(even, 64, 1), odd).astype(jnp.bfloat16)
    start9, sent9, got9 = exchange("row", row_at, n_row, lambda i: snd9.at[i], lambda i: rcv9.at[i], s9, r9)
    each(n_row, start9)
    rcv9[row_at] = snd9[row_at]
    each(n_row, got9)
    got = rcv9[...].astype(jnp.float32)
    own_rows = jnp.concatenate(
        [got[:, :8].reshape(8 * n_row, 128), got[:, 8:].reshape(8 * n_row, 128)], axis=1
    )
    lhs = jnp.transpose(own_rows).astype(jnp.bfloat16)
    start10, sent10, got10 = exchange("col", col_at, n_col, lambda i: snd10.at[i], lambda i: rcv10.at[i], s10, r10)

    def make_cells(d):
        peer = lax.rem(col_at + d, n_col)
        snd10[peer] = dot(lhs, ty_ref[peer], NN).astype(jnp.bfloat16)
        start10(d)

    each(n_col, make_cells)
    rcv10[col_at] = dot(lhs, ty_ref[col_at], NN).astype(jnp.bfloat16)
    each(n_col, got10)
    cells_ref[...] = rcv10[...]
    each(n_col, sent1)
    each(n_row, sent3)
    each(n_col, sent5)
    each(n_col, sent7)
    each(n_row, sent9)
    each(n_col, sent10)


def spectral_chain(forward, field, weight, ty, tx, n_row, n_col, spec=None):
    bf16, f32 = (jnp.bfloat16, jnp.float32)
    dma = pltpu.SemaphoreType.DMA
    modes2 = 8 * n_row
    nx = 64 * n_row
    scratch = [
        pltpu.VMEM((n_col, 256, 256), bf16),
        pltpu.VMEM((modes2, 256), f32),
        pltpu.VMEM((n_row, 16, 128), bf16),
        pltpu.VMEM((n_row, 16, 128), bf16),
        pltpu.VMEM((32, nx), bf16),
        pltpu.VMEM((2, 32, 128), bf16),
        pltpu.VMEM((n_col, 32, 128), bf16),
        pltpu.VMEM((256, 128), f32),
        pltpu.VMEM((256, 128), f32),
        pltpu.VMEM((n_col, 32, 128), bf16),
        pltpu.VMEM((n_col, 32, 128), bf16),
        pltpu.VMEM((n_row, 16, 128), bf16),
        pltpu.VMEM((n_row, 16, 128), bf16),
        pltpu.VMEM((n_col, 256, 256), bf16),
        pltpu.VMEM((n_col, 256, 256), bf16),
        dma,
    ]
    for size in (n_col, n_row, n_col, n_col, n_row, n_col):
        scratch += [dma((size,)), dma((size,))]
    vmem = pl.BlockSpec(memory_space=pltpu.VMEM)
    args = [field.reshape(n_col, 256, 256), weight, ty, tx]
    specs = [pl.BlockSpec(memory_space=pl.ANY), vmem, vmem, vmem]
    shapes = [jax.ShapeDtypeStruct((n_col, 256, 256), bf16)]
    if forward:
        shapes.append(jax.ShapeDtypeStruct((256, 128), f32))
    else:
        args.append(spec)
        specs.append(vmem)
        shapes.append(jax.ShapeDtypeStruct(weight.shape, f32))
    cells, other = pl.pallas_call(
        functools.partial(chain_kernel, forward, n_row, n_col),
        out_shape=shapes,
        in_specs=specs,
        out_specs=[vmem, vmem],
        scratch_shapes=scratch,
        compiler_params=pltpu.CompilerParams(
            collective_id=0 if forward else 1, has_side_effects=True, vmem_limit_bytes=VMEM_BYTES
        ),
        name="chain_forward" if forward else "chain_backward",
    )(*args)
    return cells.reshape(field.shape), other


def gelu_parts(pre):
    cdf = 0.5 * (1.0 + jax.scipy.special.erf(pre / math.sqrt(2.0)))
    pdf = jnp.exp(-0.5 * pre * pre) / math.sqrt(TWO_PI)
    return (pre * cdf, cdf + pre * pdf)


def conv_cells(padded, kernel, n_rows, n_cols):
    result = jnp.zeros((kernel.shape[3], n_rows, n_cols), jnp.float32)
    for tap_row in range(3):
        for tap_col in range(3):
            shifted = padded[:, tap_row : tap_row + n_rows, tap_col : tap_col + n_cols]
            result = result + jnp.einsum(
                "io,ixy->oxy", kernel[tap_row, tap_col], shifted, preferred_element_type=jnp.float32
            )
    return result


def conv_transpose(padded, kernel, n_rows, n_cols):
    result = jnp.zeros((kernel.shape[2], n_rows, n_cols), jnp.float32)
    for tap_row in range(3):
        for tap_col in range(3):
            shifted = padded[
                :, 2 - tap_row : 2 - tap_row + n_rows, 2 - tap_col : 2 - tap_col + n_cols
            ]
            result = result + jnp.einsum(
                "io,oxy->ixy", kernel[tap_row, tap_col], shifted, preferred_element_type=jnp.float32
            )
    return result


def kernel_grad(padded, grad_round, n_rows, n_cols):
    taps = []
    for tap_row in range(3):
        for tap_col in range(3):
            shifted = padded[:, tap_row : tap_row + n_rows, tap_col : tap_col + n_cols]
            taps.append(
                jnp.einsum("ixy,oxy->io", shifted, grad_round, preferred_element_type=jnp.float32)
            )
    return jnp.stack(taps).reshape(3, 3, padded.shape[0], grad_round.shape[0])


def per_device(n_row, n_col, ocean_field, cotangent, conv_weight, conv_bias, projection, mode_weight):
    chans, rows_dev, cols_dev = ocean_field.shape
    ky_dev = mode_weight.shape[0]
    kx_all = mode_weight.shape[4] * n_col
    scale = 1.0 / math.sqrt(rows_dev * n_row * cols_dev * n_col)
    ty, tx = (jnp.asarray(t) for t in tables(n_row, n_col, ky_dev, rows_dev, cols_dev, kx_all))

    padded_in = with_halo(ocean_field, (("row", 1), ("col", 2)), 1)
    spectral_cells, spectrum = spectral_chain(True, ocean_field, mode_weight, ty, tx, n_row, n_col)
    pre_act = (
        conv_cells(padded_in, conv_weight, rows_dev, cols_dev)
        + spectral_cells
        + conv_bias[:, None, None]
    )
    activ, slope = gelu_parts(pre_act)
    cot_rows = cotangent.astype(jnp.float32)
    grad_pre = projection[:, None, None] * cot_rows[None] * slope
    grad_round = grad_pre.astype(jnp.bfloat16)
    kernel_part = kernel_grad(padded_in, grad_round, rows_dev, cols_dev)
    bias_part = jnp.sum(grad_pre, axis=(1, 2))
    proj_part = jnp.sum(activ * cot_rows[None], axis=(1, 2))
    kernel_sum, bias_sum, proj_sum = lax.psum((kernel_part, bias_part, proj_part), ("row", "col"))
    padded_grad = with_halo(grad_round, (("row", 1), ("col", 2)), 1)
    spectral_back, grad_spec = spectral_chain(
        False, grad_round, mode_weight, ty, tx, n_row, n_col, spectrum
    )
    back_cells = conv_transpose(padded_grad, conv_weight, rows_dev, cols_dev)
    grad_input = back_cells + spectral_back
    return (grad_input, grad_spec, kernel_sum * scale, bias_sum * scale, proj_sum * scale)


def solution(mesh):
    placed = (
        P(None, "row", "col"),
        P("row", "col"),
        P(),
        P(),
        P(),
        P("row", None, None, None, "col"),
    )
    return jax.shard_map(
        functools.partial(per_device, mesh.shape["row"], mesh.shape["col"]),
        mesh=mesh,
        in_specs=placed,
        out_specs=(P(None, "row", "col"), P("row", None, None, None, "col"), P(), P(), P()),
        check_vma=False,
    )
```

```python
import functools
import math

import jax
import jax.numpy as jnp
import ml_dtypes
import numpy as np
from jax import lax
from jax.experimental import pallas as pl
from jax.experimental.pallas import tpu as pltpu
from jax.sharding import PartitionSpec as P

TWO_PI = 2.0 * math.pi
HIGH = lax.Precision.HIGHEST
VMEM_BYTES = 56 * 1024 * 1024


def angle_pair(products, period):
    angles = (products % period).astype(np.float32) * np.float32(TWO_PI / period)
    return (np.cos(angles).astype(ml_dtypes.bfloat16), np.sin(angles).astype(ml_dtypes.bfloat16))


def tables(n_row, n_col, ky_dev, rows_dev, cols_dev, kx_all):
    modes, nx, ny = (ky_dev * n_row, rows_dev * n_row, cols_dev * n_col)
    cosine, sine = angle_pair(np.arange(modes)[:, None] * np.arange(ny)[None, :], ny)
    ty = np.stack([cosine.reshape(n_row, ky_dev, ny), -sine.reshape(n_row, ky_dev, ny)], axis=1)
    ty = ty.reshape(2 * modes, n_col, cols_dev).transpose(1, 0, 2)
    ids = np.arange(kx_all)
    freqs = np.where(ids < modes, ids, ids - 2 * modes) % nx
    cosine, sine = angle_pair(freqs[:, None] * np.arange(nx)[None, :], nx)
    return np.ascontiguousarray(ty), np.concatenate([cosine, sine], axis=0)


NT = (((1,), (1,)), ((), ()))
NN = (((1,), (0,)), ((), ()))
TN = (((0,), (0,)), ((), ()))


def dot(a, b, dims):
    return lax.dot_general(a, b, dims, preferred_element_type=jnp.float32)


def exchange(axis, me, size, source, target, send_sem, recv_sem):
    def copy(step, peer, slot):
        return pltpu.make_async_remote_copy(
            src_ref=source(peer),
            dst_ref=target(slot),
            send_sem=send_sem.at[step],
            recv_sem=recv_sem.at[step],
            device_id={axis: peer},
            device_id_type=pl.DeviceIdType.MESH,
        )

    def start(step):
        copy(step, lax.rem(me + step, size), me).start()

    def wait_send(step):
        copy(step, lax.rem(me + step, size), me).wait_send()

    def wait_recv(step):
        origin = lax.rem(me + size - step, size)
        copy(step, lax.rem(me + step, size), origin).wait_recv()
        return origin

    return start, wait_send, wait_recv


def each(size, body):
    def step(index, carry):
        body(index)
        return carry

    lax.fori_loop(1, size, step, 0)


def part_swap(value, sign):
    rows = value.shape[0]
    is_real = (lax.broadcasted_iota(jnp.int32, value.shape, 0) & 4) == 0
    after = pltpu.roll(value, rows - 4, 0)
    before = pltpu.roll(value, 4, 0)
    return jnp.where(is_real, sign * after, -sign * before)


class Group:
    def __init__(self, names, refs):
        for name, ref in zip(names, refs):
            setattr(self, name, ref)


def push(src, dst, send_sem, recv_sem, axis, peer):
    return pltpu.make_async_remote_copy(
        src_ref=src,
        dst_ref=dst,
        send_sem=send_sem,
        recv_sem=recv_sem,
        device_id={axis: peer},
        device_id_type=pl.DeviceIdType.MESH,
    )


def aligned(value, to):
    return pl.multiple_of(value, to)


def pass_scratch(n_row, n_col):
    bf16, f32 = (jnp.bfloat16, jnp.float32)
    dma = pltpu.SemaphoreType.DMA
    found = dict(
        snd1=pltpu.VMEM((n_col, 256, 256), bf16),
        buf1=pltpu.VMEM((n_col, 256, 256), bf16),
        snd3=pltpu.VMEM((n_row, 16, 128), bf16),
        rcv3=pltpu.VMEM((n_row, 16, 128), bf16),
        snd5=pltpu.VMEM((2, 32, 128), bf16),
        rcv5=pltpu.VMEM((n_col, 32, 128), bf16),
        modes=pltpu.VMEM((256, 128), f32),
        snd7=pltpu.VMEM((n_col, 32, 128), bf16),
        rcv7=pltpu.VMEM((n_col, 32, 128), bf16),
        snd9=pltpu.VMEM((n_row, 16, 128), bf16),
        rcv9=pltpu.VMEM((n_row, 16, 128), bf16),
        snd10=pltpu.VMEM((n_col, 256, 256), bf16),
        rcv10=pltpu.VMEM((n_col, 256, 256), bf16),
        raw=pltpu.VMEM((68 * 32, 256), bf16),
        halo=pltpu.VMEM((2, 32, 256), bf16),
        edge_out=pltpu.VMEM((2, 16, 68 * 32), bf16),
        edge_in=pltpu.VMEM((2, 16, 68 * 32), bf16),
        wide=pltpu.VMEM((68 * 96, 256), bf16),
        taps=pltpu.VMEM((256, 1024), bf16),
        own=dma,
        hs=dma((2,)),
        hr=dma((2,)),
        es=dma((2,)),
        er=dma((2,)),
    )
    for step, size in ((1, n_col), (3, n_row), (5, n_col), (7, n_col), (9, n_row), (10, n_col)):
        found["s%d" % step] = dma((size,))
        found["r%d" % step] = dma((size,))
    return found


def common_scratch(n_row, n_col, nx, owners):
    bf16, f32 = (jnp.bfloat16, jnp.float32)
    dma = pltpu.SemaphoreType.DMA
    piece = 80 // owners
    return dict(
        vbuf=pltpu.VMEM((n_col, 256, 256), bf16),
        ty=pltpu.VMEM((n_col, 8 * n_row, 256), bf16),
        tx=pltpu.VMEM((512, nx), bf16),
        weight=pltpu.VMEM((4, 2, 32, 32, 32), bf16),
        stage=pltpu.VMEM((4096, 128), f32),
        cells=pltpu.VMEM((2048, 256), f32),
        cot=pltpu.VMEM((64, 256), f32),
        acc=pltpu.VMEM((8 * n_row, 256), f32),
        rows_x=pltpu.VMEM((32, nx), bf16),
        mix=pltpu.VMEM((256, 128), f32),
        outer=pltpu.VMEM((960, 256), f32),
        sums=pltpu.VMEM((128, 256), f32),
        part=pltpu.VMEM((owners, piece, 128), f32),
        got_row=pltpu.VMEM((n_row, piece, 128), f32),
        sum_row=pltpu.VMEM((piece, 128), f32),
        got_col=pltpu.VMEM((n_col, piece, 128), f32),
        total=pltpu.VMEM((piece, 128), f32),
        got_all=pltpu.VMEM((owners, piece, 128), f32),
        load=dma((4,)),
        row_s=dma((owners,)),
        row_r=dma((n_row,)),
        col_s=dma((n_col,)),
        col_r=dma((n_col,)),
        all_s=dma((n_row,)),
        all_r=dma((owners,)),
    )


def step_kernel(n_row, n_col, owners, *refs):
    (v_ref, cot_ref, w2_ref, bias_ref, proj_ref, w_hbm, ty_hbm, tx_hbm, out_ref, gspec_ref, small_ref, *rest) = refs
    nx = 64 * n_row
    names = list(pass_scratch(n_row, n_col))
    first = Group(names, rest[: len(names)])
    second = Group(names, rest[len(names) : 2 * len(names)])
    g = Group(list(common_scratch(n_row, n_col, nx, owners)), rest[2 * len(names) :])
    row_at = lax.axis_index("row")
    col_at = lax.axis_index("col")
    pairs = n_row // 2
    scale = 1.0 / math.sqrt((64 * n_row) * (256 * n_col))
    bf16, f32 = (jnp.bfloat16, jnp.float32)
    pending = []

    loads = [
        pltpu.make_async_copy(v_ref, g.vbuf, g.load.at[0]),
        pltpu.make_async_copy(ty_hbm, g.ty, g.load.at[1]),
        pltpu.make_async_copy(tx_hbm, g.tx, g.load.at[2]),
        pltpu.make_async_copy(w_hbm, g.weight, g.load.at[3]),
    ]
    for load in loads:
        load.start()
    barrier = pltpu.get_barrier_semaphore()
    each(n_col, lambda d: pl.semaphore_signal(
        barrier, inc=1, device_id={"col": lax.rem(col_at + d, n_col)}, device_id_type=pl.DeviceIdType.MESH))
    each(n_row, lambda d: pl.semaphore_signal(
        barrier, inc=1, device_id={"row": lax.rem(row_at + d, n_row)}, device_id_type=pl.DeviceIdType.MESH))
    pl.semaphore_wait(barrier, n_col - 1 + n_row - 1)

    def loop(size, body):
        def step(index, carry):
            body(index)
            return carry

        lax.fori_loop(0, size, step, 0)

    def send_halo_rows(p):
        up = lax.rem(row_at + n_row - 1, n_row)
        down = lax.rem(row_at + 1, n_row)
        copies = [
            push(p.raw.at[pl.ds(32, 32)], p.halo.at[1], p.hs.at[0], p.hr.at[0], "row", up),
            push(p.raw.at[pl.ds(64 * 32, 32)], p.halo.at[0], p.hs.at[1], p.hr.at[1], "row", down),
        ]
        for copy in copies:
            copy.start()
            pending.append(copy.wait_send)
        return copies

    def widen(p, row_copies):
        for copy in row_copies:
            copy.wait_recv()
        above = jnp.where(row_at > 0, 1.0, 0.0)
        below = jnp.where(row_at < n_row - 1, 1.0, 0.0)
        p.raw[0:32] = (p.halo[0].astype(f32) * above).astype(bf16)
        p.raw[65 * 32 : 66 * 32] = (p.halo[1].astype(f32) * below).astype(bf16)
        p.raw[66 * 32 : 68 * 32] = jnp.zeros((64, 256), bf16)
        row = lax.broadcasted_iota(jnp.int32, (32, 256), 0)
        lane = lax.broadcasted_iota(jnp.int32, (32, 256), 1)
        pick = ((row == 0) & (lane == 0)) | ((row == 16) & (lane == 255))
        edges = dot(jnp.where(pick, 1.0, 0.0).astype(bf16), p.raw[...], NT)
        p.edge_out[0] = edges[0:16].astype(bf16)
        p.edge_out[1] = edges[16:32].astype(bf16)
        left = lax.rem(col_at + n_col - 1, n_col)
        right = lax.rem(col_at + 1, n_col)
        copies = [
            push(p.edge_out.at[0], p.edge_in.at[1], p.es.at[0], p.er.at[0], "col", left),
            push(p.edge_out.at[1], p.edge_in.at[0], p.es.at[1], p.er.at[1], "col", right),
        ]
        for copy in copies:
            copy.start()
            pending.append(copy.wait_send)
        return copies

    def fill_wide(p, copies):
        for copy in copies:
            copy.wait_recv()
        row = lax.broadcasted_iota(jnp.int32, (16, 128), 0)
        lane = lax.broadcasted_iota(jnp.int32, (16, 128), 1)
        put_left = jnp.where((row == 0) & (lane == 0) & (col_at > 0), 1.0, 0.0).astype(bf16)
        put_right = jnp.where((row == 0) & (lane == 127) & (col_at < n_col - 1), 1.0, 0.0).astype(bf16)
        lanes = lax.broadcasted_iota(jnp.int32, (128, 128), 1)

        def chunk(q):
            here = p.raw[pl.ds(aligned(q * 128, 128), 128), :].astype(f32)
            from_left = dot(p.edge_in[0, :, pl.ds(aligned(q * 128, 128), 128)], put_left, TN)
            from_right = dot(p.edge_in[1, :, pl.ds(aligned(q * 128, 128), 128)], put_right, TN)
            before = pltpu.roll(here, 1, 1)
            after = pltpu.roll(here, 255, 1)
            before = jnp.concatenate([jnp.where(lanes == 0, from_left, before[:, :128]), before[:, 128:]], axis=1)
            after = jnp.concatenate([after[:, :128], jnp.where(lanes == 127, from_right, after[:, 128:])], axis=1)
            for x in range(4):
                for b, value in enumerate((before, here, after)):
                    base = aligned(q * 384 + 96 * x + 32 * b, 32)
                    p.wide[pl.ds(base, 32), :] = value[32 * x : 32 * x + 32].astype(bf16)

        loop(17, chunk)

    def convolve(p, kernel):
        padded = w2_ref[kernel]
        for x in range(8):
            p.taps[32 * x : 32 * x + 32, :] = (pltpu.roll(padded, 96 * x, 1) if x else padded).astype(bf16)

        def block(t):
            rows = p.wide[pl.ds(aligned(t * 768, 16), 1024), :]
            g.cells[pl.ds(aligned(t * 256, 256), 256), :] = dot(p.taps[...], rows, NN)

        loop(8, block)

    def to_modes(p, source, cover, cover_rows):
        own = pltpu.make_async_copy(source(col_at), p.buf1.at[col_at], p.own)
        own.start()
        start, sent, got = exchange("col", col_at, n_col, source, lambda i: p.buf1.at[i], p.s1, p.r1)
        each(n_col, start)
        pending.append(lambda: each(n_col, sent))
        cover()
        own.wait()
        g.acc[...] = dot(g.ty[col_at], p.buf1[col_at], NT)

        def add_block(d):
            origin = got(d)
            g.acc[...] += dot(g.ty[origin], p.buf1[origin], NT)

        each(n_col, add_block)
        whole = g.acc[...]
        upper = whole[:, :128].reshape(n_row, 8, 128)
        lower = whole[:, 128:].reshape(n_row, 8, 128)
        p.snd3[...] = jnp.concatenate([upper, lower], axis=1).astype(bf16)
        start3, sent3, got3 = exchange("row", row_at, n_row, lambda i: p.snd3.at[i], lambda i: p.rcv3.at[i], p.s3, p.r3)
        each(n_row, start3)
        pending.append(lambda: each(n_row, sent3))
        p.rcv3[row_at] = p.snd3[row_at]
        cover_rows()
        each(n_row, got3)
        for s in range(pairs):
            one = p.rcv3[2 * s].astype(f32)
            two = p.rcv3[2 * s + 1].astype(f32)
            even = jnp.where(low, one, pltpu.roll(two, 64, 1))
            odd = jnp.where(low, pltpu.roll(one, 64, 1), two)
            g.rows_x[0:16, 128 * s : 128 * s + 128] = even.astype(bf16)
            g.rows_x[16:32, 128 * s : 128 * s + 128] = odd.astype(bf16)
        both = dot(g.rows_x[...], g.tx[...], NT)
        coeffs = (both[:, :256] + part_swap(both[:, 256:], 1.0)) * scale
        coeffs = jnp.concatenate([coeffs[0:8], coeffs[16:24], coeffs[8:16], coeffs[24:32]], axis=0)
        p.snd5[0] = coeffs[:, :128].astype(bf16)
        p.snd5[1] = coeffs[:, 128:].astype(bf16)
        start5, sent5, got5 = exchange(
            "col", col_at, n_col, lambda i: p.snd5.at[i // 4], lambda i: p.rcv5.at[i], p.s5, p.r5
        )
        each(n_col, start5)
        pending.append(lambda: each(n_col, sent5))
        p.rcv5[col_at] = p.snd5[col_at // 4]
        g.mix[...] = jnp.zeros_like(g.mix)
        each(n_col, got5)
        for i in range(n_col):
            p.modes[32 * i : 32 * i + 32] = pltpu.roll(p.rcv5[i].astype(f32), back_shift, 1)

    def to_grid(p, cover_rows):
        g.mix[...] = pltpu.roll(g.mix[...], quarter, 1)
        for i in range(n_col):
            for odd_channel in range(2):
                upper = g.mix[pl.ds(4 * i + odd_channel, 8, stride=32), :]
                lower = g.mix[pl.ds(4 * i + 2 + odd_channel, 8, stride=32), :]
                p.snd7[i, 16 * odd_channel : 16 * odd_channel + 16] = jnp.concatenate(
                    [upper, lower], axis=0
                ).astype(bf16)
        start7, sent7, got7 = exchange("col", col_at, n_col, lambda i: p.snd7.at[i], lambda i: p.rcv7.at[i], p.s7, p.r7)
        each(n_col, start7)
        pending.append(lambda: each(n_col, sent7))
        p.rcv7[col_at] = p.snd7[col_at]
        each(n_col, got7)
        halves = [sum(p.rcv7[4 * h + q].astype(f32) for q in range(4)) for h in range(2)]
        mixed = jnp.concatenate(halves, axis=1)
        swapped = part_swap(mixed, -1.0)
        operand = jnp.concatenate([mixed, swapped], axis=1).astype(bf16)
        by_rows = dot(operand, g.tx[...], NN)
        for s in range(pairs):
            even = by_rows[0:16, 128 * s : 128 * s + 128]
            odd = by_rows[16:32, 128 * s : 128 * s + 128]
            p.snd9[2 * s] = jnp.where(low, even, pltpu.roll(odd, 64, 1)).astype(bf16)
            p.snd9[2 * s + 1] = jnp.where(low, pltpu.roll(even, 64, 1), odd).astype(bf16)
        start9, sent9, got9 = exchange("row", row_at, n_row, lambda i: p.snd9.at[i], lambda i: p.rcv9.at[i], p.s9, p.r9)
        each(n_row, start9)
        pending.append(lambda: each(n_row, sent9))
        p.rcv9[row_at] = p.snd9[row_at]
        cover_rows()
        each(n_row, got9)
        got = p.rcv9[...].astype(f32)
        own_rows = jnp.concatenate(
            [got[:, :8].reshape(8 * n_row, 128), got[:, 8:].reshape(8 * n_row, 128)], axis=1
        )
        lhs = jnp.transpose(own_rows).astype(bf16)
        start10, sent10, got10 = exchange(
            "col", col_at, n_col, lambda i: p.snd10.at[i], lambda i: p.rcv10.at[i], p.s10, p.r10
        )

        def make_cells(d):
            peer = lax.rem(col_at + d, n_col)
            p.snd10[peer] = dot(lhs, g.ty[peer], NN).astype(bf16)
            start10(d)

        each(n_col, make_cells)
        pending.append(lambda: each(n_col, sent10))

        place(col_at, dot(lhs, g.ty[col_at], NN))

        def take(d):
            origin = got10(d)
            place(origin, p.rcv10[origin].astype(f32))

        each(n_col, take)

    def nothing():
        return None

    def place(slot, value):
        for half in range(2):
            g.stage[pl.ds(aligned(half * 2048 + slot * 256, 256), 256), :] = value[:, 128 * half : 128 * half + 128]

    def placed(slot):
        return jnp.concatenate(
            [g.stage[2048 * half + 256 * slot : 2048 * half + 256 * slot + 256] for half in range(2)], axis=1
        )

    def grid_row(x):
        return jnp.concatenate([g.stage[pl.ds(2048 * half + x, 32, stride=64), :] for half in range(2)], axis=1)

    def put_grid_row(x, value):
        for half in range(2):
            g.stage[pl.ds(2048 * half + x, 32, stride=64), :] = value[:, 128 * half : 128 * half + 128]

    low = lax.broadcasted_iota(jnp.int32, (16, 128), 1) < 64
    quarter = lax.rem(col_at, 4) * 32
    back_shift = lax.rem(128 - quarter, 128)

    def cover_field():
        loads[0].wait()
        for i in range(n_col):
            place(i, g.vbuf[i].astype(f32))

        def regroup(x):
            first.raw[pl.ds(aligned(x * 32 + 32, 32), 32), :] = grid_row(x).astype(bf16)

        regroup(0)
        regroup(63)
        row_copies = send_halo_rows(first)

        def inner(x):
            regroup(x + 1)

        loop(62, inner)
        copies = widen(first, row_copies)
        g.cot[...] = cot_ref[...].astype(f32)
        fill_wide(first, copies)
        convolve(first, 0)
        loads[1].wait()
        loads[2].wait()

    to_modes(first, lambda i: v_ref.at[i], cover_field, nothing)
    loads[3].wait()
    for kl in range(4):

        def add_channel(i, sums):
            real, imag = sums
            s_re = first.modes[pl.ds(8 * i + kl, 1), :][:, :32]
            s_im = first.modes[pl.ds(8 * i + 4 + kl, 1), :][:, :32]
            w_re = g.weight[kl, 0, i].astype(f32)
            w_im = g.weight[kl, 1, i].astype(f32)
            return (real + (w_re * s_re - w_im * s_im), imag + (w_re * s_im + w_im * s_re))

        zero = jnp.zeros((32, 32), f32)
        real, imag = lax.fori_loop(0, 32, add_channel, (zero, zero))
        factor = jnp.where(row_at * 4 + kl == 0, 1.0, 2.0).astype(f32) * scale
        g.mix[32 * kl : 32 * kl + 32, 0:32] = real.astype(bf16).astype(f32) * factor
        g.mix[128 + 32 * kl : 160 + 32 * kl, 0:32] = imag.astype(bf16).astype(f32) * factor
    to_grid(first, nothing)

    bias = jnp.broadcast_to(bias_ref[...], (32, 256))
    proj = jnp.broadcast_to(proj_ref[...], (32, 256))

    def activate(x, sums):
        bias_sum, proj_sum = sums
        pre = g.cells[pl.ds(aligned(x * 32, 32), 32), :] + grid_row(x) + bias
        cdf = 0.5 * (1.0 + lax.erf(pre * math.sqrt(0.5)))
        pdf = jnp.exp(-0.5 * pre * pre) * (1.0 / math.sqrt(TWO_PI))
        cot = jnp.broadcast_to(g.cot[pl.ds(x, 1), :], (32, 256))
        grad = (proj * cot) * (cdf + pre * pdf)
        rounded = grad.astype(bf16)
        second.raw[pl.ds(aligned(x * 32 + 32, 32), 32), :] = rounded
        put_grid_row(x, rounded.astype(f32))
        return (bias_sum + grad, proj_sum + (pre * cdf) * cot)

    zero = jnp.zeros((32, 256), f32)
    bias_sum, proj_sum = lax.fori_loop(0, 64, activate, (zero, zero))
    for i in range(n_col):
        second.snd1[i] = placed(i).astype(bf16)

    piece = 80 // owners

    def cover_grad():
        row_copies = send_halo_rows(second)
        g.sums[0:32] = bias_sum
        g.sums[32:64] = proj_sum
        g.sums[64:128] = jnp.zeros((64, 256), f32)
        g.outer[...] = jnp.zeros_like(g.outer)

        def block(t):
            rows = first.wide[pl.ds(aligned(t * 768, 16), 960), :]
            grads = second.raw[pl.ds(aligned(t * 256 + 32, 32), 256), :]
            g.outer[...] += dot(rows, grads, NT)

        loop(8, block)
        copies = widen(second, row_copies)
        lane = lax.broadcasted_iota(jnp.int32, (96, 128), 1)
        taps = []
        for a in range(3):
            total = jnp.zeros((96, 128), f32)
            for x in range(8):
                here = g.outer[96 * (x + a) : 96 * (x + a) + 96, 128 * (x // 4) : 128 * (x // 4) + 128]
                total = total + (pltpu.roll(here, 128 - 32 * (x % 4), 1) if x % 4 else here)
            taps.append(jnp.where(lane < 32, total, 0.0))
        taps = jnp.concatenate(taps, axis=0)
        packed = taps[0:72]
        for q in range(1, 4):
            packed = packed + pltpu.roll(taps[72 * q : 72 * q + 72], 32 * q, 1)
        lanes_sum = lax.dot_general(
            jnp.ones((8, 256), f32), g.sums[...], NT, precision=HIGH, preferred_element_type=f32
        )
        g.part[...] = (jnp.concatenate([packed, lanes_sum], axis=0) * scale).reshape(owners, piece, 128)
        for t in range(owners):

            @pl.when(row_at != t)
            def _():
                push(g.part.at[t], g.got_row.at[row_at], g.row_s.at[t], g.row_r.at[row_at], "row", t).start()

        fill_wide(second, copies)
        convolve(second, 1)

    def sum_rows():
        @pl.when(row_at < owners)
        def _():
            g.got_row[row_at] = g.part[row_at]

            def wait(d):
                origin = lax.rem(row_at + d, n_row)
                push(g.part.at[0], g.got_row.at[origin], g.row_s.at[0], g.row_r.at[origin], "row", origin).wait_recv()

            each(n_row, wait)
            g.sum_row[...] = jnp.sum(g.got_row[...], axis=0)
            g.got_col[col_at] = g.sum_row[...]
            start, _, _ = exchange(
                "col", col_at, n_col, lambda i: g.sum_row, lambda i: g.got_col.at[i], g.col_s, g.col_r
            )
            each(n_col, start)

    def sum_cols():
        @pl.when(row_at < owners)
        def _():
            _, sent, got = exchange(
                "col", col_at, n_col, lambda i: g.sum_row, lambda i: g.got_col.at[i], g.col_s, g.col_r
            )
            each(n_col, got)
            each(n_col, sent)
            g.total[...] = jnp.sum(g.got_col[...], axis=0)
            g.got_all[row_at] = g.total[...]

            def send(d):
                peer = lax.rem(row_at + d, n_row)
                push(g.total, g.got_all.at[row_at], g.all_s.at[d], g.all_r.at[row_at], "row", peer).start()

            each(n_row, send)

    to_modes(second, lambda i: second.snd1.at[i], cover_grad, sum_rows)
    for kl in range(4):
        factor = jnp.where(row_at * 4 + kl == 0, 1.0, 2.0).astype(f32)
        g_re = second.modes[pl.ds(kl, 32, stride=8), :][:, :32] * factor
        g_im = second.modes[pl.ds(4 + kl, 32, stride=8), :][:, :32] * factor

        def one_channel(i, carry):
            s_re = first.modes[pl.ds(8 * i + kl, 1), :][:, :32]
            s_im = first.modes[pl.ds(8 * i + 4 + kl, 1), :][:, :32]
            w_re = g.weight[kl, 0, i].astype(f32)
            w_im = g.weight[kl, 1, i].astype(f32)
            gspec_ref[kl, 0, i] = g_re * s_re + g_im * s_im
            gspec_ref[kl, 1, i] = g_im * s_re - g_re * s_im
            b_re = jnp.sum(w_re * g_re + w_im * g_im, axis=0, keepdims=True)
            b_im = jnp.sum(w_re * g_im - w_im * g_re, axis=0, keepdims=True)
            g.mix[pl.ds(32 * kl + i, 1), 0:32] = b_re.astype(bf16).astype(f32) * scale
            g.mix[pl.ds(128 + 32 * kl + i, 1), 0:32] = b_im.astype(bf16).astype(f32) * scale
            return carry

        lax.fori_loop(0, 32, one_channel, 0)
    to_grid(second, sum_cols)

    def finish(x):
        put_grid_row(x, g.cells[pl.ds(aligned(x * 32, 32), 32), :] + grid_row(x))

    loop(64, finish)
    for i in range(n_col):
        out_ref[256 * i : 256 * i + 256] = placed(i)
    for t in range(owners):

        @pl.when(row_at != t)
        def _():
            arrived = push(g.part.at[t], g.got_all.at[t], g.row_s.at[t], g.all_r.at[t], "row", t)
            arrived.wait_recv()
            arrived.wait_send()

    @pl.when(row_at < owners)
    def _():
        def sent(d):
            peer = lax.rem(row_at + d, n_row)
            push(g.total, g.got_all.at[row_at], g.all_s.at[d], g.all_r.at[row_at], "row", peer).wait_send()

        each(n_row, sent)

    small_ref[...] = g.got_all[...].reshape(80, 128)
    for wait in pending:
        wait()


def per_device(n_row, n_col, ocean_field, cotangent, conv_weight, conv_bias, projection, mode_weight):
    chans, rows_dev, cols_dev = ocean_field.shape
    ky_dev = mode_weight.shape[0]
    kx_all = mode_weight.shape[4] * n_col
    owners = min(10, n_row)
    ty, tx = (jnp.asarray(t) for t in tables(n_row, n_col, ky_dev, rows_dev, cols_dev, kx_all))
    taps = conv_weight.astype(jnp.float32)
    straight = jnp.transpose(taps, (3, 0, 1, 2)).reshape(chans, 9 * chans)
    turned = jnp.transpose(taps[::-1, ::-1], (2, 0, 1, 3)).reshape(chans, 9 * chans)
    both = jnp.pad(jnp.stack([straight, turned]), ((0, 0), (0, 0), (0, 1024 - 9 * chans)))
    vmem = pl.BlockSpec(memory_space=pltpu.VMEM)
    hbm = pl.BlockSpec(memory_space=pl.ANY)
    one = pass_scratch(n_row, n_col)
    scratch = list(one.values()) * 2 + list(common_scratch(n_row, n_col, rows_dev * n_row, owners).values())
    cells, grad_spec, small = pl.pallas_call(
        functools.partial(step_kernel, n_row, n_col, owners),
        out_shape=[
            jax.ShapeDtypeStruct((chans * rows_dev, cols_dev), jnp.float32),
            jax.ShapeDtypeStruct(mode_weight.shape, jnp.float32),
            jax.ShapeDtypeStruct((80, 128), jnp.float32),
        ],
        in_specs=[hbm, vmem, vmem, vmem, vmem, hbm, hbm, hbm],
        out_specs=[vmem, vmem, vmem],
        scratch_shapes=scratch,
        compiler_params=pltpu.CompilerParams(
            collective_id=0, has_side_effects=True, vmem_limit_bytes=VMEM_BYTES
        ),
        name="layer_step",
    )(
        ocean_field.reshape(n_col, 256, cols_dev),
        cotangent,
        both,
        conv_bias.reshape(chans, 1),
        projection.reshape(chans, 1),
        mode_weight,
        ty,
        tx,
    )
    grad_conv = jnp.transpose(small[:72].reshape(72, 4, 32), (1, 0, 2)).reshape(conv_weight.shape)
    return (cells.reshape(ocean_field.shape), grad_spec, grad_conv, small[72, :32], small[72, 32:64])


def solution(mesh):
    placed = (
        P(None, "row", "col"),
        P("row", "col"),
        P(),
        P(),
        P(),
        P("row", None, None, None, "col"),
    )
    return jax.shard_map(
        functools.partial(per_device, mesh.shape["row"], mesh.shape["col"]),
        mesh=mesh,
        in_specs=placed,
        out_specs=(P(None, "row", "col"), P("row", None, None, None, "col"), P(), P(), P()),
        check_vma=False,
    )
```

```python
import functools
import math

import jax
import jax.numpy as jnp
import ml_dtypes
import numpy as np
from jax import lax
from jax.experimental import pallas as pl
from jax.experimental.pallas import tpu as pltpu
from jax.sharding import PartitionSpec as P

TWO_PI = 2.0 * math.pi
HIGH = lax.Precision.HIGHEST
HALF_FILL = 8
VMEM_BYTES = 56 * 1024 * 1024


def angle_pair(products, period):
    angles = (products % period).astype(np.float32) * np.float32(TWO_PI / period)
    return (np.cos(angles).astype(ml_dtypes.bfloat16), np.sin(angles).astype(ml_dtypes.bfloat16))


def tables(n_row, n_col, ky_dev, rows_dev, cols_dev, kx_all):
    modes, nx, ny = (ky_dev * n_row, rows_dev * n_row, cols_dev * n_col)
    cosine, sine = angle_pair(np.arange(modes)[:, None] * np.arange(ny)[None, :], ny)
    ty = np.stack([cosine.reshape(n_row, ky_dev, ny), -sine.reshape(n_row, ky_dev, ny)], axis=1)
    ty = ty.reshape(2 * modes, n_col, cols_dev).transpose(1, 0, 2)
    ids = np.arange(kx_all)
    freqs = np.where(ids < modes, ids, ids - 2 * modes) % nx
    cosine, sine = angle_pair(freqs[:, None] * np.arange(nx)[None, :], nx)
    return np.ascontiguousarray(ty), np.concatenate([cosine, sine], axis=0)


NT = (((1,), (1,)), ((), ()))
NN = (((1,), (0,)), ((), ()))
TN = (((0,), (0,)), ((), ()))


def dot(a, b, dims):
    return lax.dot_general(a, b, dims, preferred_element_type=jnp.float32)


def exchange(axis, me, size, source, target, send_sem, recv_sem):
    def copy(step, peer, slot):
        return pltpu.make_async_remote_copy(
            src_ref=source(peer),
            dst_ref=target(slot),
            send_sem=send_sem.at[step],
            recv_sem=recv_sem.at[step],
            device_id={axis: peer},
            device_id_type=pl.DeviceIdType.MESH,
        )

    def start(step):
        copy(step, lax.rem(me + step, size), me).start()

    def wait_send(step):
        copy(step, lax.rem(me + step, size), me).wait_send()

    def wait_recv(step):
        origin = lax.rem(me + size - step, size)
        copy(step, lax.rem(me + step, size), origin).wait_recv()
        return origin

    return start, wait_send, wait_recv


def each(size, body):
    def step(index, carry):
        body(index)
        return carry

    lax.fori_loop(1, size, step, 0)


def part_swap(value, sign):
    rows = value.shape[0]
    is_real = (lax.broadcasted_iota(jnp.int32, value.shape, 0) & 4) == 0
    after = pltpu.roll(value, rows - 4, 0)
    before = pltpu.roll(value, 4, 0)
    return jnp.where(is_real, sign * after, -sign * before)


class Group:
    def __init__(self, names, refs):
        for name, ref in zip(names, refs):
            setattr(self, name, ref)


def push(src, dst, send_sem, recv_sem, axis, peer):
    return pltpu.make_async_remote_copy(
        src_ref=src,
        dst_ref=dst,
        send_sem=send_sem,
        recv_sem=recv_sem,
        device_id={axis: peer},
        device_id_type=pl.DeviceIdType.MESH,
    )


def aligned(value, to):
    return pl.multiple_of(value, to)


def pass_scratch(n_row, n_col):
    bf16, f32 = (jnp.bfloat16, jnp.float32)
    dma = pltpu.SemaphoreType.DMA
    found = dict(
        snd1=pltpu.VMEM((n_col, 256, 256), bf16),
        buf1=pltpu.VMEM((n_col, 256, 256), bf16),
        snd3=pltpu.VMEM((n_row, 16, 128), bf16),
        rcv3=pltpu.VMEM((n_row, 16, 128), bf16),
        snd5=pltpu.VMEM((2, 32, 128), bf16),
        rcv5=pltpu.VMEM((n_col, 32, 128), bf16),
        modes=pltpu.VMEM((256, 128), f32),
        snd7=pltpu.VMEM((n_col, 32, 128), bf16),
        rcv7=pltpu.VMEM((n_col, 32, 128), bf16),
        snd9=pltpu.VMEM((n_row, 16, 128), bf16),
        rcv9=pltpu.VMEM((n_row, 16, 128), bf16),
        snd10=pltpu.VMEM((n_col, 256, 256), bf16),
        rcv10=pltpu.VMEM((n_col, 256, 256), bf16),
        raw=pltpu.VMEM((68 * 32, 256), bf16),
        halo=pltpu.VMEM((2, 32, 256), bf16),
        edge_out=pltpu.VMEM((2, 16, 68 * 32), bf16),
        edge_in=pltpu.VMEM((2, 16, 68 * 32), bf16),
        wide=pltpu.VMEM((68 * 96, 256), bf16),
        taps=pltpu.VMEM((256, 1024), bf16),
        own=dma,
        hs=dma((2,)),
        hr=dma((2,)),
        es=dma((2,)),
        er=dma((2,)),
    )
    for step, size in ((1, n_col), (3, n_row), (5, n_col), (7, n_col), (9, n_row), (10, n_col)):
        found["s%d" % step] = dma((size,))
        found["r%d" % step] = dma((size,))
    return found


def common_scratch(n_row, n_col, nx, owners):
    bf16, f32 = (jnp.bfloat16, jnp.float32)
    dma = pltpu.SemaphoreType.DMA
    piece = 80 // owners
    return dict(
        vbuf=pltpu.VMEM((n_col, 256, 256), bf16),
        ty=pltpu.VMEM((n_col, 8 * n_row, 256), bf16),
        tx=pltpu.VMEM((512, nx), bf16),
        weight=pltpu.VMEM((4, 2, 32, 32, 32), bf16),
        stage=pltpu.VMEM((4096, 128), f32),
        cells=pltpu.VMEM((2048, 256), f32),
        cot=pltpu.VMEM((64, 256), f32),
        acc=pltpu.VMEM((8 * n_row, 256), f32),
        rows_x=pltpu.VMEM((32, nx), bf16),
        mix=pltpu.VMEM((256, 128), f32),
        outer=pltpu.VMEM((960, 256), f32),
        sums=pltpu.VMEM((128, 256), f32),
        part=pltpu.VMEM((owners, piece, 128), f32),
        got_row=pltpu.VMEM((n_row, piece, 128), f32),
        sum_row=pltpu.VMEM((piece, 128), f32),
        got_col=pltpu.VMEM((n_col, piece, 128), f32),
        total=pltpu.VMEM((piece, 128), f32),
        got_all=pltpu.VMEM((owners, piece, 128), f32),
        load=dma((4,)),
        row_s=dma((owners,)),
        row_r=dma((n_row,)),
        col_s=dma((n_col,)),
        col_r=dma((n_col,)),
        all_s=dma((n_row,)),
        all_r=dma((owners,)),
    )


def step_kernel(n_row, n_col, owners, *refs):
    (v_ref, cot_ref, taps_ref, bias_ref, proj_ref, w_hbm, ty_hbm, tx_hbm, out_ref, modes_ref, small_ref, *rest) = refs
    nx = 64 * n_row
    names = list(pass_scratch(n_row, n_col))
    first = Group(names, rest[: len(names)])
    second = Group(names, rest[len(names) : 2 * len(names)])
    g = Group(list(common_scratch(n_row, n_col, nx, owners)), rest[2 * len(names) :])
    row_at = lax.axis_index("row")
    col_at = lax.axis_index("col")
    pairs = n_row // 2
    scale = 1.0 / math.sqrt((64 * n_row) * (256 * n_col))
    bf16, f32 = (jnp.bfloat16, jnp.float32)
    pending = []

    loads = [
        pltpu.make_async_copy(v_ref, g.vbuf, g.load.at[0]),
        pltpu.make_async_copy(ty_hbm, g.ty, g.load.at[1]),
        pltpu.make_async_copy(tx_hbm, g.tx, g.load.at[2]),
        pltpu.make_async_copy(w_hbm, g.weight, g.load.at[3]),
    ]
    for load in loads:
        load.start()
    barrier = pltpu.get_barrier_semaphore()
    each(n_col, lambda d: pl.semaphore_signal(
        barrier, inc=1, device_id={"col": lax.rem(col_at + d, n_col)}, device_id_type=pl.DeviceIdType.MESH))
    each(n_row, lambda d: pl.semaphore_signal(
        barrier, inc=1, device_id={"row": lax.rem(row_at + d, n_row)}, device_id_type=pl.DeviceIdType.MESH))
    pl.semaphore_wait(barrier, n_col - 1 + n_row - 1)

    def loop(size, body):
        def step(index, carry):
            body(index)
            return carry

        lax.fori_loop(0, size, step, 0)

    def send_halo_rows(p):
        up = lax.rem(row_at + n_row - 1, n_row)
        down = lax.rem(row_at + 1, n_row)
        copies = [
            push(p.raw.at[pl.ds(32, 32)], p.halo.at[1], p.hs.at[0], p.hr.at[0], "row", up),
            push(p.raw.at[pl.ds(64 * 32, 32)], p.halo.at[0], p.hs.at[1], p.hr.at[1], "row", down),
        ]
        for copy in copies:
            copy.start()
            pending.append(copy.wait_send)
        return copies

    def widen(p, row_copies):
        for copy in row_copies:
            copy.wait_recv()
        above = jnp.where(row_at > 0, 1.0, 0.0)
        below = jnp.where(row_at < n_row - 1, 1.0, 0.0)
        p.raw[0:32] = (p.halo[0].astype(f32) * above).astype(bf16)
        p.raw[65 * 32 : 66 * 32] = (p.halo[1].astype(f32) * below).astype(bf16)
        p.raw[66 * 32 : 68 * 32] = jnp.zeros((64, 256), bf16)
        row = lax.broadcasted_iota(jnp.int32, (32, 256), 0)
        lane = lax.broadcasted_iota(jnp.int32, (32, 256), 1)
        pick = ((row == 0) & (lane == 0)) | ((row == 16) & (lane == 255))
        edges = dot(jnp.where(pick, 1.0, 0.0).astype(bf16), p.raw[...], NT)
        p.edge_out[0] = edges[0:16].astype(bf16)
        p.edge_out[1] = edges[16:32].astype(bf16)
        left = lax.rem(col_at + n_col - 1, n_col)
        right = lax.rem(col_at + 1, n_col)
        copies = [
            push(p.edge_out.at[0], p.edge_in.at[1], p.es.at[0], p.er.at[0], "col", left),
            push(p.edge_out.at[1], p.edge_in.at[0], p.es.at[1], p.er.at[1], "col", right),
        ]
        for copy in copies:
            copy.start()
            pending.append(copy.wait_send)
        return copies

    def fill_wide(p, start, stop):
        row = lax.broadcasted_iota(jnp.int32, (16, 128), 0)
        lane = lax.broadcasted_iota(jnp.int32, (16, 128), 1)
        put_left = jnp.where((row == 0) & (lane == 0) & (col_at > 0), 1.0, 0.0).astype(bf16)
        put_right = jnp.where((row == 0) & (lane == 127) & (col_at < n_col - 1), 1.0, 0.0).astype(bf16)
        lanes = lax.broadcasted_iota(jnp.int32, (128, 128), 1)

        def chunk(q):
            here = p.raw[pl.ds(aligned(q * 128, 128), 128), :].astype(f32)
            from_left = dot(p.edge_in[0, :, pl.ds(aligned(q * 128, 128), 128)], put_left, TN)
            from_right = dot(p.edge_in[1, :, pl.ds(aligned(q * 128, 128), 128)], put_right, TN)
            before = pltpu.roll(here, 1, 1)
            after = pltpu.roll(here, 255, 1)
            before = jnp.concatenate([jnp.where(lanes == 0, from_left, before[:, :128]), before[:, 128:]], axis=1)
            after = jnp.concatenate([after[:, :128], jnp.where(lanes == 127, from_right, after[:, 128:])], axis=1)
            for x in range(4):
                for b, value in enumerate((before, here, after)):
                    base = aligned(q * 384 + 96 * x + 32 * b, 32)
                    p.wide[pl.ds(base, 32), :] = value[32 * x : 32 * x + 32].astype(bf16)

        loop(stop - start, lambda q: chunk(q + start))

    def spread_taps(p, turned):
        row = lax.broadcasted_iota(jnp.int32, (32, 1024), 0)
        lane = lax.broadcasted_iota(jnp.int32, (32, 1024), 1)
        padded = jnp.zeros((32, 1024), f32)
        for m in range(9):
            source = 8 - m if turned else m
            spot = jnp.where(lane == row + 32 * m, 1.0, 0.0).astype(bf16)
            padded = padded + dot(taps_ref[32 * source : 32 * source + 32, :], spot, NN if turned else TN)
        for x in range(8):
            p.taps[32 * x : 32 * x + 32, :] = (pltpu.roll(padded, 96 * x, 1) if x else padded).astype(bf16)

    def convolve(p):
        def block(t):
            rows = p.wide[pl.ds(aligned(t * 768, 16), 1024), :]
            g.cells[pl.ds(aligned(t * 256, 256), 256), :] = dot(p.taps[...], rows, NN)

        loop(8, block)

    def to_modes(p, source, cover, cover_rows):
        own = pltpu.make_async_copy(source(col_at), p.buf1.at[col_at], p.own)
        own.start()
        start, sent, got = exchange("col", col_at, n_col, source, lambda i: p.buf1.at[i], p.s1, p.r1)
        each(n_col, start)
        pending.append(lambda: each(n_col, sent))
        cover()
        own.wait()
        g.acc[...] = dot(g.ty[col_at], p.buf1[col_at], NT)

        def add_block(d):
            origin = got(d)
            g.acc[...] += dot(g.ty[origin], p.buf1[origin], NT)

        each(n_col, add_block)
        whole = g.acc[...]
        upper = whole[:, :128].reshape(n_row, 8, 128)
        lower = whole[:, 128:].reshape(n_row, 8, 128)
        p.snd3[...] = jnp.concatenate([upper, lower], axis=1).astype(bf16)
        start3, sent3, got3 = exchange("row", row_at, n_row, lambda i: p.snd3.at[i], lambda i: p.rcv3.at[i], p.s3, p.r3)
        each(n_row, start3)
        pending.append(lambda: each(n_row, sent3))
        p.rcv3[row_at] = p.snd3[row_at]
        cover_rows()
        each(n_row, got3)
        for s in range(pairs):
            one = p.rcv3[2 * s].astype(f32)
            two = p.rcv3[2 * s + 1].astype(f32)
            even = jnp.where(low, one, pltpu.roll(two, 64, 1))
            odd = jnp.where(low, pltpu.roll(one, 64, 1), two)
            g.rows_x[0:16, 128 * s : 128 * s + 128] = even.astype(bf16)
            g.rows_x[16:32, 128 * s : 128 * s + 128] = odd.astype(bf16)
        both = dot(g.rows_x[...], g.tx[...], NT)
        coeffs = (both[:, :256] + part_swap(both[:, 256:], 1.0)) * scale
        coeffs = jnp.concatenate([coeffs[0:8], coeffs[16:24], coeffs[8:16], coeffs[24:32]], axis=0)
        p.snd5[0] = coeffs[:, :128].astype(bf16)
        p.snd5[1] = coeffs[:, 128:].astype(bf16)
        start5, sent5, got5 = exchange(
            "col", col_at, n_col, lambda i: p.snd5.at[i // 4], lambda i: p.rcv5.at[i], p.s5, p.r5
        )
        each(n_col, start5)
        pending.append(lambda: each(n_col, sent5))
        p.rcv5[col_at] = p.snd5[col_at // 4]
        g.mix[...] = jnp.zeros_like(g.mix)
        each(n_col, got5)
        for i in range(n_col):
            p.modes[32 * i : 32 * i + 32] = pltpu.roll(p.rcv5[i].astype(f32), back_shift, 1)

    def to_grid(p, cover_rows, cover_cells):
        g.mix[...] = pltpu.roll(g.mix[...], quarter, 1)
        for i in range(n_col):
            for odd_channel in range(2):
                upper = g.mix[pl.ds(4 * i + odd_channel, 8, stride=32), :]
                lower = g.mix[pl.ds(4 * i + 2 + odd_channel, 8, stride=32), :]
                p.snd7[i, 16 * odd_channel : 16 * odd_channel + 16] = jnp.concatenate(
                    [upper, lower], axis=0
                ).astype(bf16)
        start7, sent7, got7 = exchange("col", col_at, n_col, lambda i: p.snd7.at[i], lambda i: p.rcv7.at[i], p.s7, p.r7)
        each(n_col, start7)
        pending.append(lambda: each(n_col, sent7))
        p.rcv7[col_at] = p.snd7[col_at]
        each(n_col, got7)
        halves = [sum(p.rcv7[4 * h + q].astype(f32) for q in range(4)) for h in range(2)]
        mixed = jnp.concatenate(halves, axis=1)
        swapped = part_swap(mixed, -1.0)
        operand = jnp.concatenate([mixed, swapped], axis=1).astype(bf16)
        by_rows = dot(operand, g.tx[...], NN)
        for s in range(pairs):
            even = by_rows[0:16, 128 * s : 128 * s + 128]
            odd = by_rows[16:32, 128 * s : 128 * s + 128]
            p.snd9[2 * s] = jnp.where(low, even, pltpu.roll(odd, 64, 1)).astype(bf16)
            p.snd9[2 * s + 1] = jnp.where(low, pltpu.roll(even, 64, 1), odd).astype(bf16)
        start9, sent9, got9 = exchange("row", row_at, n_row, lambda i: p.snd9.at[i], lambda i: p.rcv9.at[i], p.s9, p.r9)
        each(n_row, start9)
        pending.append(lambda: each(n_row, sent9))
        p.rcv9[row_at] = p.snd9[row_at]
        cover_rows()
        each(n_row, got9)
        got = p.rcv9[...].astype(f32)
        own_rows = jnp.concatenate(
            [got[:, :8].reshape(8 * n_row, 128), got[:, 8:].reshape(8 * n_row, 128)], axis=1
        )
        lhs = jnp.transpose(own_rows).astype(bf16)
        start10, sent10, got10 = exchange(
            "col", col_at, n_col, lambda i: p.snd10.at[i], lambda i: p.rcv10.at[i], p.s10, p.r10
        )

        def make_cells(d):
            peer = lax.rem(col_at + d, n_col)
            p.snd10[peer] = dot(lhs, g.ty[peer], NN).astype(bf16)
            start10(d)

        each(n_col, make_cells)
        pending.append(lambda: each(n_col, sent10))
        cover_cells()
        place(col_at, dot(lhs, g.ty[col_at], NN))

        def take(d):
            origin = got10(d)
            place(origin, p.rcv10[origin].astype(f32))

        each(n_col, take)

    def nothing():
        return None

    def rest_of_conv(p):
        fill_wide(p, HALF_FILL, 17)
        convolve(p)

    def place(slot, value):
        for half in range(2):
            g.stage[pl.ds(aligned(half * 2048 + slot * 256, 256), 256), :] = value[:, 128 * half : 128 * half + 128]

    def placed(slot):
        return jnp.concatenate(
            [g.stage[2048 * half + 256 * slot : 2048 * half + 256 * slot + 256] for half in range(2)], axis=1
        )

    def grid_row(x):
        return jnp.concatenate([g.stage[pl.ds(2048 * half + x, 32, stride=64), :] for half in range(2)], axis=1)

    def put_grid_row(x, value):
        for half in range(2):
            g.stage[pl.ds(2048 * half + x, 32, stride=64), :] = value[:, 128 * half : 128 * half + 128]

    low = lax.broadcasted_iota(jnp.int32, (16, 128), 1) < 64
    quarter = lax.rem(col_at, 4) * 32
    back_shift = lax.rem(128 - quarter, 128)

    def cover_field():
        loads[0].wait()
        for i in range(n_col):
            place(i, g.vbuf[i].astype(f32))

        def regroup(x):
            first.raw[pl.ds(aligned(x * 32 + 32, 32), 32), :] = grid_row(x).astype(bf16)

        regroup(0)
        regroup(63)
        row_copies = send_halo_rows(first)

        def inner(x):
            regroup(x + 1)

        loop(62, inner)
        copies = widen(first, row_copies)
        g.cot[...] = cot_ref[...].astype(f32)
        spread_taps(first, False)
        for copy in copies:
            copy.wait_recv()
        fill_wide(first, 0, HALF_FILL)
        loads[1].wait()
        loads[2].wait()

    to_modes(first, lambda i: v_ref.at[i], cover_field, nothing)
    loads[3].wait()
    for kl in range(4):

        def add_channel(i, sums):
            real, imag = sums
            s_re = first.modes[pl.ds(8 * i + kl, 1), :][:, :32]
            s_im = first.modes[pl.ds(8 * i + 4 + kl, 1), :][:, :32]
            w_re = g.weight[kl, 0, i].astype(f32)
            w_im = g.weight[kl, 1, i].astype(f32)
            return (real + (w_re * s_re - w_im * s_im), imag + (w_re * s_im + w_im * s_re))

        zero = jnp.zeros((32, 32), f32)
        real, imag = lax.fori_loop(0, 32, add_channel, (zero, zero))
        factor = jnp.where(row_at * 4 + kl == 0, 1.0, 2.0).astype(f32) * scale
        g.mix[32 * kl : 32 * kl + 32, 0:32] = real.astype(bf16).astype(f32) * factor
        g.mix[128 + 32 * kl : 160 + 32 * kl, 0:32] = imag.astype(bf16).astype(f32) * factor
    to_grid(first, nothing, lambda: rest_of_conv(first))

    def column(ref):
        diagonal = lax.broadcasted_iota(jnp.int32, (32, 32), 0) == lax.broadcasted_iota(jnp.int32, (32, 32), 1)
        value = jnp.sum(jnp.where(diagonal, jnp.broadcast_to(ref[...], (32, 32)), 0.0), axis=1, keepdims=True)
        return jnp.broadcast_to(value, (32, 256))

    bias = column(bias_ref)
    proj = column(proj_ref)

    def activate(x, sums):
        bias_sum, proj_sum = sums
        pre = g.cells[pl.ds(aligned(x * 32, 32), 32), :] + grid_row(x) + bias
        cdf = 0.5 * (1.0 + lax.erf(pre * math.sqrt(0.5)))
        pdf = jnp.exp(-0.5 * pre * pre) * (1.0 / math.sqrt(TWO_PI))
        cot = jnp.broadcast_to(g.cot[pl.ds(x, 1), :], (32, 256))
        grad = (proj * cot) * (cdf + pre * pdf)
        rounded = grad.astype(bf16)
        second.raw[pl.ds(aligned(x * 32 + 32, 32), 32), :] = rounded
        put_grid_row(x, rounded.astype(f32))
        return (bias_sum + grad, proj_sum + (pre * cdf) * cot)

    zero = jnp.zeros((32, 256), f32)
    bias_sum, proj_sum = lax.fori_loop(0, 64, activate, (zero, zero))
    for i in range(n_col):
        second.snd1[i] = placed(i).astype(bf16)

    piece = 80 // owners

    def cover_grad():
        row_copies = send_halo_rows(second)
        g.sums[0:32] = bias_sum
        g.sums[32:64] = proj_sum
        g.sums[64:128] = jnp.zeros((64, 256), f32)
        g.outer[...] = jnp.zeros_like(g.outer)

        def block(t):
            rows = first.wide[pl.ds(aligned(t * 768, 16), 960), :]
            grads = second.raw[pl.ds(aligned(t * 256 + 32, 32), 256), :]
            g.outer[...] += dot(rows, grads, NT)

        loop(8, block)
        copies = widen(second, row_copies)
        lane = lax.broadcasted_iota(jnp.int32, (96, 128), 1)
        taps = []
        for a in range(3):
            total = jnp.zeros((96, 128), f32)
            for x in range(8):
                here = g.outer[96 * (x + a) : 96 * (x + a) + 96, 128 * (x // 4) : 128 * (x // 4) + 128]
                total = total + (pltpu.roll(here, 128 - 32 * (x % 4), 1) if x % 4 else here)
            taps.append(jnp.where(lane < 32, total, 0.0))
        taps = jnp.concatenate(taps, axis=0)
        packed = taps[0:72]
        for q in range(1, 4):
            packed = packed + pltpu.roll(taps[72 * q : 72 * q + 72], 32 * q, 1)
        lanes_sum = lax.dot_general(
            jnp.ones((8, 256), f32), g.sums[...], NT, precision=HIGH, preferred_element_type=f32
        )
        g.part[...] = (jnp.concatenate([packed, lanes_sum], axis=0) * scale).reshape(owners, piece, 128)
        for t in range(owners):

            @pl.when(row_at != t)
            def _():
                push(g.part.at[t], g.got_row.at[row_at], g.row_s.at[t], g.row_r.at[row_at], "row", t).start()

        spread_taps(second, True)
        for copy in copies:
            copy.wait_recv()
        fill_wide(second, 0, HALF_FILL)

    def sum_rows():
        @pl.when(row_at < owners)
        def _():
            g.got_row[row_at] = g.part[row_at]

            def wait(d):
                origin = lax.rem(row_at + d, n_row)
                push(g.part.at[0], g.got_row.at[origin], g.row_s.at[0], g.row_r.at[origin], "row", origin).wait_recv()

            each(n_row, wait)
            g.sum_row[...] = jnp.sum(g.got_row[...], axis=0)
            g.got_col[col_at] = g.sum_row[...]
            start, _, _ = exchange(
                "col", col_at, n_col, lambda i: g.sum_row, lambda i: g.got_col.at[i], g.col_s, g.col_r
            )
            each(n_col, start)

    def sum_cols():
        @pl.when(row_at < owners)
        def _():
            _, sent, got = exchange(
                "col", col_at, n_col, lambda i: g.sum_row, lambda i: g.got_col.at[i], g.col_s, g.col_r
            )
            each(n_col, got)
            each(n_col, sent)
            g.total[...] = jnp.sum(g.got_col[...], axis=0)
            g.got_all[row_at] = g.total[...]

            def send(d):
                peer = lax.rem(row_at + d, n_row)
                push(g.total, g.got_all.at[row_at], g.all_s.at[d], g.all_r.at[row_at], "row", peer).start()

            each(n_row, send)

    to_modes(second, lambda i: second.snd1.at[i], cover_grad, sum_rows)
    own_mode = lax.broadcasted_iota(jnp.int32, (256, 128), 0) & 3
    second.modes[...] = second.modes[...] * jnp.where(row_at * 4 + own_mode == 0, 1.0, 2.0)
    for kl in range(4):
        g_re = second.modes[pl.ds(kl, 32, stride=8), :][:, :32]
        g_im = second.modes[pl.ds(4 + kl, 32, stride=8), :][:, :32]

        def one_channel(i, carry):
            w_re = g.weight[kl, 0, i].astype(f32)
            w_im = g.weight[kl, 1, i].astype(f32)
            b_re = jnp.sum(w_re * g_re + w_im * g_im, axis=0, keepdims=True)
            b_im = jnp.sum(w_re * g_im - w_im * g_re, axis=0, keepdims=True)
            g.mix[pl.ds(32 * kl + i, 1), 0:32] = b_re.astype(bf16).astype(f32) * scale
            g.mix[pl.ds(128 + 32 * kl + i, 1), 0:32] = b_im.astype(bf16).astype(f32) * scale
            return carry

        lax.fori_loop(0, 32, one_channel, 0)
    to_grid(second, sum_cols, lambda: rest_of_conv(second))

    def finish(x):
        put_grid_row(x, g.cells[pl.ds(aligned(x * 32, 32), 32), :] + grid_row(x))

    modes_ref[0] = first.modes[...]
    modes_ref[1] = second.modes[...]
    loop(64, finish)
    for i in range(n_col):
        out_ref[256 * i : 256 * i + 256] = placed(i)
    for t in range(owners):

        @pl.when(row_at != t)
        def _():
            arrived = push(g.part.at[t], g.got_all.at[t], g.row_s.at[t], g.all_r.at[t], "row", t)
            arrived.wait_recv()
            arrived.wait_send()

    @pl.when(row_at < owners)
    def _():
        def sent(d):
            peer = lax.rem(row_at + d, n_row)
            push(g.total, g.got_all.at[row_at], g.all_s.at[d], g.all_r.at[row_at], "row", peer).wait_send()

        each(n_row, sent)

    small_ref[...] = g.got_all[...].reshape(80, 128)
    for wait in pending:
        wait()


def outputs_kernel(cells_ref, modes_ref, small_ref, out_ref, gspec_ref, conv_ref, bias_ref, proj_ref):
    out_ref[...] = cells_ref[...]
    kl = pl.program_id(0) // 2
    first = lax.rem(pl.program_id(0), 2) * 16
    g_re = modes_ref[pl.ds(256 + kl, 32, stride=8), :][:, :32]
    g_im = modes_ref[pl.ds(260 + kl, 32, stride=8), :][:, :32]
    for i in range(16):
        s_re = modes_ref[pl.ds(8 * (first + i) + kl, 1), :][:, :32]
        s_im = modes_ref[pl.ds(8 * (first + i) + 4 + kl, 1), :][:, :32]
        gspec_ref[0, 0, i] = g_re * s_re + g_im * s_im
        gspec_ref[0, 1, i] = g_im * s_re - g_re * s_im

    @pl.when(pl.program_id(0) == 0)
    def _():
        for q in range(4):
            rows = small_ref[0:72]
            conv_ref[72 * q : 72 * q + 72] = (pltpu.roll(rows, 128 - 32 * q, 1) if q else rows)[:, :32]
        rows = small_ref[72:80]
        bias_ref[...] = rows[0:1, :32]
        proj_ref[...] = pltpu.roll(rows, 96, 1)[0:1, :32]


def per_device(n_row, n_col, ocean_field, cotangent, conv_weight, conv_bias, projection, mode_weight):
    chans, rows_dev, cols_dev = ocean_field.shape
    ky_dev = mode_weight.shape[0]
    kx_all = mode_weight.shape[4] * n_col
    owners = min(10, n_row)
    ty, tx = (jnp.asarray(t) for t in tables(n_row, n_col, ky_dev, rows_dev, cols_dev, kx_all))
    vmem = pl.BlockSpec(memory_space=pltpu.VMEM)
    hbm = pl.BlockSpec(memory_space=pl.ANY)
    one = pass_scratch(n_row, n_col)
    scratch = list(one.values()) * 2 + list(common_scratch(n_row, n_col, rows_dev * n_row, owners).values())
    cells, modes, small = pl.pallas_call(
        functools.partial(step_kernel, n_row, n_col, owners),
        out_shape=[
            jax.ShapeDtypeStruct((chans * rows_dev, cols_dev), jnp.float32),
            jax.ShapeDtypeStruct((2, 256, 128), jnp.float32),
            jax.ShapeDtypeStruct((80, 128), jnp.float32),
        ],
        in_specs=[hbm, vmem, vmem, vmem, vmem, hbm, hbm, hbm],
        out_specs=[vmem, vmem, vmem],
        scratch_shapes=scratch,
        compiler_params=pltpu.CompilerParams(
            collective_id=0, has_side_effects=True, vmem_limit_bytes=VMEM_BYTES
        ),
        name="layer_step",
    )(
        ocean_field.reshape(n_col, 256, cols_dev),
        cotangent,
        conv_weight.reshape(9 * chans, chans),
        conv_bias.reshape(1, chans),
        projection.reshape(1, chans),
        mode_weight,
        ty,
        tx,
    )
    whole = lambda *shape: pl.BlockSpec(shape, lambda t: (0,) * len(shape))
    grad_input, grad_spec, grad_conv, grad_bias, grad_proj = pl.pallas_call(
        outputs_kernel,
        grid=(8,),
        out_shape=[
            jax.ShapeDtypeStruct((chans * rows_dev, cols_dev), jnp.float32),
            jax.ShapeDtypeStruct(mode_weight.shape, jnp.float32),
            jax.ShapeDtypeStruct((9 * chans, chans), jnp.float32),
            jax.ShapeDtypeStruct((1, chans), jnp.float32),
            jax.ShapeDtypeStruct((1, chans), jnp.float32),
        ],
        in_specs=[pl.BlockSpec((256, 256), lambda t: (t, 0)), whole(512, 128), whole(80, 128)],
        out_specs=[
            pl.BlockSpec((256, 256), lambda t: (t, 0)),
            pl.BlockSpec((1, 2, 16, 32, 32), lambda t: (t // 2, 0, t % 2, 0, 0)),
            whole(9 * chans, chans),
            whole(1, chans),
            whole(1, chans),
        ],
        compiler_params=pltpu.CompilerParams(vmem_limit_bytes=VMEM_BYTES),
        name="layer_outputs",
    )(cells, modes.reshape(512, 128), small)
    return (
        grad_input.reshape(ocean_field.shape),
        grad_spec,
        grad_conv.reshape(conv_weight.shape),
        grad_bias.reshape(chans),
        grad_proj.reshape(chans),
    )


def solution(mesh):
    placed = (
        P(None, "row", "col"),
        P("row", "col"),
        P(),
        P(),
        P(),
        P("row", None, None, None, "col"),
    )
    return jax.shard_map(
        functools.partial(per_device, mesh.shape["row"], mesh.shape["col"]),
        mesh=mesh,
        in_specs=placed,
        out_specs=(P(None, "row", "col"), P("row", None, None, None, "col"), P(), P(), P()),
        check_vma=False,
    )
```

```python
import functools
import math

import jax
import jax.numpy as jnp
import ml_dtypes
import numpy as np
from jax import lax
from jax.experimental import pallas as pl
from jax.experimental.pallas import tpu as pltpu
from jax.sharding import PartitionSpec as P

TWO_PI = 2.0 * math.pi
HIGH = lax.Precision.HIGHEST
HALF_FILL = 8
VMEM_BYTES = 56 * 1024 * 1024


def angle_pair(products, period):
    angles = (products % period).astype(np.float32) * np.float32(TWO_PI / period)
    return (np.cos(angles).astype(ml_dtypes.bfloat16), np.sin(angles).astype(ml_dtypes.bfloat16))


def tables(n_row, n_col, ky_dev, rows_dev, cols_dev, kx_all):
    modes, nx, ny = (ky_dev * n_row, rows_dev * n_row, cols_dev * n_col)
    cosine, sine = angle_pair(np.arange(modes)[:, None] * np.arange(ny)[None, :], ny)
    ty = np.stack([cosine.reshape(n_row, ky_dev, ny), -sine.reshape(n_row, ky_dev, ny)], axis=1)
    ty = ty.reshape(2 * modes, n_col, cols_dev).transpose(1, 0, 2)
    ids = np.arange(kx_all)
    freqs = np.where(ids < modes, ids, ids - 2 * modes) % nx
    cosine, sine = angle_pair(freqs[:, None] * np.arange(nx)[None, :], nx)
    return np.ascontiguousarray(ty), np.concatenate([cosine, sine], axis=0)


NT = (((1,), (1,)), ((), ()))
NN = (((1,), (0,)), ((), ()))
TN = (((0,), (0,)), ((), ()))


def dot(a, b, dims):
    return lax.dot_general(a, b, dims, preferred_element_type=jnp.float32)


def exchange(axis, me, size, source, target, send_sem, recv_sem):
    def copy(step, peer, slot):
        return pltpu.make_async_remote_copy(
            src_ref=source(peer),
            dst_ref=target(slot),
            send_sem=send_sem.at[step],
            recv_sem=recv_sem.at[step],
            device_id={axis: peer},
            device_id_type=pl.DeviceIdType.MESH,
        )

    def start(step):
        copy(step, lax.rem(me + step, size), me).start()

    def wait_send(step):
        copy(step, lax.rem(me + step, size), me).wait_send()

    def wait_recv(step):
        origin = lax.rem(me + size - step, size)
        copy(step, lax.rem(me + step, size), origin).wait_recv()
        return origin

    return start, wait_send, wait_recv


def each(size, body):
    def step(index, carry):
        body(index)
        return carry

    lax.fori_loop(1, size, step, 0)


def part_swap(value, sign):
    rows = value.shape[0]
    is_real = (lax.broadcasted_iota(jnp.int32, value.shape, 0) & 4) == 0
    after = pltpu.roll(value, rows - 4, 0)
    before = pltpu.roll(value, 4, 0)
    return jnp.where(is_real, sign * after, -sign * before)


class Group:
    def __init__(self, names, refs):
        for name, ref in zip(names, refs):
            setattr(self, name, ref)


def push(src, dst, send_sem, recv_sem, axis, peer):
    return pltpu.make_async_remote_copy(
        src_ref=src,
        dst_ref=dst,
        send_sem=send_sem,
        recv_sem=recv_sem,
        device_id={axis: peer},
        device_id_type=pl.DeviceIdType.MESH,
    )


def aligned(value, to):
    return pl.multiple_of(value, to)


def pass_scratch(n_row, n_col):
    bf16, f32 = (jnp.bfloat16, jnp.float32)
    dma = pltpu.SemaphoreType.DMA
    found = dict(
        snd1=pltpu.VMEM((n_col, 256, 256), bf16),
        buf1=pltpu.VMEM((n_col, 256, 256), bf16),
        snd3=pltpu.VMEM((n_row, 16, 128), bf16),
        rcv3=pltpu.VMEM((n_row, 16, 128), bf16),
        snd5=pltpu.VMEM((2, 32, 128), bf16),
        rcv5=pltpu.VMEM((n_col, 32, 128), bf16),
        modes=pltpu.VMEM((256, 128), f32),
        snd7=pltpu.VMEM((n_col, 32, 128), bf16),
        rcv7=pltpu.VMEM((n_col, 32, 128), bf16),
        snd9=pltpu.VMEM((n_row, 16, 128), bf16),
        rcv9=pltpu.VMEM((n_row, 16, 128), bf16),
        snd10=pltpu.VMEM((n_col, 256, 256), bf16),
        rcv10=pltpu.VMEM((n_col, 256, 256), bf16),
        raw=pltpu.VMEM((68 * 32, 256), bf16),
        halo=pltpu.VMEM((2, 32, 256), bf16),
        edge_out=pltpu.VMEM((2, 16, 68 * 32), bf16),
        edge_in=pltpu.VMEM((2, 16, 68 * 32), bf16),
        wide=pltpu.VMEM((68 * 96, 256), bf16),
        taps=pltpu.VMEM((256, 1024), bf16),
        own=dma,
        hs=dma((2,)),
        hr=dma((2,)),
        es=dma((2,)),
        er=dma((2,)),
    )
    for step, size in ((1, n_col), (3, n_row), (5, n_col), (7, n_col), (9, n_row), (10, n_col)):
        found["s%d" % step] = dma((size,))
        found["r%d" % step] = dma((size,))
    return found


def common_scratch(n_row, n_col, nx, owners):
    bf16, f32 = (jnp.bfloat16, jnp.float32)
    dma = pltpu.SemaphoreType.DMA
    piece = 80 // owners
    return dict(
        vbuf=pltpu.VMEM((n_col, 256, 256), bf16),
        ty=pltpu.VMEM((n_col, 8 * n_row, 256), bf16),
        tx=pltpu.VMEM((512, nx), bf16),
        weight=pltpu.VMEM((4, 2, 32, 32, 32), bf16),
        stage=pltpu.VMEM((4096, 128), f32),
        bias=pltpu.VMEM((32, 256), f32),
        proj=pltpu.VMEM((32, 256), f32),
        bias_rows=pltpu.VMEM((256, 256), f32),
        proj_rows=pltpu.VMEM((256, 256), f32),
        cot=pltpu.VMEM((64, 256), f32),
        acc=pltpu.VMEM((8 * n_row, 256), f32),
        rows_x=pltpu.VMEM((32, nx), bf16),
        mix=pltpu.VMEM((256, 128), f32),
        outer=pltpu.VMEM((960, 256), f32),
        sums=pltpu.VMEM((128, 256), f32),
        part=pltpu.VMEM((owners, piece, 128), f32),
        got_row=pltpu.VMEM((n_row, piece, 128), f32),
        sum_row=pltpu.VMEM((piece, 128), f32),
        got_col=pltpu.VMEM((n_col, piece, 128), f32),
        total=pltpu.VMEM((piece, 128), f32),
        got_all=pltpu.VMEM((owners, piece, 128), f32),
        load=dma((4,)),
        row_s=dma((owners,)),
        row_r=dma((n_row,)),
        col_s=dma((n_col,)),
        col_r=dma((n_col,)),
        all_s=dma((n_row,)),
        all_r=dma((owners,)),
    )


def step_kernel(n_row, n_col, owners, *refs):
    (v_ref, cot_ref, taps_ref, bias_ref, proj_ref, w_hbm, ty_hbm, tx_hbm, out_ref, modes_ref, small_ref, *rest) = refs
    nx = 64 * n_row
    names = list(pass_scratch(n_row, n_col))
    first = Group(names, rest[: len(names)])
    second = Group(names, rest[len(names) : 2 * len(names)])
    g = Group(list(common_scratch(n_row, n_col, nx, owners)), rest[2 * len(names) :])
    row_at = lax.axis_index("row")
    col_at = lax.axis_index("col")
    pairs = n_row // 2
    scale = 1.0 / math.sqrt((64 * n_row) * (256 * n_col))
    bf16, f32 = (jnp.bfloat16, jnp.float32)
    pending = []

    loads = [
        pltpu.make_async_copy(v_ref, g.vbuf, g.load.at[0]),
        pltpu.make_async_copy(ty_hbm, g.ty, g.load.at[1]),
        pltpu.make_async_copy(tx_hbm, g.tx, g.load.at[2]),
        pltpu.make_async_copy(w_hbm, g.weight, g.load.at[3]),
    ]
    for load in loads:
        load.start()
    barrier = pltpu.get_barrier_semaphore()
    each(n_col, lambda d: pl.semaphore_signal(
        barrier, inc=1, device_id={"col": lax.rem(col_at + d, n_col)}, device_id_type=pl.DeviceIdType.MESH))
    each(n_row, lambda d: pl.semaphore_signal(
        barrier, inc=1, device_id={"row": lax.rem(row_at + d, n_row)}, device_id_type=pl.DeviceIdType.MESH))
    pl.semaphore_wait(barrier, n_col - 1 + n_row - 1)

    def loop(size, body):
        def step(index, carry):
            body(index)
            return carry

        lax.fori_loop(0, size, step, 0)

    def send_halo_rows(p):
        up = lax.rem(row_at + n_row - 1, n_row)
        down = lax.rem(row_at + 1, n_row)
        copies = [
            push(p.raw.at[pl.ds(32, 32)], p.halo.at[1], p.hs.at[0], p.hr.at[0], "row", up),
            push(p.raw.at[pl.ds(64 * 32, 32)], p.halo.at[0], p.hs.at[1], p.hr.at[1], "row", down),
        ]
        for copy in copies:
            copy.start()
            pending.append(copy.wait_send)
        return copies

    def widen(p, row_copies):
        for copy in row_copies:
            copy.wait_recv()
        above = jnp.where(row_at > 0, 1.0, 0.0)
        below = jnp.where(row_at < n_row - 1, 1.0, 0.0)
        p.raw[0:32] = (p.halo[0].astype(f32) * above).astype(bf16)
        p.raw[65 * 32 : 66 * 32] = (p.halo[1].astype(f32) * below).astype(bf16)
        p.raw[66 * 32 : 68 * 32] = jnp.zeros((64, 256), bf16)
        row = lax.broadcasted_iota(jnp.int32, (32, 256), 0)
        lane = lax.broadcasted_iota(jnp.int32, (32, 256), 1)
        pick = ((row == 0) & (lane == 0)) | ((row == 16) & (lane == 255))
        edges = dot(jnp.where(pick, 1.0, 0.0).astype(bf16), p.raw[...], NT)
        p.edge_out[0] = edges[0:16].astype(bf16)
        p.edge_out[1] = edges[16:32].astype(bf16)
        left = lax.rem(col_at + n_col - 1, n_col)
        right = lax.rem(col_at + 1, n_col)
        copies = [
            push(p.edge_out.at[0], p.edge_in.at[1], p.es.at[0], p.er.at[0], "col", left),
            push(p.edge_out.at[1], p.edge_in.at[0], p.es.at[1], p.er.at[1], "col", right),
        ]
        for copy in copies:
            copy.start()
            pending.append(copy.wait_send)
        return copies

    def fill_wide(p, start, stop):
        row = lax.broadcasted_iota(jnp.int32, (16, 128), 0)
        lane = lax.broadcasted_iota(jnp.int32, (16, 128), 1)
        put_left = jnp.where((row == 0) & (lane == 0) & (col_at > 0), 1.0, 0.0).astype(bf16)
        put_right = jnp.where((row == 0) & (lane == 127) & (col_at < n_col - 1), 1.0, 0.0).astype(bf16)
        lanes = lax.broadcasted_iota(jnp.int32, (128, 128), 1)

        def chunk(q):
            here = p.raw[pl.ds(aligned(q * 128, 128), 128), :].astype(f32)
            from_left = dot(p.edge_in[0, :, pl.ds(aligned(q * 128, 128), 128)], put_left, TN)
            from_right = dot(p.edge_in[1, :, pl.ds(aligned(q * 128, 128), 128)], put_right, TN)
            before = pltpu.roll(here, 1, 1)
            after = pltpu.roll(here, 255, 1)
            before = jnp.concatenate([jnp.where(lanes == 0, from_left, before[:, :128]), before[:, 128:]], axis=1)
            after = jnp.concatenate([after[:, :128], jnp.where(lanes == 127, from_right, after[:, 128:])], axis=1)
            for x in range(4):
                for b, value in enumerate((before, here, after)):
                    base = aligned(q * 384 + 96 * x + 32 * b, 32)
                    p.wide[pl.ds(base, 32), :] = value[32 * x : 32 * x + 32].astype(bf16)

        loop(stop - start, lambda q: chunk(q + start))

    def spread_taps(p, turned):
        row = lax.broadcasted_iota(jnp.int32, (32, 1024), 0)
        lane = lax.broadcasted_iota(jnp.int32, (32, 1024), 1)
        padded = jnp.zeros((32, 1024), f32)
        for m in range(9):
            source = 8 - m if turned else m
            spot = jnp.where(lane == row + 32 * m, 1.0, 0.0).astype(bf16)
            padded = padded + dot(taps_ref[32 * source : 32 * source + 32, :], spot, NN if turned else TN)
        for x in range(8):
            p.taps[32 * x : 32 * x + 32, :] = (pltpu.roll(padded, 96 * x, 1) if x else padded).astype(bf16)

    def convolve(p):
        def block(t):
            rows = p.wide[pl.ds(aligned(t * 768, 16), 1024), :]
            result = dot(p.taps[...], rows, NN)
            for x in range(8):
                put_grid_row(8 * t + x, result[32 * x : 32 * x + 32])

        loop(8, block)

    def to_modes(p, source, started, cover, cover_rows):
        own = pltpu.make_async_copy(source(col_at), p.buf1.at[col_at], p.own)
        own.start()
        start, sent, got = exchange("col", col_at, n_col, source, lambda i: p.buf1.at[i], p.s1, p.r1)
        if not started:
            each(n_col, start)
        pending.append(lambda: each(n_col, sent))
        cover()
        own.wait()
        g.acc[...] = dot(g.ty[col_at], p.buf1[col_at], NT)

        def add_block(d):
            origin = got(d)
            g.acc[...] += dot(g.ty[origin], p.buf1[origin], NT)

        each(n_col, add_block)
        whole = g.acc[...]
        upper = whole[:, :128].reshape(n_row, 8, 128)
        lower = whole[:, 128:].reshape(n_row, 8, 128)
        p.snd3[...] = jnp.concatenate([upper, lower], axis=1).astype(bf16)
        start3, sent3, got3 = exchange("row", row_at, n_row, lambda i: p.snd3.at[i], lambda i: p.rcv3.at[i], p.s3, p.r3)
        each(n_row, start3)
        pending.append(lambda: each(n_row, sent3))
        p.rcv3[row_at] = p.snd3[row_at]
        cover_rows()
        each(n_row, got3)
        for s in range(pairs):
            one = p.rcv3[2 * s].astype(f32)
            two = p.rcv3[2 * s + 1].astype(f32)
            even = jnp.where(low, one, pltpu.roll(two, 64, 1))
            odd = jnp.where(low, pltpu.roll(one, 64, 1), two)
            g.rows_x[0:16, 128 * s : 128 * s + 128] = even.astype(bf16)
            g.rows_x[16:32, 128 * s : 128 * s + 128] = odd.astype(bf16)
        both = dot(g.rows_x[...], g.tx[...], NT)
        coeffs = (both[:, :256] + part_swap(both[:, 256:], 1.0)) * scale
        coeffs = jnp.concatenate([coeffs[0:8], coeffs[16:24], coeffs[8:16], coeffs[24:32]], axis=0)
        p.snd5[0] = coeffs[:, :128].astype(bf16)
        p.snd5[1] = coeffs[:, 128:].astype(bf16)
        start5, sent5, got5 = exchange(
            "col", col_at, n_col, lambda i: p.snd5.at[i // 4], lambda i: p.rcv5.at[i], p.s5, p.r5
        )
        each(n_col, start5)
        pending.append(lambda: each(n_col, sent5))
        p.rcv5[col_at] = p.snd5[col_at // 4]
        g.mix[...] = jnp.zeros_like(g.mix)
        each(n_col, got5)
        for i in range(n_col):
            p.modes[32 * i : 32 * i + 32] = pltpu.roll(p.rcv5[i].astype(f32), back_shift, 1)

    def to_grid(p, cover_rows, cover_cells, use):
        g.mix[...] = pltpu.roll(g.mix[...], quarter, 1)
        for i in range(n_col):
            for odd_channel in range(2):
                upper = g.mix[pl.ds(4 * i + odd_channel, 8, stride=32), :]
                lower = g.mix[pl.ds(4 * i + 2 + odd_channel, 8, stride=32), :]
                p.snd7[i, 16 * odd_channel : 16 * odd_channel + 16] = jnp.concatenate(
                    [upper, lower], axis=0
                ).astype(bf16)
        start7, sent7, got7 = exchange("col", col_at, n_col, lambda i: p.snd7.at[i], lambda i: p.rcv7.at[i], p.s7, p.r7)
        each(n_col, start7)
        pending.append(lambda: each(n_col, sent7))
        p.rcv7[col_at] = p.snd7[col_at]
        each(n_col, got7)
        halves = [sum(p.rcv7[4 * h + q].astype(f32) for q in range(4)) for h in range(2)]
        mixed = jnp.concatenate(halves, axis=1)
        swapped = part_swap(mixed, -1.0)
        operand = jnp.concatenate([mixed, swapped], axis=1).astype(bf16)
        by_rows = dot(operand, g.tx[...], NN)
        for s in range(pairs):
            even = by_rows[0:16, 128 * s : 128 * s + 128]
            odd = by_rows[16:32, 128 * s : 128 * s + 128]
            p.snd9[2 * s] = jnp.where(low, even, pltpu.roll(odd, 64, 1)).astype(bf16)
            p.snd9[2 * s + 1] = jnp.where(low, pltpu.roll(even, 64, 1), odd).astype(bf16)
        start9, sent9, got9 = exchange("row", row_at, n_row, lambda i: p.snd9.at[i], lambda i: p.rcv9.at[i], p.s9, p.r9)
        each(n_row, start9)
        pending.append(lambda: each(n_row, sent9))
        p.rcv9[row_at] = p.snd9[row_at]
        cover_rows()
        each(n_row, got9)
        got = p.rcv9[...].astype(f32)
        own_rows = jnp.concatenate(
            [got[:, :8].reshape(8 * n_row, 128), got[:, 8:].reshape(8 * n_row, 128)], axis=1
        )
        lhs = jnp.transpose(own_rows).astype(bf16)
        start10, sent10, got10 = exchange(
            "col", col_at, n_col, lambda i: p.snd10.at[i], lambda i: p.rcv10.at[i], p.s10, p.r10
        )

        def make_cells(d):
            peer = lax.rem(col_at + d, n_col)
            p.snd10[peer] = dot(lhs, g.ty[peer], NN).astype(bf16)
            start10(d)

        each(n_col, make_cells)
        pending.append(lambda: each(n_col, sent10))
        cover_cells()
        use(col_at, dot(lhs, g.ty[col_at], NN), 0)

        def take(d):
            origin = got10(d)
            use(origin, p.rcv10[origin].astype(f32), d)

        each(n_col, take)

    def first_fill(p):
        for copy in p.edge_copies:
            copy.wait_recv()
        fill_wide(p, 0, HALF_FILL)

    def rest_of_conv(p):
        fill_wide(p, HALF_FILL, 17)
        convolve(p)

    def regroup(p):
        def one(x):
            p.raw[pl.ds(aligned(x * 32 + 32, 32), 32), :] = grid_row(x).astype(bf16)

        one(0)
        one(63)
        p.row_copies = send_halo_rows(p)
        loop(62, lambda x: one(x + 1))

    def widen_now(p):
        p.edge_copies = widen(p, p.row_copies)

    def place(slot, value):
        for half in range(2):
            g.stage[pl.ds(aligned(half * 2048 + slot * 256, 256), 256), :] = value[:, 128 * half : 128 * half + 128]

    def placed(slot):
        return jnp.concatenate(
            [g.stage[pl.ds(aligned(half * 2048 + slot * 256, 256), 256), :] for half in range(2)], axis=1
        )

    def grid_row(x):
        return jnp.concatenate([g.stage[pl.ds(2048 * half + x, 32, stride=64), :] for half in range(2)], axis=1)

    def put_grid_row(x, value):
        for half in range(2):
            g.stage[pl.ds(2048 * half + x, 32, stride=64), :] = value[:, 128 * half : 128 * half + 128]

    low = lax.broadcasted_iota(jnp.int32, (16, 128), 1) < 64
    quarter = lax.rem(col_at, 4) * 32
    back_shift = lax.rem(128 - quarter, 128)

    def cover_field():
        loads[0].wait()
        for i in range(n_col):
            place(i, g.vbuf[i].astype(f32))

        regroup(first)
        g.cot[...] = cot_ref[...].astype(f32)
        spread_taps(first, False)
        g.bias[...] = column(bias_ref)
        g.proj[...] = column(proj_ref)
        loads[1].wait()
        loads[2].wait()

    def column(ref):
        diagonal = lax.broadcasted_iota(jnp.int32, (32, 32), 0) == lax.broadcasted_iota(jnp.int32, (32, 32), 1)
        value = jnp.sum(jnp.where(diagonal, jnp.broadcast_to(ref[...], (32, 32)), 0.0), axis=1, keepdims=True)
        return jnp.broadcast_to(value, (32, 256))

    to_modes(first, lambda i: v_ref.at[i], False, cover_field, lambda: widen_now(first))
    loads[3].wait()
    for kl in range(4):

        def add_channel(i, sums):
            real, imag = sums
            s_re = first.modes[pl.ds(8 * i + kl, 1), :][:, :32]
            s_im = first.modes[pl.ds(8 * i + 4 + kl, 1), :][:, :32]
            w_re = g.weight[kl, 0, i].astype(f32)
            w_im = g.weight[kl, 1, i].astype(f32)
            return (real + (w_re * s_re - w_im * s_im), imag + (w_re * s_im + w_im * s_re))

        zero = jnp.zeros((32, 32), f32)
        real, imag = lax.fori_loop(0, 32, add_channel, (zero, zero))
        factor = jnp.where(row_at * 4 + kl == 0, 1.0, 2.0).astype(f32) * scale
        g.mix[32 * kl : 32 * kl + 32, 0:32] = real.astype(bf16).astype(f32) * factor
        g.mix[128 + 32 * kl : 160 + 32 * kl, 0:32] = imag.astype(bf16).astype(f32) * factor

    back_start, _, _ = exchange(
        "col", col_at, n_col, lambda i: second.snd1.at[i], lambda i: second.buf1.at[i], second.s1, second.r1
    )

    def activate(slot, cells, d):
        conv = placed(slot)
        rounded = []
        for ch in range(4):
            channel = slot * 4 + ch
            rows = slice(64 * ch, 64 * ch + 64)
            bias = jnp.broadcast_to(g.bias[pl.ds(channel, 1), :], (64, 256))
            proj = jnp.broadcast_to(g.proj[pl.ds(channel, 1), :], (64, 256))
            pre = conv[rows] + cells[rows] + bias
            cdf = 0.5 * (1.0 + lax.erf(pre * math.sqrt(0.5)))
            pdf = jnp.exp(-0.5 * pre * pre) * (1.0 / math.sqrt(TWO_PI))
            grad = (proj * g.cot[...]) * (cdf + pre * pdf)
            rounded.append(grad.astype(bf16))
            second.snd1[slot, 64 * ch : 64 * ch + 64] = rounded[ch]
            at = pl.ds(aligned(channel * 8, 8), 8)
            g.bias_rows[at, :] = jnp.sum(grad.reshape(8, 8, 256), axis=0)
            g.proj_rows[at, :] = jnp.sum(((pre * cdf) * g.cot[...]).reshape(8, 8, 256), axis=0)
        if not isinstance(d, int):
            back_start(n_col - d)
        place(slot, jnp.concatenate(rounded, axis=0).astype(f32))

    to_grid(first, lambda: first_fill(first), lambda: rest_of_conv(first), activate)

    piece = 80 // owners

    def cover_grad():
        regroup(second)
        of_channel = (lax.broadcasted_iota(jnp.int32, (32, 256), 1) // 8) == lax.broadcasted_iota(
            jnp.int32, (32, 256), 0
        )
        gather = jnp.where(of_channel, 1.0, 0.0)
        for at, rows in ((0, g.bias_rows), (32, g.proj_rows)):
            g.sums[at : at + 32] = lax.dot_general(
                gather, rows[...], NN, precision=HIGH, preferred_element_type=f32
            )
        g.sums[64:128] = jnp.zeros((64, 256), f32)
        g.outer[...] = jnp.zeros_like(g.outer)

        def block(t):
            rows = first.wide[pl.ds(aligned(t * 768, 16), 960), :]
            grads = second.raw[pl.ds(aligned(t * 256 + 32, 32), 256), :]
            g.outer[...] += dot(rows, grads, NT)

        loop(8, block)
        lane = lax.broadcasted_iota(jnp.int32, (96, 128), 1)
        taps = []
        for a in range(3):
            total = jnp.zeros((96, 128), f32)
            for x in range(8):
                here = g.outer[96 * (x + a) : 96 * (x + a) + 96, 128 * (x // 4) : 128 * (x // 4) + 128]
                total = total + (pltpu.roll(here, 128 - 32 * (x % 4), 1) if x % 4 else here)
            taps.append(jnp.where(lane < 32, total, 0.0))
        taps = jnp.concatenate(taps, axis=0)
        packed = taps[0:72]
        for q in range(1, 4):
            packed = packed + pltpu.roll(taps[72 * q : 72 * q + 72], 32 * q, 1)
        lanes_sum = lax.dot_general(
            jnp.ones((8, 256), f32), g.sums[...], NT, precision=HIGH, preferred_element_type=f32
        )
        g.part[...] = (jnp.concatenate([packed, lanes_sum], axis=0) * scale).reshape(owners, piece, 128)
        for t in range(owners):

            @pl.when(row_at != t)
            def _():
                push(g.part.at[t], g.got_row.at[row_at], g.row_s.at[t], g.row_r.at[row_at], "row", t).start()

        spread_taps(second, True)

    def sum_rows():
        @pl.when(row_at < owners)
        def _():
            g.got_row[row_at] = g.part[row_at]

            def wait(d):
                origin = lax.rem(row_at + d, n_row)
                push(g.part.at[0], g.got_row.at[origin], g.row_s.at[0], g.row_r.at[origin], "row", origin).wait_recv()

            each(n_row, wait)
            g.sum_row[...] = jnp.sum(g.got_row[...], axis=0)
            g.got_col[col_at] = g.sum_row[...]
            start, _, _ = exchange(
                "col", col_at, n_col, lambda i: g.sum_row, lambda i: g.got_col.at[i], g.col_s, g.col_r
            )
            each(n_col, start)

    def sum_cols():
        @pl.when(row_at < owners)
        def _():
            _, sent, got = exchange(
                "col", col_at, n_col, lambda i: g.sum_row, lambda i: g.got_col.at[i], g.col_s, g.col_r
            )
            each(n_col, got)
            each(n_col, sent)
            g.total[...] = jnp.sum(g.got_col[...], axis=0)
            g.got_all[row_at] = g.total[...]

            def send(d):
                peer = lax.rem(row_at + d, n_row)
                push(g.total, g.got_all.at[row_at], g.all_s.at[d], g.all_r.at[row_at], "row", peer).start()

            each(n_row, send)

    def cover_rows_back():
        widen_now(second)
        sum_rows()

    def cover_rows_out():
        first_fill(second)
        sum_cols()

    def write_out(slot, cells, d):
        out_ref[pl.ds(aligned(slot * 256, 256), 256), :] = placed(slot) + cells

    to_modes(second, lambda i: second.snd1.at[i], True, cover_grad, cover_rows_back)
    own_mode = lax.broadcasted_iota(jnp.int32, (256, 128), 0) & 3
    second.modes[...] = second.modes[...] * jnp.where(row_at * 4 + own_mode == 0, 1.0, 2.0)
    for kl in range(4):
        g_re = second.modes[pl.ds(kl, 32, stride=8), :][:, :32]
        g_im = second.modes[pl.ds(4 + kl, 32, stride=8), :][:, :32]

        def one_channel(i, carry):
            w_re = g.weight[kl, 0, i].astype(f32)
            w_im = g.weight[kl, 1, i].astype(f32)
            b_re = jnp.sum(w_re * g_re + w_im * g_im, axis=0, keepdims=True)
            b_im = jnp.sum(w_re * g_im - w_im * g_re, axis=0, keepdims=True)
            g.mix[pl.ds(32 * kl + i, 1), 0:32] = b_re.astype(bf16).astype(f32) * scale
            g.mix[pl.ds(128 + 32 * kl + i, 1), 0:32] = b_im.astype(bf16).astype(f32) * scale
            return carry

        lax.fori_loop(0, 32, one_channel, 0)
    to_grid(second, cover_rows_out, lambda: rest_of_conv(second), write_out)

    modes_ref[0] = first.modes[...]
    modes_ref[1] = second.modes[...]
    for t in range(owners):

        @pl.when(row_at != t)
        def _():
            arrived = push(g.part.at[t], g.got_all.at[t], g.row_s.at[t], g.all_r.at[t], "row", t)
            arrived.wait_recv()
            arrived.wait_send()

    @pl.when(row_at < owners)
    def _():
        def sent(d):
            peer = lax.rem(row_at + d, n_row)
            push(g.total, g.got_all.at[row_at], g.all_s.at[d], g.all_r.at[row_at], "row", peer).wait_send()

        each(n_row, sent)

    small_ref[...] = g.got_all[...].reshape(80, 128)
    for wait in pending:
        wait()


def outputs_kernel(cells_ref, modes_ref, small_ref, out_ref, gspec_ref, conv_ref, bias_ref, proj_ref):
    out_ref[...] = cells_ref[...]
    kl = pl.program_id(0) // 2
    first = lax.rem(pl.program_id(0), 2) * 16
    g_re = modes_ref[pl.ds(256 + kl, 32, stride=8), :][:, :32]
    g_im = modes_ref[pl.ds(260 + kl, 32, stride=8), :][:, :32]
    for i in range(16):
        s_re = modes_ref[pl.ds(8 * (first + i) + kl, 1), :][:, :32]
        s_im = modes_ref[pl.ds(8 * (first + i) + 4 + kl, 1), :][:, :32]
        gspec_ref[0, 0, i] = g_re * s_re + g_im * s_im
        gspec_ref[0, 1, i] = g_im * s_re - g_re * s_im

    @pl.when(pl.program_id(0) == 0)
    def _():
        for q in range(4):
            rows = small_ref[0:72]
            conv_ref[72 * q : 72 * q + 72] = (pltpu.roll(rows, 128 - 32 * q, 1) if q else rows)[:, :32]
        rows = small_ref[72:80]
        bias_ref[...] = rows[0:1, :32]
        proj_ref[...] = pltpu.roll(rows, 96, 1)[0:1, :32]


def per_device(n_row, n_col, ocean_field, cotangent, conv_weight, conv_bias, projection, mode_weight):
    chans, rows_dev, cols_dev = ocean_field.shape
    ky_dev = mode_weight.shape[0]
    kx_all = mode_weight.shape[4] * n_col
    owners = min(10, n_row)
    ty, tx = (jnp.asarray(t) for t in tables(n_row, n_col, ky_dev, rows_dev, cols_dev, kx_all))
    vmem = pl.BlockSpec(memory_space=pltpu.VMEM)
    hbm = pl.BlockSpec(memory_space=pl.ANY)
    one = pass_scratch(n_row, n_col)
    scratch = list(one.values()) * 2 + list(common_scratch(n_row, n_col, rows_dev * n_row, owners).values())
    cells, modes, small = pl.pallas_call(
        functools.partial(step_kernel, n_row, n_col, owners),
        out_shape=[
            jax.ShapeDtypeStruct((chans * rows_dev, cols_dev), jnp.float32),
            jax.ShapeDtypeStruct((2, 256, 128), jnp.float32),
            jax.ShapeDtypeStruct((80, 128), jnp.float32),
        ],
        in_specs=[hbm, vmem, vmem, vmem, vmem, hbm, hbm, hbm],
        out_specs=[vmem, vmem, vmem],
        scratch_shapes=scratch,
        compiler_params=pltpu.CompilerParams(
            collective_id=0, has_side_effects=True, vmem_limit_bytes=VMEM_BYTES
        ),
        name="layer_step",
    )(
        ocean_field.reshape(n_col, 256, cols_dev),
        cotangent,
        conv_weight.reshape(9 * chans, chans),
        conv_bias.reshape(1, chans),
        projection.reshape(1, chans),
        mode_weight,
        ty,
        tx,
    )
    whole = lambda *shape: pl.BlockSpec(shape, lambda t: (0,) * len(shape))
    grad_input, grad_spec, grad_conv, grad_bias, grad_proj = pl.pallas_call(
        outputs_kernel,
        grid=(8,),
        out_shape=[
            jax.ShapeDtypeStruct((chans * rows_dev, cols_dev), jnp.float32),
            jax.ShapeDtypeStruct(mode_weight.shape, jnp.float32),
            jax.ShapeDtypeStruct((9 * chans, chans), jnp.float32),
            jax.ShapeDtypeStruct((1, chans), jnp.float32),
            jax.ShapeDtypeStruct((1, chans), jnp.float32),
        ],
        in_specs=[pl.BlockSpec((256, 256), lambda t: (t, 0)), whole(512, 128), whole(80, 128)],
        out_specs=[
            pl.BlockSpec((256, 256), lambda t: (t, 0)),
            pl.BlockSpec((1, 2, 16, 32, 32), lambda t: (t // 2, 0, t % 2, 0, 0)),
            whole(9 * chans, chans),
            whole(1, chans),
            whole(1, chans),
        ],
        compiler_params=pltpu.CompilerParams(vmem_limit_bytes=VMEM_BYTES),
        name="layer_outputs",
    )(cells, modes.reshape(512, 128), small)
    return (
        grad_input.reshape(ocean_field.shape),
        grad_spec,
        grad_conv.reshape(conv_weight.shape),
        grad_bias.reshape(chans),
        grad_proj.reshape(chans),
    )


def solution(mesh):
    placed = (
        P(None, "row", "col"),
        P("row", "col"),
        P(),
        P(),
        P(),
        P("row", None, None, None, "col"),
    )
    return jax.shard_map(
        functools.partial(per_device, mesh.shape["row"], mesh.shape["col"]),
        mesh=mesh,
        in_specs=placed,
        out_specs=(P(None, "row", "col"), P("row", None, None, None, "col"), P(), P(), P()),
        check_vma=False,
    )
```

```python
import functools
import math

import jax
import jax.numpy as jnp
import ml_dtypes
import numpy as np
from jax import lax
from jax.experimental import pallas as pl
from jax.experimental.pallas import tpu as pltpu
from jax.sharding import PartitionSpec as P

TWO_PI = 2.0 * math.pi
HIGH = lax.Precision.HIGHEST
HALF_FILL = 8
VMEM_BYTES = 56 * 1024 * 1024


def angle_pair(products, period):
    angles = (products % period).astype(np.float32) * np.float32(TWO_PI / period)
    return (np.cos(angles).astype(ml_dtypes.bfloat16), np.sin(angles).astype(ml_dtypes.bfloat16))


def tables(n_row, n_col, ky_dev, rows_dev, cols_dev, kx_all):
    modes, nx, ny = (ky_dev * n_row, rows_dev * n_row, cols_dev * n_col)
    cosine, sine = angle_pair(np.arange(modes)[:, None] * np.arange(ny)[None, :], ny)
    ty = np.stack([cosine.reshape(n_row, ky_dev, ny), -sine.reshape(n_row, ky_dev, ny)], axis=1)
    ty = ty.reshape(2 * modes, n_col, cols_dev).transpose(1, 0, 2)
    ids = np.arange(kx_all)
    freqs = np.where(ids < modes, ids, ids - 2 * modes) % nx
    cosine, sine = angle_pair(freqs[:, None] * np.arange(nx)[None, :], nx)
    return np.ascontiguousarray(ty), np.concatenate([cosine, sine], axis=0)


NT = (((1,), (1,)), ((), ()))
NN = (((1,), (0,)), ((), ()))
TN = (((0,), (0,)), ((), ()))


def dot(a, b, dims):
    return lax.dot_general(a, b, dims, preferred_element_type=jnp.float32)


def push(src, dst, send_sem, recv_sem, axis, peer):
    return pltpu.make_async_remote_copy(
        src_ref=src,
        dst_ref=dst,
        send_sem=send_sem,
        recv_sem=recv_sem,
        device_id={axis: peer},
        device_id_type=pl.DeviceIdType.MESH,
    )


class Exchange:
    def __init__(self, axis, me, size, source, slots, send_sem, recv_sem, shared):
        (self.axis, self.me, self.size, self.source, self.slots) = (axis, me, size, source, slots)
        (self.send_sem, self.recv_sem, self.shared) = (send_sem, recv_sem, shared)

    def peer(self, step):
        return (self.me + step) & (self.size - 1)

    def copy(self, step, src, dst, peer):
        recv_sem = self.recv_sem if self.shared else self.recv_sem.at[step]
        return push(src, dst, self.send_sem, recv_sem, self.axis, peer)

    def start(self, step):
        peer = self.peer(step)
        self.copy(step, self.source(peer), self.slots.at[self.me], peer).start()

    def start_all(self):
        each(self.size, self.start)

    def take(self, step):
        origin = (self.me - step) & (self.size - 1)
        self.copy(step, self.slots.at[origin], self.slots.at[origin], origin).wait_recv()
        return origin

    def every(self):
        rest = self.slots.at[pl.ds(0, self.size - 1)]
        return self.copy(1, rest, rest, self.peer(1))

    def take_all(self):
        self.every().wait_recv()

    def sent(self):
        self.every().wait_send()


def each(size, body):
    def step(index, carry):
        body(index)
        return carry

    lax.fori_loop(1, size, step, 0)


def part_swap(value, sign):
    rows = value.shape[0]
    is_real = (lax.broadcasted_iota(jnp.int32, value.shape, 0) & 4) == 0
    after = pltpu.roll(value, rows - 4, 0)
    before = pltpu.roll(value, 4, 0)
    return jnp.where(is_real, sign * after, -sign * before)


class Group:
    def __init__(self, names, refs):
        for name, ref in zip(names, refs):
            setattr(self, name, ref)


def aligned(value, to):
    return pl.multiple_of(value, to)


def pass_scratch(n_row, n_col):
    bf16, f32 = (jnp.bfloat16, jnp.float32)
    dma = pltpu.SemaphoreType.DMA
    found = dict(
        snd1=pltpu.VMEM((n_col, 256, 256), bf16),
        buf1=pltpu.VMEM((n_col, 256, 256), bf16),
        snd3=pltpu.VMEM((n_row, 16, 128), bf16),
        rcv3=pltpu.VMEM((n_row, 16, 128), bf16),
        snd5=pltpu.VMEM((2, 32, 128), bf16),
        rcv5=pltpu.VMEM((n_col, 32, 128), bf16),
        modes=pltpu.VMEM((256, 128), f32),
        snd7=pltpu.VMEM((n_col, 32, 128), bf16),
        rcv7=pltpu.VMEM((n_col, 32, 128), bf16),
        snd9=pltpu.VMEM((n_row, 16, 128), bf16),
        rcv9=pltpu.VMEM((n_row, 16, 128), bf16),
        snd10=pltpu.VMEM((n_col, 256, 256), bf16),
        rcv10=pltpu.VMEM((n_col, 256, 256), bf16),
        raw=pltpu.VMEM((68 * 32, 256), bf16),
        halo=pltpu.VMEM((2, 32, 256), bf16),
        edge_out=pltpu.VMEM((2, 16, 68 * 32), bf16),
        edge_in=pltpu.VMEM((2, 16, 68 * 32), bf16),
        wide=pltpu.VMEM((68 * 96, 256), bf16),
        taps=pltpu.VMEM((256, 1024), bf16),
        own=dma,
        hs=dma((2,)),
        hr=dma((2,)),
        es=dma((2,)),
        er=dma((2,)),
    )
    for step, size in ((1, n_col), (3, n_row), (5, n_col), (7, n_col), (9, n_row), (10, n_col)):
        found["s%d" % step] = dma
        found["r%d" % step] = dma((size,)) if step in (1, 10) else dma
    return found


def common_scratch(n_row, n_col, nx, owners):
    bf16, f32 = (jnp.bfloat16, jnp.float32)
    dma = pltpu.SemaphoreType.DMA
    piece = 80 // owners
    return dict(
        vbuf=pltpu.VMEM((n_col, 256, 256), bf16),
        ty=pltpu.VMEM((n_col, 8 * n_row, 256), bf16),
        tx=pltpu.VMEM((512, nx), bf16),
        weight=pltpu.VMEM((4, 2, 32, 32, 32), bf16),
        stage=pltpu.VMEM((4096, 128), f32),
        bias=pltpu.VMEM((32, 256), f32),
        proj=pltpu.VMEM((32, 256), f32),
        bias_rows=pltpu.VMEM((256, 256), f32),
        proj_rows=pltpu.VMEM((256, 256), f32),
        cot=pltpu.VMEM((64, 256), f32),
        out=pltpu.VMEM((2048, 256), f32),
        out_s=dma,
        acc=pltpu.VMEM((8 * n_row, 256), f32),
        rows_x=pltpu.VMEM((32, nx), bf16),
        mix=pltpu.VMEM((256, 128), f32),
        outer=pltpu.VMEM((960, 256), f32),
        sums=pltpu.VMEM((128, 256), f32),
        part=pltpu.VMEM((owners, piece, 128), f32),
        got_row=pltpu.VMEM((n_row, piece, 128), f32),
        sum_row=pltpu.VMEM((piece, 128), f32),
        got_col=pltpu.VMEM((n_col, piece, 128), f32),
        total=pltpu.VMEM((piece, 128), f32),
        got_all=pltpu.VMEM((owners, piece, 128), f32),
        load=dma((4,)),
        row_s=dma((owners,)),
        row_r=dma,
        col_s=dma,
        col_r=dma,
        all_s=dma,
        all_r=dma((owners,)),
    )


def step_kernel(n_row, n_col, owners, *refs):
    (v_ref, cot_ref, taps_ref, bias_ref, proj_ref, w_hbm, ty_hbm, tx_hbm, out_ref, modes_ref, small_ref, *rest) = refs
    nx = 64 * n_row
    names = list(pass_scratch(n_row, n_col))
    first = Group(names, rest[: len(names)])
    second = Group(names, rest[len(names) : 2 * len(names)])
    g = Group(list(common_scratch(n_row, n_col, nx, owners)), rest[2 * len(names) :])
    row_at = lax.axis_index("row")
    col_at = lax.axis_index("col")
    pairs = n_row // 2
    scale = 1.0 / math.sqrt((64 * n_row) * (256 * n_col))
    bf16, f32 = (jnp.bfloat16, jnp.float32)
    pending = []

    loads = [
        pltpu.make_async_copy(v_ref, g.vbuf, g.load.at[0]),
        pltpu.make_async_copy(ty_hbm, g.ty, g.load.at[1]),
        pltpu.make_async_copy(tx_hbm, g.tx, g.load.at[2]),
        pltpu.make_async_copy(w_hbm, g.weight, g.load.at[3]),
    ]
    for load in loads:
        load.start()
    barrier = pltpu.get_barrier_semaphore()
    each(n_col, lambda d: pl.semaphore_signal(
        barrier, inc=1, device_id={"col": (col_at + d) & (n_col - 1)}, device_id_type=pl.DeviceIdType.MESH))
    each(n_row, lambda d: pl.semaphore_signal(
        barrier, inc=1, device_id={"row": (row_at + d) & (n_row - 1)}, device_id_type=pl.DeviceIdType.MESH))
    pl.semaphore_wait(barrier, n_col - 1 + n_row - 1)

    def loop(size, body):
        def step(index, carry):
            body(index)
            return carry

        lax.fori_loop(0, size, step, 0)

    def send_halo_rows(p):
        up = lax.rem(row_at + n_row - 1, n_row)
        down = lax.rem(row_at + 1, n_row)
        copies = [
            push(p.raw.at[pl.ds(32, 32)], p.halo.at[1], p.hs.at[0], p.hr.at[0], "row", up),
            push(p.raw.at[pl.ds(64 * 32, 32)], p.halo.at[0], p.hs.at[1], p.hr.at[1], "row", down),
        ]
        for copy in copies:
            copy.start()
            pending.append(copy.wait_send)
        return copies

    def widen(p, row_copies):
        for copy in row_copies:
            copy.wait_recv()
        above = jnp.where(row_at > 0, 1.0, 0.0)
        below = jnp.where(row_at < n_row - 1, 1.0, 0.0)
        p.raw[0:32] = (p.halo[0].astype(f32) * above).astype(bf16)
        p.raw[65 * 32 : 66 * 32] = (p.halo[1].astype(f32) * below).astype(bf16)
        p.raw[66 * 32 : 68 * 32] = jnp.zeros((64, 256), bf16)
        row = lax.broadcasted_iota(jnp.int32, (32, 256), 0)
        lane = lax.broadcasted_iota(jnp.int32, (32, 256), 1)
        pick = ((row == 0) & (lane == 0)) | ((row == 16) & (lane == 255))
        edges = dot(jnp.where(pick, 1.0, 0.0).astype(bf16), p.raw[...], NT)
        p.edge_out[0] = edges[0:16].astype(bf16)
        p.edge_out[1] = edges[16:32].astype(bf16)
        left = lax.rem(col_at + n_col - 1, n_col)
        right = lax.rem(col_at + 1, n_col)
        copies = [
            push(p.edge_out.at[0], p.edge_in.at[1], p.es.at[0], p.er.at[0], "col", left),
            push(p.edge_out.at[1], p.edge_in.at[0], p.es.at[1], p.er.at[1], "col", right),
        ]
        for copy in copies:
            copy.start()
            pending.append(copy.wait_send)
        return copies

    def fill_wide(p, start, stop):
        row = lax.broadcasted_iota(jnp.int32, (16, 128), 0)
        lane = lax.broadcasted_iota(jnp.int32, (16, 128), 1)
        put_left = jnp.where((row == 0) & (lane == 0) & (col_at > 0), 1.0, 0.0).astype(bf16)
        put_right = jnp.where((row == 0) & (lane == 127) & (col_at < n_col - 1), 1.0, 0.0).astype(bf16)
        lanes = lax.broadcasted_iota(jnp.int32, (128, 128), 1)

        def chunk(q):
            here = p.raw[pl.ds(aligned(q * 128, 128), 128), :].astype(f32)
            from_left = dot(p.edge_in[0, :, pl.ds(aligned(q * 128, 128), 128)], put_left, TN)
            from_right = dot(p.edge_in[1, :, pl.ds(aligned(q * 128, 128), 128)], put_right, TN)
            before = pltpu.roll(here, 1, 1)
            after = pltpu.roll(here, 255, 1)
            before = jnp.concatenate([jnp.where(lanes == 0, from_left, before[:, :128]), before[:, 128:]], axis=1)
            after = jnp.concatenate([after[:, :128], jnp.where(lanes == 127, from_right, after[:, 128:])], axis=1)
            for x in range(4):
                for b, value in enumerate((before, here, after)):
                    base = aligned(q * 384 + 96 * x + 32 * b, 32)
                    p.wide[pl.ds(base, 32), :] = value[32 * x : 32 * x + 32].astype(bf16)

        loop(stop - start, lambda q: chunk(q + start))

    def spread_taps(p, turned):
        row = lax.broadcasted_iota(jnp.int32, (32, 1024), 0)
        lane = lax.broadcasted_iota(jnp.int32, (32, 1024), 1)
        padded = jnp.zeros((32, 1024), f32)
        for m in range(9):
            source = 8 - m if turned else m
            spot = jnp.where(lane == row + 32 * m, 1.0, 0.0).astype(bf16)
            padded = padded + dot(taps_ref[32 * source : 32 * source + 32, :], spot, NN if turned else TN)
        for x in range(8):
            p.taps[32 * x : 32 * x + 32, :] = (pltpu.roll(padded, 96 * x, 1) if x else padded).astype(bf16)

    def convolve(p):
        def block(t):
            rows = p.wide[pl.ds(aligned(t * 768, 16), 1024), :]
            result = dot(p.taps[...], rows, NN)
            for x in range(8):
                put_grid_row(8 * t + x, result[32 * x : 32 * x + 32])

        loop(8, block)

    def to_modes(p, source, started, cover, cover_rows):
        own = pltpu.make_async_copy(source(col_at), p.buf1.at[col_at], p.own)
        own.start()
        fields = Exchange("col", col_at, n_col, source, p.buf1, p.s1, p.r1, False)
        if not started:
            fields.start_all()
        pending.append(fields.sent)
        cover()
        own.wait()
        g.acc[...] = dot(g.ty[col_at], p.buf1[col_at], NT)

        def add_block(d):
            origin = fields.take(d)
            g.acc[...] += dot(g.ty[origin], p.buf1[origin], NT)

        each(n_col, add_block)
        whole = g.acc[...]
        upper = whole[:, :128].reshape(n_row, 8, 128)
        lower = whole[:, 128:].reshape(n_row, 8, 128)
        p.snd3[...] = jnp.concatenate([upper, lower], axis=1).astype(bf16)
        rows = Exchange("row", row_at, n_row, lambda i: p.snd3.at[i], p.rcv3, p.s3, p.r3, True)
        rows.start_all()
        pending.append(rows.sent)
        p.rcv3[row_at] = p.snd3[row_at]
        cover_rows()
        rows.take_all()
        for s in range(pairs):
            one = p.rcv3[2 * s].astype(f32)
            two = p.rcv3[2 * s + 1].astype(f32)
            even = jnp.where(low, one, pltpu.roll(two, 64, 1))
            odd = jnp.where(low, pltpu.roll(one, 64, 1), two)
            g.rows_x[0:16, 128 * s : 128 * s + 128] = even.astype(bf16)
            g.rows_x[16:32, 128 * s : 128 * s + 128] = odd.astype(bf16)
        both = dot(g.rows_x[...], g.tx[...], NT)
        coeffs = (both[:, :256] + part_swap(both[:, 256:], 1.0)) * scale
        coeffs = jnp.concatenate([coeffs[0:8], coeffs[16:24], coeffs[8:16], coeffs[24:32]], axis=0)
        p.snd5[0] = coeffs[:, :128].astype(bf16)
        p.snd5[1] = coeffs[:, 128:].astype(bf16)
        parts = Exchange("col", col_at, n_col, lambda i: p.snd5.at[i // 4], p.rcv5, p.s5, p.r5, True)
        parts.start_all()
        pending.append(parts.sent)
        p.rcv5[col_at] = p.snd5[col_at // 4]
        g.mix[...] = jnp.zeros_like(g.mix)
        parts.take_all()
        for i in range(n_col):
            p.modes[32 * i : 32 * i + 32] = pltpu.roll(p.rcv5[i].astype(f32), back_shift, 1)

    def to_grid(p, cover_rows, cover_cells, use):
        g.mix[...] = pltpu.roll(g.mix[...], quarter, 1)
        for i in range(n_col):
            for odd_channel in range(2):
                upper = g.mix[pl.ds(4 * i + odd_channel, 8, stride=32), :]
                lower = g.mix[pl.ds(4 * i + 2 + odd_channel, 8, stride=32), :]
                p.snd7[i, 16 * odd_channel : 16 * odd_channel + 16] = jnp.concatenate(
                    [upper, lower], axis=0
                ).astype(bf16)
        parts = Exchange("col", col_at, n_col, lambda i: p.snd7.at[i], p.rcv7, p.s7, p.r7, True)
        parts.start_all()
        pending.append(parts.sent)
        p.rcv7[col_at] = p.snd7[col_at]
        parts.take_all()
        halves = [sum(p.rcv7[4 * h + q].astype(f32) for q in range(4)) for h in range(2)]
        mixed = jnp.concatenate(halves, axis=1)
        swapped = part_swap(mixed, -1.0)
        operand = jnp.concatenate([mixed, swapped], axis=1).astype(bf16)
        by_rows = dot(operand, g.tx[...], NN)
        for s in range(pairs):
            even = by_rows[0:16, 128 * s : 128 * s + 128]
            odd = by_rows[16:32, 128 * s : 128 * s + 128]
            p.snd9[2 * s] = jnp.where(low, even, pltpu.roll(odd, 64, 1)).astype(bf16)
            p.snd9[2 * s + 1] = jnp.where(low, pltpu.roll(even, 64, 1), odd).astype(bf16)
        rows = Exchange("row", row_at, n_row, lambda i: p.snd9.at[i], p.rcv9, p.s9, p.r9, True)
        rows.start_all()
        pending.append(rows.sent)
        p.rcv9[row_at] = p.snd9[row_at]
        cover_rows()
        rows.take_all()
        got = p.rcv9[...].astype(f32)
        own_rows = jnp.concatenate(
            [got[:, :8].reshape(8 * n_row, 128), got[:, 8:].reshape(8 * n_row, 128)], axis=1
        )
        lhs = jnp.transpose(own_rows).astype(bf16)
        cells = Exchange("col", col_at, n_col, lambda i: p.snd10.at[i], p.rcv10, p.s10, p.r10, False)

        def make_cells(d):
            peer = cells.peer(d)
            p.snd10[peer] = dot(lhs, g.ty[peer], NN).astype(bf16)
            cells.start(d)

        each(n_col, make_cells)
        pending.append(cells.sent)
        cover_cells()
        use(col_at, dot(lhs, g.ty[col_at], NN), 0)

        def take(d):
            origin = cells.take(d)
            use(origin, p.rcv10[origin].astype(f32), d)

        each(n_col, take)

    def first_fill(p):
        for copy in p.edge_copies:
            copy.wait_recv()
        fill_wide(p, 0, HALF_FILL)

    def rest_of_conv(p):
        fill_wide(p, HALF_FILL, 17)
        convolve(p)

    def regroup(p):
        def one(x):
            p.raw[pl.ds(aligned(x * 32 + 32, 32), 32), :] = grid_row(x).astype(bf16)

        one(0)
        one(63)
        p.row_copies = send_halo_rows(p)
        loop(62, lambda x: one(x + 1))

    def widen_now(p):
        p.edge_copies = widen(p, p.row_copies)

    def place(slot, value):
        for half in range(2):
            g.stage[pl.ds(aligned(half * 2048 + slot * 256, 256), 256), :] = value[:, 128 * half : 128 * half + 128]

    def placed(slot):
        return jnp.concatenate(
            [g.stage[pl.ds(aligned(half * 2048 + slot * 256, 256), 256), :] for half in range(2)], axis=1
        )

    def grid_row(x):
        return jnp.concatenate([g.stage[pl.ds(2048 * half + x, 32, stride=64), :] for half in range(2)], axis=1)

    def put_grid_row(x, value):
        for half in range(2):
            g.stage[pl.ds(2048 * half + x, 32, stride=64), :] = value[:, 128 * half : 128 * half + 128]

    low = lax.broadcasted_iota(jnp.int32, (16, 128), 1) < 64
    quarter = lax.rem(col_at, 4) * 32
    back_shift = lax.rem(128 - quarter, 128)

    def cover_field():
        loads[0].wait()
        for i in range(n_col):
            place(i, g.vbuf[i].astype(f32))

        regroup(first)
        g.cot[...] = cot_ref[...].astype(f32)
        spread_taps(first, False)
        g.bias[...] = column(bias_ref)
        g.proj[...] = column(proj_ref)
        loads[1].wait()
        loads[2].wait()

    def column(ref):
        diagonal = lax.broadcasted_iota(jnp.int32, (32, 32), 0) == lax.broadcasted_iota(jnp.int32, (32, 32), 1)
        value = jnp.sum(jnp.where(diagonal, jnp.broadcast_to(ref[...], (32, 32)), 0.0), axis=1, keepdims=True)
        return jnp.broadcast_to(value, (32, 256))

    to_modes(first, lambda i: v_ref.at[i], False, cover_field, lambda: widen_now(first))
    loads[3].wait()
    for kl in range(4):

        def add_channel(i, sums):
            real, imag = sums
            s_re = first.modes[pl.ds(8 * i + kl, 1), :][:, :32]
            s_im = first.modes[pl.ds(8 * i + 4 + kl, 1), :][:, :32]
            w_re = g.weight[kl, 0, i].astype(f32)
            w_im = g.weight[kl, 1, i].astype(f32)
            return (real + (w_re * s_re - w_im * s_im), imag + (w_re * s_im + w_im * s_re))

        zero = jnp.zeros((32, 32), f32)
        real, imag = lax.fori_loop(0, 32, add_channel, (zero, zero))
        factor = jnp.where(row_at * 4 + kl == 0, 1.0, 2.0).astype(f32) * scale
        g.mix[32 * kl : 32 * kl + 32, 0:32] = real.astype(bf16).astype(f32) * factor
        g.mix[128 + 32 * kl : 160 + 32 * kl, 0:32] = imag.astype(bf16).astype(f32) * factor

    back = Exchange("col", col_at, n_col, lambda i: second.snd1.at[i], second.buf1, second.s1, second.r1, False)

    def activate(slot, cells, d):
        conv = placed(slot)
        rounded = []
        for ch in range(4):
            channel = slot * 4 + ch
            rows = slice(64 * ch, 64 * ch + 64)
            bias = jnp.broadcast_to(g.bias[pl.ds(channel, 1), :], (64, 256))
            proj = jnp.broadcast_to(g.proj[pl.ds(channel, 1), :], (64, 256))
            pre = conv[rows] + cells[rows] + bias
            cdf = 0.5 * (1.0 + lax.erf(pre * math.sqrt(0.5)))
            pdf = jnp.exp(-0.5 * pre * pre) * (1.0 / math.sqrt(TWO_PI))
            grad = (proj * g.cot[...]) * (cdf + pre * pdf)
            rounded.append(grad.astype(bf16))
            second.snd1[slot, 64 * ch : 64 * ch + 64] = rounded[ch]
            at = pl.ds(aligned(channel * 8, 8), 8)
            g.bias_rows[at, :] = jnp.sum(grad.reshape(8, 8, 256), axis=0)
            g.proj_rows[at, :] = jnp.sum(((pre * cdf) * g.cot[...]).reshape(8, 8, 256), axis=0)
        if not isinstance(d, int):
            back.start(n_col - d)
        place(slot, jnp.concatenate(rounded, axis=0).astype(f32))

    to_grid(first, lambda: first_fill(first), lambda: rest_of_conv(first), activate)

    piece = 80 // owners

    def cover_grad():
        regroup(second)
        of_channel = (lax.broadcasted_iota(jnp.int32, (32, 256), 1) // 8) == lax.broadcasted_iota(
            jnp.int32, (32, 256), 0
        )
        gather = jnp.where(of_channel, 1.0, 0.0)
        for at, rows in ((0, g.bias_rows), (32, g.proj_rows)):
            g.sums[at : at + 32] = lax.dot_general(
                gather, rows[...], NN, precision=HIGH, preferred_element_type=f32
            )
        g.sums[64:128] = jnp.zeros((64, 256), f32)
        g.outer[...] = jnp.zeros_like(g.outer)

        def block(t):
            rows = first.wide[pl.ds(aligned(t * 768, 16), 960), :]
            grads = second.raw[pl.ds(aligned(t * 256 + 32, 32), 256), :]
            g.outer[...] += dot(rows, grads, NT)

        loop(8, block)
        lane = lax.broadcasted_iota(jnp.int32, (96, 128), 1)
        taps = []
        for a in range(3):
            total = jnp.zeros((96, 128), f32)
            for x in range(8):
                here = g.outer[96 * (x + a) : 96 * (x + a) + 96, 128 * (x // 4) : 128 * (x // 4) + 128]
                total = total + (pltpu.roll(here, 128 - 32 * (x % 4), 1) if x % 4 else here)
            taps.append(jnp.where(lane < 32, total, 0.0))
        taps = jnp.concatenate(taps, axis=0)
        packed = taps[0:72]
        for q in range(1, 4):
            packed = packed + pltpu.roll(taps[72 * q : 72 * q + 72], 32 * q, 1)
        lanes_sum = lax.dot_general(
            jnp.ones((8, 256), f32), g.sums[...], NT, precision=HIGH, preferred_element_type=f32
        )
        g.part[...] = (jnp.concatenate([packed, lanes_sum], axis=0) * scale).reshape(owners, piece, 128)
        for t in range(owners):

            @pl.when(row_at != t)
            def _():
                push(g.part.at[t], g.got_row.at[row_at], g.row_s.at[t], g.row_r, "row", t).start()

        spread_taps(second, True)

    def sum_rows():
        @pl.when(row_at < owners)
        def _():
            g.got_row[row_at] = g.part[row_at]
            Exchange("row", row_at, n_row, None, g.got_row, g.row_s.at[0], g.row_r, True).take_all()
            g.sum_row[...] = jnp.sum(g.got_row[...], axis=0)
            g.got_col[col_at] = g.sum_row[...]
            Exchange("col", col_at, n_col, lambda i: g.sum_row, g.got_col, g.col_s, g.col_r, True).start_all()

    def sum_cols():
        @pl.when(row_at < owners)
        def _():
            sums = Exchange("col", col_at, n_col, lambda i: g.sum_row, g.got_col, g.col_s, g.col_r, True)
            sums.take_all()
            sums.sent()
            g.total[...] = jnp.sum(g.got_col[...], axis=0)
            g.got_all[row_at] = g.total[...]

            def send(d):
                peer = (row_at + d) & (n_row - 1)
                push(g.total, g.got_all.at[row_at], g.all_s, g.all_r.at[row_at], "row", peer).start()

            each(n_row, send)

    def cover_rows_back():
        widen_now(second)
        sum_rows()

    def cover_rows_out():
        first_fill(second)
        sum_cols()

    def write_out(slot, cells, d):
        at = pl.ds(aligned(slot * 256, 256), 256)
        g.out[at, :] = placed(slot) + cells
        pltpu.make_async_copy(g.out.at[at], out_ref.at[at], g.out_s).start()

    to_modes(second, lambda i: second.snd1.at[i], True, cover_grad, cover_rows_back)
    own_mode = lax.broadcasted_iota(jnp.int32, (256, 128), 0) & 3
    second.modes[...] = second.modes[...] * jnp.where(row_at * 4 + own_mode == 0, 1.0, 2.0)
    for kl in range(4):
        g_re = second.modes[pl.ds(kl, 32, stride=8), :][:, :32]
        g_im = second.modes[pl.ds(4 + kl, 32, stride=8), :][:, :32]

        def one_channel(i, carry):
            w_re = g.weight[kl, 0, i].astype(f32)
            w_im = g.weight[kl, 1, i].astype(f32)
            b_re = jnp.sum(w_re * g_re + w_im * g_im, axis=0, keepdims=True)
            b_im = jnp.sum(w_re * g_im - w_im * g_re, axis=0, keepdims=True)
            g.mix[pl.ds(32 * kl + i, 1), 0:32] = b_re.astype(bf16).astype(f32) * scale
            g.mix[pl.ds(128 + 32 * kl + i, 1), 0:32] = b_im.astype(bf16).astype(f32) * scale
            return carry

        lax.fori_loop(0, 32, one_channel, 0)
    to_grid(second, cover_rows_out, lambda: rest_of_conv(second), write_out)

    modes_ref[0] = first.modes[...]
    modes_ref[1] = second.modes[...]
    for t in range(owners):

        @pl.when(row_at != t)
        def _():
            arrived = push(g.part.at[t], g.got_all.at[t], g.row_s.at[t], g.all_r.at[t], "row", t)
            arrived.wait_recv()
            arrived.wait_send()

    @pl.when(row_at < owners)
    def _():
        Exchange("row", row_at, n_row, None, g.got_row, g.all_s, g.row_r, True).sent()

    small_ref[...] = g.got_all[...].reshape(80, 128)
    for wait in pending:
        wait()
    pltpu.make_async_copy(g.out, out_ref, g.out_s).wait()


def outputs_kernel(cells_ref, modes_ref, small_ref, out_ref, gspec_ref, conv_ref, bias_ref, proj_ref, weight, sems):
    copies = []
    for q in range(4):
        at = pl.ds(512 * q, 512)
        copies.append(pltpu.make_async_copy(cells_ref.at[at], out_ref.at[at], sems.at[q]))
        copies[q].start()
    for kl in range(4):
        g_re = modes_ref[pl.ds(256 + kl, 32, stride=8), :][:, :32]
        g_im = modes_ref[pl.ds(260 + kl, 32, stride=8), :][:, :32]
        for i in range(32):
            s_re = modes_ref[8 * i + kl : 8 * i + kl + 1, :][:, :32]
            s_im = modes_ref[8 * i + 4 + kl : 8 * i + 5 + kl, :][:, :32]
            weight[kl, 0, i] = g_re * s_re + g_im * s_im
            weight[kl, 1, i] = g_im * s_re - g_re * s_im
        copies.append(pltpu.make_async_copy(weight.at[kl], gspec_ref.at[kl], sems.at[4 + kl]))
        copies[4 + kl].start()
    for q in range(4):
        rows = small_ref[0:72]
        conv_ref[72 * q : 72 * q + 72] = (pltpu.roll(rows, 128 - 32 * q, 1) if q else rows)[:, :32]
    rows = small_ref[72:80]
    bias_ref[...] = rows[0:1, :32]
    proj_ref[...] = pltpu.roll(rows, 96, 1)[0:1, :32]
    for copy in copies:
        copy.wait()


def per_device(n_row, n_col, ocean_field, cotangent, conv_weight, conv_bias, projection, mode_weight):
    chans, rows_dev, cols_dev = ocean_field.shape
    ky_dev = mode_weight.shape[0]
    kx_all = mode_weight.shape[4] * n_col
    owners = min(10, n_row)
    ty, tx = (jnp.asarray(t) for t in tables(n_row, n_col, ky_dev, rows_dev, cols_dev, kx_all))
    vmem = pl.BlockSpec(memory_space=pltpu.VMEM)
    hbm = pl.BlockSpec(memory_space=pl.ANY)
    one = pass_scratch(n_row, n_col)
    scratch = list(one.values()) * 2 + list(common_scratch(n_row, n_col, rows_dev * n_row, owners).values())
    cells, modes, small = pl.pallas_call(
        functools.partial(step_kernel, n_row, n_col, owners),
        out_shape=[
            jax.ShapeDtypeStruct((chans * rows_dev, cols_dev), jnp.float32),
            jax.ShapeDtypeStruct((2, 256, 128), jnp.float32),
            jax.ShapeDtypeStruct((80, 128), jnp.float32),
        ],
        in_specs=[hbm, vmem, vmem, vmem, vmem, hbm, hbm, hbm],
        out_specs=[hbm, vmem, vmem],
        scratch_shapes=scratch,
        compiler_params=pltpu.CompilerParams(
            collective_id=0, has_side_effects=True, vmem_limit_bytes=VMEM_BYTES
        ),
        name="layer_step",
    )(
        ocean_field.reshape(n_col, 256, cols_dev),
        cotangent,
        conv_weight.reshape(9 * chans, chans),
        conv_bias.reshape(1, chans),
        projection.reshape(1, chans),
        mode_weight,
        ty,
        tx,
    )
    grad_input, grad_spec, grad_conv, grad_bias, grad_proj = pl.pallas_call(
        outputs_kernel,
        out_shape=[
            jax.ShapeDtypeStruct((chans * rows_dev, cols_dev), jnp.float32),
            jax.ShapeDtypeStruct(mode_weight.shape, jnp.float32),
            jax.ShapeDtypeStruct((9 * chans, chans), jnp.float32),
            jax.ShapeDtypeStruct((1, chans), jnp.float32),
            jax.ShapeDtypeStruct((1, chans), jnp.float32),
        ],
        in_specs=[hbm, vmem, vmem],
        out_specs=[hbm, hbm, vmem, vmem, vmem],
        scratch_shapes=[pltpu.VMEM(mode_weight.shape, jnp.float32), pltpu.SemaphoreType.DMA((8,))],
        compiler_params=pltpu.CompilerParams(vmem_limit_bytes=VMEM_BYTES),
        name="layer_outputs",
    )(cells, modes.reshape(512, 128), small)
    return (
        grad_input.reshape(ocean_field.shape),
        grad_spec,
        grad_conv.reshape(conv_weight.shape),
        grad_bias.reshape(chans),
        grad_proj.reshape(chans),
    )


def solution(mesh):
    placed = (
        P(None, "row", "col"),
        P("row", "col"),
        P(),
        P(),
        P(),
        P("row", None, None, None, "col"),
    )
    return jax.shard_map(
        functools.partial(per_device, mesh.shape["row"], mesh.shape["col"]),
        mesh=mesh,
        in_specs=placed,
        out_specs=(P(None, "row", "col"), P("row", None, None, None, "col"), P(), P(), P()),
        check_vma=False,
    )
```

```python
import functools
import math

import jax
import jax.numpy as jnp
import ml_dtypes
import numpy as np
from jax import lax
from jax.experimental import pallas as pl
from jax.experimental.pallas import tpu as pltpu
from jax.sharding import PartitionSpec as P

TWO_PI = 2.0 * math.pi
HIGH = lax.Precision.HIGHEST
HALF_FILL = 8
VMEM_BYTES = 56 * 1024 * 1024


def angle_pair(products, period):
    angles = (products % period).astype(np.float32) * np.float32(TWO_PI / period)
    return (np.cos(angles).astype(ml_dtypes.bfloat16), np.sin(angles).astype(ml_dtypes.bfloat16))


def tables(n_row, n_col, ky_dev, rows_dev, cols_dev, kx_all):
    modes, nx, ny = (ky_dev * n_row, rows_dev * n_row, cols_dev * n_col)
    cosine, sine = angle_pair(np.arange(modes)[:, None] * np.arange(ny)[None, :], ny)
    ty = np.stack([cosine.reshape(n_row, ky_dev, ny), -sine.reshape(n_row, ky_dev, ny)], axis=1)
    ty = ty.reshape(2 * modes, n_col, cols_dev).transpose(1, 0, 2)
    ids = np.arange(kx_all)
    freqs = np.where(ids < modes, ids, ids - 2 * modes) % nx
    cosine, sine = angle_pair(freqs[:, None] * np.arange(nx)[None, :], nx)
    return np.ascontiguousarray(ty), np.concatenate([cosine, sine], axis=0)


NT = (((1,), (1,)), ((), ()))
NN = (((1,), (0,)), ((), ()))
TN = (((0,), (0,)), ((), ()))


def dot(a, b, dims):
    return lax.dot_general(a, b, dims, preferred_element_type=jnp.float32)


def push(src, dst, send_sem, recv_sem, axis, peer):
    return pltpu.make_async_remote_copy(
        src_ref=src,
        dst_ref=dst,
        send_sem=send_sem,
        recv_sem=recv_sem,
        device_id={axis: peer},
        device_id_type=pl.DeviceIdType.MESH,
    )


class Exchange:
    def __init__(self, axis, me, size, source, slots, send_sem, recv_sem, shared):
        (self.axis, self.me, self.size, self.source, self.slots) = (axis, me, size, source, slots)
        (self.send_sem, self.recv_sem, self.shared) = (send_sem, recv_sem, shared)

    def peer(self, step):
        return (self.me + step) & (self.size - 1)

    def copy(self, step, src, dst, peer):
        recv_sem = self.recv_sem if self.shared else self.recv_sem.at[step]
        return push(src, dst, self.send_sem, recv_sem, self.axis, peer)

    def start(self, step):
        peer = self.peer(step)
        self.copy(step, self.source(peer), self.slots.at[self.me], peer).start()

    def start_all(self):
        each(self.size, self.start)

    def take(self, step):
        origin = (self.me - step) & (self.size - 1)
        self.copy(step, self.slots.at[origin], self.slots.at[origin], origin).wait_recv()
        return origin

    def every(self):
        rest = self.slots.at[pl.ds(0, self.size - 1)]
        return self.copy(1, rest, rest, self.peer(1))

    def take_all(self):
        self.every().wait_recv()

    def sent(self):
        self.every().wait_send()


def each(size, body):
    def step(index, carry):
        body(index)
        return carry

    lax.fori_loop(1, size, step, 0)


def part_swap(value, sign):
    rows = value.shape[0]
    is_real = (lax.broadcasted_iota(jnp.int32, value.shape, 0) & 4) == 0
    after = pltpu.roll(value, rows - 4, 0)
    before = pltpu.roll(value, 4, 0)
    return jnp.where(is_real, sign * after, -sign * before)


class Group:
    def __init__(self, names, refs):
        for name, ref in zip(names, refs):
            setattr(self, name, ref)


def aligned(value, to):
    return pl.multiple_of(value, to)


def pass_scratch(n_row, n_col):
    bf16, f32 = (jnp.bfloat16, jnp.float32)
    dma = pltpu.SemaphoreType.DMA
    found = dict(
        snd1=pltpu.VMEM((n_col, 256, 256), bf16),
        buf1=pltpu.VMEM((n_col, 256, 256), bf16),
        snd3=pltpu.VMEM((n_row, 16, 128), bf16),
        rcv3=pltpu.VMEM((n_row, 16, 128), bf16),
        snd5=pltpu.VMEM((2, 32, 128), bf16),
        rcv5=pltpu.VMEM((n_col, 32, 128), bf16),
        modes=pltpu.VMEM((256, 128), f32),
        snd7=pltpu.VMEM((n_col, 32, 128), bf16),
        rcv7=pltpu.VMEM((n_col, 32, 128), bf16),
        snd9=pltpu.VMEM((n_row, 16, 128), bf16),
        rcv9=pltpu.VMEM((n_row, 16, 128), bf16),
        snd10=pltpu.VMEM((n_col, 256, 256), bf16),
        rcv10=pltpu.VMEM((n_col, 256, 256), bf16),
        raw=pltpu.VMEM((68 * 32, 256), bf16),
        halo=pltpu.VMEM((2, 32, 256), bf16),
        edge_out=pltpu.VMEM((2, 16, 68 * 32), bf16),
        edge_in=pltpu.VMEM((2, 16, 68 * 32), bf16),
        wide=pltpu.VMEM((68 * 96, 256), bf16),
        taps=pltpu.VMEM((256, 1024), bf16),
        own=dma,
        hs=dma((2,)),
        hr=dma((2,)),
        es=dma((2,)),
        er=dma((2,)),
    )
    for step, size in ((1, n_col), (3, n_row), (5, n_col), (7, n_col), (9, n_row), (10, n_col)):
        found["s%d" % step] = dma
        found["r%d" % step] = dma((size,)) if step in (1, 10) else dma
    return found


def common_scratch(n_row, n_col, nx, owners):
    bf16, f32 = (jnp.bfloat16, jnp.float32)
    dma = pltpu.SemaphoreType.DMA
    piece = 80 // owners
    return dict(
        vbuf=pltpu.VMEM((n_col, 256, 256), bf16),
        ty=pltpu.VMEM((n_col, 8 * n_row, 256), bf16),
        tx=pltpu.VMEM((512, nx), bf16),
        weight=pltpu.VMEM((4, 2, 32, 32, 32), bf16),
        stage=pltpu.VMEM((4096, 128), f32),
        bias=pltpu.VMEM((32, 256), f32),
        proj=pltpu.VMEM((32, 256), f32),
        bias_rows=pltpu.VMEM((256, 256), f32),
        proj_rows=pltpu.VMEM((256, 256), f32),
        cot=pltpu.VMEM((64, 256), f32),
        out=pltpu.VMEM((2048, 256), f32),
        out_s=dma,
        acc=pltpu.VMEM((8 * n_row, 256), f32),
        rows_x=pltpu.VMEM((32, nx), bf16),
        mix=pltpu.VMEM((256, 128), f32),
        outer=pltpu.VMEM((960, 256), f32),
        sums=pltpu.VMEM((128, 256), f32),
        part=pltpu.VMEM((owners, piece, 128), f32),
        got_row=pltpu.VMEM((n_row, piece, 128), f32),
        sum_row=pltpu.VMEM((piece, 128), f32),
        got_col=pltpu.VMEM((n_col, piece, 128), f32),
        total=pltpu.VMEM((piece, 128), f32),
        got_all=pltpu.VMEM((owners, piece, 128), f32),
        load=dma((4,)),
        row_s=dma((owners,)),
        row_r=dma,
        col_s=dma,
        col_r=dma,
        all_s=dma,
        all_r=dma((owners,)),
    )


def step_kernel(n_row, n_col, owners, *refs):
    (v_ref, cot_ref, taps_ref, bias_ref, proj_ref, w_hbm, ty_hbm, tx_hbm, out_ref, modes_ref, small_ref, *rest) = refs
    nx = 64 * n_row
    names = list(pass_scratch(n_row, n_col))
    first = Group(names, rest[: len(names)])
    second = Group(names, rest[len(names) : 2 * len(names)])
    g = Group(list(common_scratch(n_row, n_col, nx, owners)), rest[2 * len(names) :])
    row_at = lax.axis_index("row")
    col_at = lax.axis_index("col")
    pairs = n_row // 2
    scale = 1.0 / math.sqrt((64 * n_row) * (256 * n_col))
    bf16, f32 = (jnp.bfloat16, jnp.float32)
    pending = []

    loads = [
        pltpu.make_async_copy(v_ref, g.vbuf, g.load.at[0]),
        pltpu.make_async_copy(ty_hbm, g.ty, g.load.at[1]),
        pltpu.make_async_copy(tx_hbm, g.tx, g.load.at[2]),
        pltpu.make_async_copy(w_hbm, g.weight, g.load.at[3]),
    ]
    for load in loads:
        load.start()
    barrier = pltpu.get_barrier_semaphore()
    each(n_col, lambda d: pl.semaphore_signal(
        barrier, inc=1, device_id={"col": (col_at + d) & (n_col - 1)}, device_id_type=pl.DeviceIdType.MESH))
    each(n_row, lambda d: pl.semaphore_signal(
        barrier, inc=1, device_id={"row": (row_at + d) & (n_row - 1)}, device_id_type=pl.DeviceIdType.MESH))
    pl.semaphore_wait(barrier, n_col - 1 + n_row - 1)

    def loop(size, body):
        def step(index, carry):
            body(index)
            return carry

        lax.fori_loop(0, size, step, 0)

    def send_halo_rows(p):
        up = lax.rem(row_at + n_row - 1, n_row)
        down = lax.rem(row_at + 1, n_row)
        copies = [
            push(p.raw.at[pl.ds(32, 32)], p.halo.at[1], p.hs.at[0], p.hr.at[0], "row", up),
            push(p.raw.at[pl.ds(64 * 32, 32)], p.halo.at[0], p.hs.at[1], p.hr.at[1], "row", down),
        ]
        for copy in copies:
            copy.start()
            pending.append(copy.wait_send)
        return copies

    def widen(p, row_copies):
        for copy in row_copies:
            copy.wait_recv()
        above = jnp.where(row_at > 0, 1.0, 0.0)
        below = jnp.where(row_at < n_row - 1, 1.0, 0.0)
        p.raw[0:32] = (p.halo[0].astype(f32) * above).astype(bf16)
        p.raw[65 * 32 : 66 * 32] = (p.halo[1].astype(f32) * below).astype(bf16)
        p.raw[66 * 32 : 68 * 32] = jnp.zeros((64, 256), bf16)
        row = lax.broadcasted_iota(jnp.int32, (32, 256), 0)
        lane = lax.broadcasted_iota(jnp.int32, (32, 256), 1)
        pick = ((row == 0) & (lane == 0)) | ((row == 16) & (lane == 255))
        edges = dot(jnp.where(pick, 1.0, 0.0).astype(bf16), p.raw[...], NT)
        p.edge_out[0] = edges[0:16].astype(bf16)
        p.edge_out[1] = edges[16:32].astype(bf16)
        left = lax.rem(col_at + n_col - 1, n_col)
        right = lax.rem(col_at + 1, n_col)
        copies = [
            push(p.edge_out.at[0], p.edge_in.at[1], p.es.at[0], p.er.at[0], "col", left),
            push(p.edge_out.at[1], p.edge_in.at[0], p.es.at[1], p.er.at[1], "col", right),
        ]
        for copy in copies:
            copy.start()
            pending.append(copy.wait_send)
        return copies

    def fill_wide(p, start, stop):
        row = lax.broadcasted_iota(jnp.int32, (16, 128), 0)
        lane = lax.broadcasted_iota(jnp.int32, (16, 128), 1)
        put_left = jnp.where((row == 0) & (lane == 0) & (col_at > 0), 1.0, 0.0).astype(bf16)
        put_right = jnp.where((row == 0) & (lane == 127) & (col_at < n_col - 1), 1.0, 0.0).astype(bf16)
        lanes = lax.broadcasted_iota(jnp.int32, (128, 128), 1)

        def chunk(q):
            here = p.raw[pl.ds(aligned(q * 128, 128), 128), :].astype(f32)
            from_left = dot(p.edge_in[0, :, pl.ds(aligned(q * 128, 128), 128)], put_left, TN)
            from_right = dot(p.edge_in[1, :, pl.ds(aligned(q * 128, 128), 128)], put_right, TN)
            before = pltpu.roll(here, 1, 1)
            after = pltpu.roll(here, 255, 1)
            before = jnp.concatenate([jnp.where(lanes == 0, from_left, before[:, :128]), before[:, 128:]], axis=1)
            after = jnp.concatenate([after[:, :128], jnp.where(lanes == 127, from_right, after[:, 128:])], axis=1)
            for x in range(4):
                for b, value in enumerate((before, here, after)):
                    base = aligned(q * 384 + 96 * x + 32 * b, 32)
                    p.wide[pl.ds(base, 32), :] = value[32 * x : 32 * x + 32].astype(bf16)

        loop(stop - start, lambda q: chunk(q + start))

    def spread_taps(p, turned):
        row = lax.broadcasted_iota(jnp.int32, (32, 1024), 0)
        lane = lax.broadcasted_iota(jnp.int32, (32, 1024), 1)
        padded = jnp.zeros((32, 1024), f32)
        for m in range(9):
            source = 8 - m if turned else m
            spot = jnp.where(lane == row + 32 * m, 1.0, 0.0).astype(bf16)
            padded = padded + dot(taps_ref[32 * source : 32 * source + 32, :], spot, NN if turned else TN)
        for x in range(8):
            p.taps[32 * x : 32 * x + 32, :] = (pltpu.roll(padded, 96 * x, 1) if x else padded).astype(bf16)

    def convolve(p):
        def block(t):
            rows = p.wide[pl.ds(aligned(t * 768, 16), 1024), :]
            result = dot(p.taps[...], rows, NN)
            for x in range(8):
                put_grid_row(8 * t + x, result[32 * x : 32 * x + 32])

        loop(8, block)

    def to_modes(p, source, started, cover, cover_rows):
        own = pltpu.make_async_copy(source(col_at), p.buf1.at[col_at], p.own)
        own.start()
        fields = Exchange("col", col_at, n_col, source, p.buf1, p.s1, p.r1, False)
        if not started:
            fields.start_all()
        pending.append(fields.sent)
        cover()
        own.wait()
        g.acc[...] = dot(g.ty[col_at], p.buf1[col_at], NT)

        def add_block(d):
            origin = fields.take(d)
            g.acc[...] += dot(g.ty[origin], p.buf1[origin], NT)

        each(n_col, add_block)
        whole = g.acc[...]
        upper = whole[:, :128].reshape(n_row, 8, 128)
        lower = whole[:, 128:].reshape(n_row, 8, 128)
        p.snd3[...] = jnp.concatenate([upper, lower], axis=1).astype(bf16)
        rows = Exchange("row", row_at, n_row, lambda i: p.snd3.at[i], p.rcv3, p.s3, p.r3, True)
        rows.start_all()
        pending.append(rows.sent)
        p.rcv3[row_at] = p.snd3[row_at]
        cover_rows()
        rows.take_all()
        for s in range(pairs):
            one = p.rcv3[2 * s].astype(f32)
            two = p.rcv3[2 * s + 1].astype(f32)
            even = jnp.where(low, one, pltpu.roll(two, 64, 1))
            odd = jnp.where(low, pltpu.roll(one, 64, 1), two)
            g.rows_x[0:16, 128 * s : 128 * s + 128] = even.astype(bf16)
            g.rows_x[16:32, 128 * s : 128 * s + 128] = odd.astype(bf16)
        both = dot(g.rows_x[...], g.tx[...], NT)
        coeffs = (both[:, :256] + part_swap(both[:, 256:], 1.0)) * scale
        coeffs = jnp.concatenate([coeffs[0:8], coeffs[16:24], coeffs[8:16], coeffs[24:32]], axis=0)
        p.snd5[0] = coeffs[:, :128].astype(bf16)
        p.snd5[1] = coeffs[:, 128:].astype(bf16)
        parts = Exchange("col", col_at, n_col, lambda i: p.snd5.at[i // 4], p.rcv5, p.s5, p.r5, True)
        parts.start_all()
        pending.append(parts.sent)
        p.rcv5[col_at] = p.snd5[col_at // 4]
        g.mix[...] = jnp.zeros_like(g.mix)
        parts.take_all()
        for i in range(n_col):
            p.modes[32 * i : 32 * i + 32] = pltpu.roll(p.rcv5[i].astype(f32), back_shift, 1)

    def to_grid(p, cover_rows, cover_cells, use):
        g.mix[...] = pltpu.roll(g.mix[...], quarter, 1)
        for i in range(n_col):
            for odd_channel in range(2):
                upper = g.mix[pl.ds(4 * i + odd_channel, 8, stride=32), :]
                lower = g.mix[pl.ds(4 * i + 2 + odd_channel, 8, stride=32), :]
                p.snd7[i, 16 * odd_channel : 16 * odd_channel + 16] = jnp.concatenate(
                    [upper, lower], axis=0
                ).astype(bf16)
        parts = Exchange("col", col_at, n_col, lambda i: p.snd7.at[i], p.rcv7, p.s7, p.r7, True)
        parts.start_all()
        pending.append(parts.sent)
        p.rcv7[col_at] = p.snd7[col_at]
        parts.take_all()
        halves = [sum(p.rcv7[4 * h + q].astype(f32) for q in range(4)) for h in range(2)]
        mixed = jnp.concatenate(halves, axis=1)
        swapped = part_swap(mixed, -1.0)
        operand = jnp.concatenate([mixed, swapped], axis=1).astype(bf16)
        by_rows = dot(operand, g.tx[...], NN)
        for s in range(pairs):
            even = by_rows[0:16, 128 * s : 128 * s + 128]
            odd = by_rows[16:32, 128 * s : 128 * s + 128]
            p.snd9[2 * s] = jnp.where(low, even, pltpu.roll(odd, 64, 1)).astype(bf16)
            p.snd9[2 * s + 1] = jnp.where(low, pltpu.roll(even, 64, 1), odd).astype(bf16)
        rows = Exchange("row", row_at, n_row, lambda i: p.snd9.at[i], p.rcv9, p.s9, p.r9, True)
        rows.start_all()
        pending.append(rows.sent)
        p.rcv9[row_at] = p.snd9[row_at]
        cover_rows()
        rows.take_all()
        got = p.rcv9[...].astype(f32)
        own_rows = jnp.concatenate(
            [got[:, :8].reshape(8 * n_row, 128), got[:, 8:].reshape(8 * n_row, 128)], axis=1
        )
        lhs = jnp.transpose(own_rows).astype(bf16)
        cells = Exchange("col", col_at, n_col, lambda i: p.snd10.at[i], p.rcv10, p.s10, p.r10, False)

        def make_cells(d):
            peer = cells.peer(d)
            p.snd10[peer] = dot(lhs, g.ty[peer], NN).astype(bf16)
            cells.start(d)

        each(n_col, make_cells)
        pending.append(cells.sent)
        cover_cells()
        use(col_at, dot(lhs, g.ty[col_at], NN), 0)

        def take(d):
            origin = cells.take(d)
            use(origin, p.rcv10[origin].astype(f32), d)

        each(n_col, take)

    def first_fill(p):
        for copy in p.edge_copies:
            copy.wait_recv()
        fill_wide(p, 0, HALF_FILL)

    def rest_of_conv(p):
        fill_wide(p, HALF_FILL, 17)
        convolve(p)

    def regroup(p):
        def one(x):
            p.raw[pl.ds(aligned(x * 32 + 32, 32), 32), :] = grid_row(x).astype(bf16)

        one(0)
        one(63)
        p.row_copies = send_halo_rows(p)
        loop(62, lambda x: one(x + 1))

    def widen_now(p):
        p.edge_copies = widen(p, p.row_copies)

    def place(slot, value):
        for half in range(2):
            g.stage[pl.ds(aligned(half * 2048 + slot * 256, 256), 256), :] = value[:, 128 * half : 128 * half + 128]

    def placed(slot):
        return jnp.concatenate(
            [g.stage[pl.ds(aligned(half * 2048 + slot * 256, 256), 256), :] for half in range(2)], axis=1
        )

    def grid_row(x):
        return jnp.concatenate([g.stage[pl.ds(2048 * half + x, 32, stride=64), :] for half in range(2)], axis=1)

    def put_grid_row(x, value):
        for half in range(2):
            g.stage[pl.ds(2048 * half + x, 32, stride=64), :] = value[:, 128 * half : 128 * half + 128]

    low = lax.broadcasted_iota(jnp.int32, (16, 128), 1) < 64
    quarter = lax.rem(col_at, 4) * 32
    back_shift = lax.rem(128 - quarter, 128)

    def cover_field():
        loads[0].wait()
        for i in range(n_col):
            place(i, g.vbuf[i].astype(f32))

        regroup(first)
        g.cot[...] = cot_ref[...].astype(f32)
        spread_taps(first, False)
        g.bias[...] = column(bias_ref)
        g.proj[...] = column(proj_ref)
        loads[1].wait()
        loads[2].wait()

    def column(ref):
        diagonal = lax.broadcasted_iota(jnp.int32, (32, 32), 0) == lax.broadcasted_iota(jnp.int32, (32, 32), 1)
        value = jnp.sum(jnp.where(diagonal, jnp.broadcast_to(ref[...], (32, 32)), 0.0), axis=1, keepdims=True)
        return jnp.broadcast_to(value, (32, 256))

    to_modes(first, lambda i: v_ref.at[i], False, cover_field, lambda: widen_now(first))
    loads[3].wait()
    for kl in range(4):

        def add_channel(i, sums):
            real, imag = sums
            s_re = first.modes[pl.ds(8 * i + kl, 1), :][:, :32]
            s_im = first.modes[pl.ds(8 * i + 4 + kl, 1), :][:, :32]
            w_re = g.weight[kl, 0, i].astype(f32)
            w_im = g.weight[kl, 1, i].astype(f32)
            return (real + (w_re * s_re - w_im * s_im), imag + (w_re * s_im + w_im * s_re))

        zero = jnp.zeros((32, 32), f32)
        real, imag = lax.fori_loop(0, 32, add_channel, (zero, zero))
        factor = jnp.where(row_at * 4 + kl == 0, 1.0, 2.0).astype(f32) * scale
        g.mix[32 * kl : 32 * kl + 32, 0:32] = real.astype(bf16).astype(f32) * factor
        g.mix[128 + 32 * kl : 160 + 32 * kl, 0:32] = imag.astype(bf16).astype(f32) * factor

    back = Exchange("col", col_at, n_col, lambda i: second.snd1.at[i], second.buf1, second.s1, second.r1, False)

    def activate(slot, cells, d):
        conv = placed(slot)
        rounded = []
        for ch in range(4):
            channel = slot * 4 + ch
            rows = slice(64 * ch, 64 * ch + 64)
            bias = jnp.broadcast_to(g.bias[pl.ds(channel, 1), :], (64, 256))
            proj = jnp.broadcast_to(g.proj[pl.ds(channel, 1), :], (64, 256))
            pre = conv[rows] + cells[rows] + bias
            cdf = 0.5 * (1.0 + lax.erf(pre * math.sqrt(0.5)))
            pdf = jnp.exp(-0.5 * pre * pre) * (1.0 / math.sqrt(TWO_PI))
            grad = (proj * g.cot[...]) * (cdf + pre * pdf)
            rounded.append(grad.astype(bf16))
            second.snd1[slot, 64 * ch : 64 * ch + 64] = rounded[ch]
            at = pl.ds(aligned(channel * 8, 8), 8)
            g.bias_rows[at, :] = jnp.sum(grad.reshape(8, 8, 256), axis=0)
            g.proj_rows[at, :] = jnp.sum(((pre * cdf) * g.cot[...]).reshape(8, 8, 256), axis=0)
        if not isinstance(d, int):
            back.start(n_col - d)
        place(slot, jnp.concatenate(rounded, axis=0).astype(f32))

    to_grid(first, lambda: first_fill(first), lambda: rest_of_conv(first), activate)

    piece = 80 // owners

    def cover_grad():
        regroup(second)
        of_channel = (lax.broadcasted_iota(jnp.int32, (32, 256), 1) // 8) == lax.broadcasted_iota(
            jnp.int32, (32, 256), 0
        )
        gather = jnp.where(of_channel, 1.0, 0.0)
        for at, rows in ((0, g.bias_rows), (32, g.proj_rows)):
            g.sums[at : at + 32] = lax.dot_general(
                gather, rows[...], NN, precision=HIGH, preferred_element_type=f32
            )
        g.sums[64:128] = jnp.zeros((64, 256), f32)
        g.outer[...] = jnp.zeros_like(g.outer)

        def block(t):
            rows = first.wide[pl.ds(aligned(t * 768, 16), 960), :]
            grads = second.raw[pl.ds(aligned(t * 256 + 32, 32), 256), :]
            g.outer[...] += dot(rows, grads, NT)

        loop(8, block)
        lane = lax.broadcasted_iota(jnp.int32, (96, 128), 1)
        taps = []
        for a in range(3):
            total = jnp.zeros((96, 128), f32)
            for x in range(8):
                here = g.outer[96 * (x + a) : 96 * (x + a) + 96, 128 * (x // 4) : 128 * (x // 4) + 128]
                total = total + (pltpu.roll(here, 128 - 32 * (x % 4), 1) if x % 4 else here)
            taps.append(jnp.where(lane < 32, total, 0.0))
        taps = jnp.concatenate(taps, axis=0)
        packed = taps[0:72]
        for q in range(1, 4):
            packed = packed + pltpu.roll(taps[72 * q : 72 * q + 72], 32 * q, 1)
        lanes_sum = lax.dot_general(
            jnp.ones((8, 256), f32), g.sums[...], NT, precision=HIGH, preferred_element_type=f32
        )
        g.part[...] = (jnp.concatenate([packed, lanes_sum], axis=0) * scale).reshape(owners, piece, 128)
        for t in range(owners):

            @pl.when(row_at != t)
            def _():
                push(g.part.at[t], g.got_row.at[row_at], g.row_s.at[t], g.row_r, "row", t).start()

        spread_taps(second, True)

    def sum_rows():
        @pl.when(row_at < owners)
        def _():
            g.got_row[row_at] = g.part[row_at]
            Exchange("row", row_at, n_row, None, g.got_row, g.row_s.at[0], g.row_r, True).take_all()
            g.sum_row[...] = jnp.sum(g.got_row[...], axis=0)
            g.got_col[col_at] = g.sum_row[...]
            Exchange("col", col_at, n_col, lambda i: g.sum_row, g.got_col, g.col_s, g.col_r, True).start_all()

    def sum_cols():
        @pl.when(row_at < owners)
        def _():
            sums = Exchange("col", col_at, n_col, lambda i: g.sum_row, g.got_col, g.col_s, g.col_r, True)
            sums.take_all()
            sums.sent()
            g.total[...] = jnp.sum(g.got_col[...], axis=0)
            g.got_all[row_at] = g.total[...]

            def send(d):
                peer = (row_at + d) & (n_row - 1)
                push(g.total, g.got_all.at[row_at], g.all_s, g.all_r.at[row_at], "row", peer).start()

            each(n_row, send)

    def cover_rows_back():
        widen_now(second)
        sum_rows()

    def cover_rows_out():
        first_fill(second)
        sum_cols()

    def write_out(slot, cells, d):
        at = pl.ds(aligned(slot * 256, 256), 256)
        g.out[at, :] = placed(slot) + cells
        pltpu.make_async_copy(g.out.at[at], out_ref.at[at], g.out_s).start()

    to_modes(second, lambda i: second.snd1.at[i], True, cover_grad, cover_rows_back)
    own_mode = lax.broadcasted_iota(jnp.int32, (256, 128), 0) & 3
    second.modes[...] = second.modes[...] * jnp.where(row_at * 4 + own_mode == 0, 1.0, 2.0)
    for kl in range(4):
        g_re = second.modes[pl.ds(kl, 32, stride=8), :][:, :32]
        g_im = second.modes[pl.ds(4 + kl, 32, stride=8), :][:, :32]

        def one_channel(i, carry):
            w_re = g.weight[kl, 0, i].astype(f32)
            w_im = g.weight[kl, 1, i].astype(f32)
            b_re = jnp.sum(w_re * g_re + w_im * g_im, axis=0, keepdims=True)
            b_im = jnp.sum(w_re * g_im - w_im * g_re, axis=0, keepdims=True)
            g.mix[pl.ds(32 * kl + i, 1), 0:32] = b_re.astype(bf16).astype(f32) * scale
            g.mix[pl.ds(128 + 32 * kl + i, 1), 0:32] = b_im.astype(bf16).astype(f32) * scale
            return carry

        lax.fori_loop(0, 32, one_channel, 0)
    to_grid(second, cover_rows_out, lambda: rest_of_conv(second), write_out)

    modes_ref[0] = first.modes[...]
    modes_ref[1] = second.modes[...]
    for t in range(owners):

        @pl.when(row_at != t)
        def _():
            arrived = push(g.part.at[t], g.got_all.at[t], g.row_s.at[t], g.all_r.at[t], "row", t)
            arrived.wait_recv()
            arrived.wait_send()

    @pl.when(row_at < owners)
    def _():
        Exchange("row", row_at, n_row, None, g.got_row, g.all_s, g.row_r, True).sent()

    small_ref[...] = g.got_all[...].reshape(80, 128)
    for wait in pending:
        wait()
    pltpu.make_async_copy(g.out, out_ref, g.out_s).wait()


def outputs_kernel(cells_ref, modes_ref, small_ref, out_ref, gspec_ref, conv_ref, bias_ref, proj_ref, weight, cells, sems):
    copies = []
    loads = []
    parts = [pl.ds(512 * q, 512) for q in range(4)]
    for q, at in enumerate(parts):
        loads.append(pltpu.make_async_copy(cells_ref.at[at], cells.at[at], sems.at[q]))
        loads[q].start()
    for kl in range(4):
        g_re = modes_ref[pl.ds(256 + kl, 32, stride=8), :][:, :32]
        g_im = modes_ref[pl.ds(260 + kl, 32, stride=8), :][:, :32]
        for i in range(32):
            s_re = modes_ref[8 * i + kl : 8 * i + kl + 1, :][:, :32]
            s_im = modes_ref[8 * i + 4 + kl : 8 * i + 5 + kl, :][:, :32]
            weight[kl, 0, i] = g_re * s_re + g_im * s_im
            weight[kl, 1, i] = g_im * s_re - g_re * s_im
        copies.append(pltpu.make_async_copy(weight.at[kl], gspec_ref.at[kl], sems.at[4 + kl]))
        copies[-1].start()
        loads[kl].wait()
        copies.append(pltpu.make_async_copy(cells.at[parts[kl]], out_ref.at[parts[kl]], sems.at[8 + kl]))
        copies[-1].start()
    for q in range(4):
        rows = small_ref[0:72]
        conv_ref[72 * q : 72 * q + 72] = (pltpu.roll(rows, 128 - 32 * q, 1) if q else rows)[:, :32]
    rows = small_ref[72:80]
    bias_ref[...] = rows[0:1, :32]
    proj_ref[...] = pltpu.roll(rows, 96, 1)[0:1, :32]
    for copy in copies:
        copy.wait()


def per_device(n_row, n_col, ocean_field, cotangent, conv_weight, conv_bias, projection, mode_weight):
    chans, rows_dev, cols_dev = ocean_field.shape
    ky_dev = mode_weight.shape[0]
    kx_all = mode_weight.shape[4] * n_col
    owners = min(10, n_row)
    ty, tx = (jnp.asarray(t) for t in tables(n_row, n_col, ky_dev, rows_dev, cols_dev, kx_all))
    vmem = pl.BlockSpec(memory_space=pltpu.VMEM)
    hbm = pl.BlockSpec(memory_space=pl.ANY)
    one = pass_scratch(n_row, n_col)
    scratch = list(one.values()) * 2 + list(common_scratch(n_row, n_col, rows_dev * n_row, owners).values())
    cells, modes, small = pl.pallas_call(
        functools.partial(step_kernel, n_row, n_col, owners),
        out_shape=[
            jax.ShapeDtypeStruct((chans * rows_dev, cols_dev), jnp.float32),
            jax.ShapeDtypeStruct((2, 256, 128), jnp.float32),
            jax.ShapeDtypeStruct((80, 128), jnp.float32),
        ],
        in_specs=[hbm, vmem, vmem, vmem, vmem, hbm, hbm, hbm],
        out_specs=[hbm, vmem, vmem],
        scratch_shapes=scratch,
        compiler_params=pltpu.CompilerParams(
            collective_id=0, has_side_effects=True, vmem_limit_bytes=VMEM_BYTES
        ),
        name="layer_step",
    )(
        ocean_field.reshape(n_col, 256, cols_dev),
        cotangent,
        conv_weight.reshape(9 * chans, chans),
        conv_bias.reshape(1, chans),
        projection.reshape(1, chans),
        mode_weight,
        ty,
        tx,
    )
    grad_input, grad_spec, grad_conv, grad_bias, grad_proj = pl.pallas_call(
        outputs_kernel,
        out_shape=[
            jax.ShapeDtypeStruct((chans * rows_dev, cols_dev), jnp.float32),
            jax.ShapeDtypeStruct(mode_weight.shape, jnp.float32),
            jax.ShapeDtypeStruct((9 * chans, chans), jnp.float32),
            jax.ShapeDtypeStruct((1, chans), jnp.float32),
            jax.ShapeDtypeStruct((1, chans), jnp.float32),
        ],
        in_specs=[hbm, vmem, vmem],
        out_specs=[hbm, hbm, vmem, vmem, vmem],
        scratch_shapes=[
            pltpu.VMEM(mode_weight.shape, jnp.float32),
            pltpu.VMEM((chans * rows_dev, cols_dev), jnp.float32),
            pltpu.SemaphoreType.DMA((12,)),
        ],
        compiler_params=pltpu.CompilerParams(vmem_limit_bytes=VMEM_BYTES),
        name="layer_outputs",
    )(cells, modes.reshape(512, 128), small)
    return (
        grad_input.reshape(ocean_field.shape),
        grad_spec,
        grad_conv.reshape(conv_weight.shape),
        grad_bias.reshape(chans),
        grad_proj.reshape(chans),
    )


def solution(mesh):
    placed = (
        P(None, "row", "col"),
        P("row", "col"),
        P(),
        P(),
        P(),
        P("row", None, None, None, "col"),
    )
    return jax.shard_map(
        functools.partial(per_device, mesh.shape["row"], mesh.shape["col"]),
        mesh=mesh,
        in_specs=placed,
        out_specs=(P(None, "row", "col"), P("row", None, None, None, "col"), P(), P(), P()),
        check_vma=False,
    )
```

```python
import functools
import math

import jax
import jax.numpy as jnp
import ml_dtypes
import numpy as np
from jax import lax
from jax.experimental import pallas as pl
from jax.experimental.pallas import tpu as pltpu
from jax.sharding import PartitionSpec as P

TWO_PI = 2.0 * math.pi
HIGH = lax.Precision.HIGHEST
HALF_FILL = 8
VMEM_BYTES = 56 * 1024 * 1024


def angle_pair(products, period):
    angles = (products % period).astype(np.float32) * np.float32(TWO_PI / period)
    return (np.cos(angles).astype(ml_dtypes.bfloat16), np.sin(angles).astype(ml_dtypes.bfloat16))


def tables(n_row, n_col, ky_dev, rows_dev, cols_dev, kx_all):
    modes, nx, ny = (ky_dev * n_row, rows_dev * n_row, cols_dev * n_col)
    cosine, sine = angle_pair(np.arange(modes)[:, None] * np.arange(ny)[None, :], ny)
    ty = np.stack([cosine.reshape(n_row, ky_dev, ny), -sine.reshape(n_row, ky_dev, ny)], axis=1)
    ty = ty.reshape(2 * modes, n_col, cols_dev).transpose(1, 0, 2)
    ids = np.arange(kx_all)
    freqs = np.where(ids < modes, ids, ids - 2 * modes) % nx
    cosine, sine = angle_pair(freqs[:, None] * np.arange(nx)[None, :], nx)
    return np.ascontiguousarray(ty), np.concatenate([cosine, sine], axis=0)


NT = (((1,), (1,)), ((), ()))
NN = (((1,), (0,)), ((), ()))
TN = (((0,), (0,)), ((), ()))


def dot(a, b, dims):
    return lax.dot_general(a, b, dims, preferred_element_type=jnp.float32)


def push(src, dst, send_sem, recv_sem, axis, peer):
    return pltpu.make_async_remote_copy(
        src_ref=src,
        dst_ref=dst,
        send_sem=send_sem,
        recv_sem=recv_sem,
        device_id={axis: peer},
        device_id_type=pl.DeviceIdType.MESH,
    )


class Exchange:
    def __init__(self, axis, me, size, source, slots, send_sem, recv_sem, shared):
        (self.axis, self.me, self.size, self.source, self.slots) = (axis, me, size, source, slots)
        (self.send_sem, self.recv_sem, self.shared) = (send_sem, recv_sem, shared)

    def peer(self, step):
        return (self.me + step) & (self.size - 1)

    def copy(self, step, src, dst, peer):
        recv_sem = self.recv_sem if self.shared else self.recv_sem.at[step]
        return push(src, dst, self.send_sem, recv_sem, self.axis, peer)

    def start(self, step):
        peer = self.peer(step)
        self.copy(step, self.source(peer), self.slots.at[self.me], peer).start()

    def start_all(self):
        each(self.size, self.start)

    def take(self, step):
        origin = (self.me - step) & (self.size - 1)
        self.copy(step, self.slots.at[origin], self.slots.at[origin], origin).wait_recv()
        return origin

    def every(self):
        rest = self.slots.at[pl.ds(0, self.size - 1)]
        return self.copy(1, rest, rest, self.peer(1))

    def take_all(self):
        self.every().wait_recv()

    def sent(self):
        self.every().wait_send()


def each(size, body):
    def step(index, carry):
        body(index)
        return carry

    lax.fori_loop(1, size, step, 0)


def part_swap(value, sign):
    rows = value.shape[0]
    is_real = (lax.broadcasted_iota(jnp.int32, value.shape, 0) & 4) == 0
    after = pltpu.roll(value, rows - 4, 0)
    before = pltpu.roll(value, 4, 0)
    return jnp.where(is_real, sign * after, -sign * before)


class Group:
    def __init__(self, names, refs):
        for name, ref in zip(names, refs):
            setattr(self, name, ref)


def aligned(value, to):
    return pl.multiple_of(value, to)


def pass_scratch(n_row, n_col):
    bf16, f32 = (jnp.bfloat16, jnp.float32)
    dma = pltpu.SemaphoreType.DMA
    found = dict(
        snd1=pltpu.VMEM((n_col, 256, 256), bf16),
        buf1=pltpu.VMEM((n_col, 256, 256), bf16),
        snd3=pltpu.VMEM((n_row, 16, 128), bf16),
        rcv3=pltpu.VMEM((n_row, 16, 128), bf16),
        snd5=pltpu.VMEM((2, 32, 128), bf16),
        rcv5=pltpu.VMEM((n_col, 32, 128), bf16),
        modes=pltpu.VMEM((256, 128), f32),
        flat=pltpu.VMEM((64, 128), f32),
        snd7=pltpu.VMEM((n_col, 32, 128), bf16),
        rcv7=pltpu.VMEM((n_col, 32, 128), bf16),
        snd9=pltpu.VMEM((n_row, 16, 128), bf16),
        rcv9=pltpu.VMEM((n_row, 16, 128), bf16),
        snd10=pltpu.VMEM((n_col, 256, 256), bf16),
        rcv10=pltpu.VMEM((n_col, 256, 256), bf16),
        raw=pltpu.VMEM((68 * 32, 256), bf16),
        halo=pltpu.VMEM((2, 32, 256), bf16),
        edge_out=pltpu.VMEM((2, 16, 68 * 32), bf16),
        edge_in=pltpu.VMEM((2, 16, 68 * 32), bf16),
        wide=pltpu.VMEM((68 * 96, 256), bf16),
        taps=pltpu.VMEM((256, 1024), bf16),
        own=dma,
        hs=dma((2,)),
        hr=dma((2,)),
        es=dma((2,)),
        er=dma((2,)),
    )
    for step, size in ((1, n_col), (3, n_row), (5, n_col), (7, n_col), (9, n_row), (10, n_col)):
        found["s%d" % step] = dma
        found["r%d" % step] = dma((size,)) if step in (1, 10) else dma
    return found


def common_scratch(n_row, n_col, nx, owners):
    bf16, f32 = (jnp.bfloat16, jnp.float32)
    dma = pltpu.SemaphoreType.DMA
    piece = 80 // owners
    return dict(
        vbuf=pltpu.VMEM((n_col, 256, 256), bf16),
        ty=pltpu.VMEM((n_col, 8 * n_row, 256), bf16),
        tx=pltpu.VMEM((512, nx), bf16),
        weight=pltpu.VMEM((4, 2, 32, 32, 32), bf16),
        stage=pltpu.VMEM((4096, 128), f32),
        bias=pltpu.VMEM((32, 256), f32),
        proj=pltpu.VMEM((32, 256), f32),
        bias_rows=pltpu.VMEM((256, 256), f32),
        proj_rows=pltpu.VMEM((256, 256), f32),
        cot=pltpu.VMEM((64, 256), f32),
        out=pltpu.VMEM((2048, 256), f32),
        out_s=dma,
        acc=pltpu.VMEM((8 * n_row, 256), f32),
        rows_x=pltpu.VMEM((32, nx), bf16),
        mix=pltpu.VMEM((256, 128), f32),
        packed=pltpu.VMEM((2, 32, 32, 128), f32),
        mixed_back=pltpu.VMEM((64, 128), f32),
        outer=pltpu.VMEM((960, 256), f32),
        sums=pltpu.VMEM((128, 256), f32),
        part=pltpu.VMEM((owners, piece, 128), f32),
        got_row=pltpu.VMEM((n_row, piece, 128), f32),
        sum_row=pltpu.VMEM((piece, 128), f32),
        got_col=pltpu.VMEM((n_col, piece, 128), f32),
        total=pltpu.VMEM((piece, 128), f32),
        got_all=pltpu.VMEM((owners, piece, 128), f32),
        load=dma((4,)),
        row_s=dma((owners,)),
        row_r=dma,
        col_s=dma,
        col_r=dma,
        all_s=dma,
        all_r=dma((owners,)),
    )


def step_kernel(n_row, n_col, owners, *refs):
    (v_ref, cot_ref, taps_ref, bias_ref, proj_ref, w_hbm, ty_hbm, tx_hbm, out_ref, modes_ref, small_ref, *rest) = refs
    nx = 64 * n_row
    names = list(pass_scratch(n_row, n_col))
    first = Group(names, rest[: len(names)])
    second = Group(names, rest[len(names) : 2 * len(names)])
    g = Group(list(common_scratch(n_row, n_col, nx, owners)), rest[2 * len(names) :])
    row_at = lax.axis_index("row")
    col_at = lax.axis_index("col")
    pairs = n_row // 2
    scale = 1.0 / math.sqrt((64 * n_row) * (256 * n_col))
    bf16, f32 = (jnp.bfloat16, jnp.float32)
    pending = []

    loads = [
        pltpu.make_async_copy(v_ref, g.vbuf, g.load.at[0]),
        pltpu.make_async_copy(ty_hbm, g.ty, g.load.at[1]),
        pltpu.make_async_copy(tx_hbm, g.tx, g.load.at[2]),
        pltpu.make_async_copy(w_hbm, g.weight, g.load.at[3]),
    ]
    for load in loads:
        load.start()
    barrier = pltpu.get_barrier_semaphore()
    each(n_col, lambda d: pl.semaphore_signal(
        barrier, inc=1, device_id={"col": (col_at + d) & (n_col - 1)}, device_id_type=pl.DeviceIdType.MESH))
    each(n_row, lambda d: pl.semaphore_signal(
        barrier, inc=1, device_id={"row": (row_at + d) & (n_row - 1)}, device_id_type=pl.DeviceIdType.MESH))
    pl.semaphore_wait(barrier, n_col - 1 + n_row - 1)

    def loop(size, body):
        def step(index, carry):
            body(index)
            return carry

        lax.fori_loop(0, size, step, 0)

    def send_halo_rows(p):
        up = lax.rem(row_at + n_row - 1, n_row)
        down = lax.rem(row_at + 1, n_row)
        copies = [
            push(p.raw.at[pl.ds(32, 32)], p.halo.at[1], p.hs.at[0], p.hr.at[0], "row", up),
            push(p.raw.at[pl.ds(64 * 32, 32)], p.halo.at[0], p.hs.at[1], p.hr.at[1], "row", down),
        ]
        for copy in copies:
            copy.start()
            pending.append(copy.wait_send)
        return copies

    def widen(p, row_copies):
        for copy in row_copies:
            copy.wait_recv()
        above = jnp.where(row_at > 0, 1.0, 0.0)
        below = jnp.where(row_at < n_row - 1, 1.0, 0.0)
        p.raw[0:32] = (p.halo[0].astype(f32) * above).astype(bf16)
        p.raw[65 * 32 : 66 * 32] = (p.halo[1].astype(f32) * below).astype(bf16)
        p.raw[66 * 32 : 68 * 32] = jnp.zeros((64, 256), bf16)
        row = lax.broadcasted_iota(jnp.int32, (32, 256), 0)
        lane = lax.broadcasted_iota(jnp.int32, (32, 256), 1)
        pick = ((row == 0) & (lane == 0)) | ((row == 16) & (lane == 255))
        edges = dot(jnp.where(pick, 1.0, 0.0).astype(bf16), p.raw[...], NT)
        p.edge_out[0] = edges[0:16].astype(bf16)
        p.edge_out[1] = edges[16:32].astype(bf16)
        left = lax.rem(col_at + n_col - 1, n_col)
        right = lax.rem(col_at + 1, n_col)
        copies = [
            push(p.edge_out.at[0], p.edge_in.at[1], p.es.at[0], p.er.at[0], "col", left),
            push(p.edge_out.at[1], p.edge_in.at[0], p.es.at[1], p.er.at[1], "col", right),
        ]
        for copy in copies:
            copy.start()
            pending.append(copy.wait_send)
        return copies

    def fill_wide(p, start, stop):
        row = lax.broadcasted_iota(jnp.int32, (16, 128), 0)
        lane = lax.broadcasted_iota(jnp.int32, (16, 128), 1)
        put_left = jnp.where((row == 0) & (lane == 0) & (col_at > 0), 1.0, 0.0).astype(bf16)
        put_right = jnp.where((row == 0) & (lane == 127) & (col_at < n_col - 1), 1.0, 0.0).astype(bf16)
        lanes = lax.broadcasted_iota(jnp.int32, (128, 128), 1)

        def chunk(q):
            here = p.raw[pl.ds(aligned(q * 128, 128), 128), :].astype(f32)
            from_left = dot(p.edge_in[0, :, pl.ds(aligned(q * 128, 128), 128)], put_left, TN)
            from_right = dot(p.edge_in[1, :, pl.ds(aligned(q * 128, 128), 128)], put_right, TN)
            before = pltpu.roll(here, 1, 1)
            after = pltpu.roll(here, 255, 1)
            before = jnp.concatenate([jnp.where(lanes == 0, from_left, before[:, :128]), before[:, 128:]], axis=1)
            after = jnp.concatenate([after[:, :128], jnp.where(lanes == 127, from_right, after[:, 128:])], axis=1)
            for x in range(4):
                for b, value in enumerate((before, here, after)):
                    base = aligned(q * 384 + 96 * x + 32 * b, 32)
                    p.wide[pl.ds(base, 32), :] = value[32 * x : 32 * x + 32].astype(bf16)

        loop(stop - start, lambda q: chunk(q + start))

    def spread_taps(p, turned):
        row = lax.broadcasted_iota(jnp.int32, (32, 1024), 0)
        lane = lax.broadcasted_iota(jnp.int32, (32, 1024), 1)
        padded = jnp.zeros((32, 1024), f32)
        for m in range(9):
            source = 8 - m if turned else m
            spot = jnp.where(lane == row + 32 * m, 1.0, 0.0).astype(bf16)
            padded = padded + dot(taps_ref[32 * source : 32 * source + 32, :], spot, NN if turned else TN)
        for x in range(8):
            p.taps[32 * x : 32 * x + 32, :] = (pltpu.roll(padded, 96 * x, 1) if x else padded).astype(bf16)

    def convolve(p):
        def block(t):
            rows = p.wide[pl.ds(aligned(t * 768, 16), 1024), :]
            result = dot(p.taps[...], rows, NN)
            for x in range(8):
                put_grid_row(8 * t + x, result[32 * x : 32 * x + 32])

        loop(8, block)

    def to_modes(p, source, started, cover, cover_rows):
        own = pltpu.make_async_copy(source(col_at), p.buf1.at[col_at], p.own)
        own.start()
        fields = Exchange("col", col_at, n_col, source, p.buf1, p.s1, p.r1, False)
        if not started:
            fields.start_all()
        pending.append(fields.sent)
        cover()
        own.wait()
        g.acc[...] = dot(g.ty[col_at], p.buf1[col_at], NT)

        def add_block(d):
            origin = fields.take(d)
            g.acc[...] += dot(g.ty[origin], p.buf1[origin], NT)

        each(n_col, add_block)
        whole = g.acc[...]
        upper = whole[:, :128].reshape(n_row, 8, 128)
        lower = whole[:, 128:].reshape(n_row, 8, 128)
        p.snd3[...] = jnp.concatenate([upper, lower], axis=1).astype(bf16)
        rows = Exchange("row", row_at, n_row, lambda i: p.snd3.at[i], p.rcv3, p.s3, p.r3, True)
        rows.start_all()
        pending.append(rows.sent)
        p.rcv3[row_at] = p.snd3[row_at]
        cover_rows()
        rows.take_all()
        for s in range(pairs):
            one = p.rcv3[2 * s].astype(f32)
            two = p.rcv3[2 * s + 1].astype(f32)
            even = jnp.where(low, one, pltpu.roll(two, 64, 1))
            odd = jnp.where(low, pltpu.roll(one, 64, 1), two)
            g.rows_x[0:16, 128 * s : 128 * s + 128] = even.astype(bf16)
            g.rows_x[16:32, 128 * s : 128 * s + 128] = odd.astype(bf16)
        both = dot(g.rows_x[...], g.tx[...], NT)
        coeffs = (both[:, :256] + part_swap(both[:, 256:], 1.0)) * scale
        coeffs = jnp.concatenate([coeffs[0:8], coeffs[16:24], coeffs[8:16], coeffs[24:32]], axis=0)
        p.snd5[0] = coeffs[:, :128].astype(bf16)
        p.snd5[1] = coeffs[:, 128:].astype(bf16)
        parts = Exchange("col", col_at, n_col, lambda i: p.snd5.at[i // 4], p.rcv5, p.s5, p.r5, True)
        parts.start_all()
        pending.append(parts.sent)
        p.rcv5[col_at] = p.snd5[col_at // 4]
        parts.take_all()
        for i in range(n_col):
            p.modes[32 * i : 32 * i + 32] = pltpu.roll(p.rcv5[i].astype(f32), back_shift, 1)

    def to_grid(p, cover_rows, cover_cells, use):
        for i in range(n_col):
            for odd_channel in range(2):
                upper = g.mix[pl.ds(4 * i + odd_channel, 8, stride=32), :]
                lower = g.mix[pl.ds(4 * i + 2 + odd_channel, 8, stride=32), :]
                p.snd7[i, 16 * odd_channel : 16 * odd_channel + 16] = jnp.concatenate(
                    [upper, lower], axis=0
                ).astype(bf16)
        parts = Exchange("col", col_at, n_col, lambda i: p.snd7.at[i], p.rcv7, p.s7, p.r7, True)
        parts.start_all()
        pending.append(parts.sent)
        p.rcv7[col_at] = p.snd7[col_at]
        parts.take_all()
        halves = [sum(p.rcv7[4 * h + q].astype(f32) for q in range(4)) for h in range(2)]
        mixed = jnp.concatenate(halves, axis=1)
        swapped = part_swap(mixed, -1.0)
        operand = jnp.concatenate([mixed, swapped], axis=1).astype(bf16)
        by_rows = dot(operand, g.tx[...], NN)
        for s in range(pairs):
            even = by_rows[0:16, 128 * s : 128 * s + 128]
            odd = by_rows[16:32, 128 * s : 128 * s + 128]
            p.snd9[2 * s] = jnp.where(low, even, pltpu.roll(odd, 64, 1)).astype(bf16)
            p.snd9[2 * s + 1] = jnp.where(low, pltpu.roll(even, 64, 1), odd).astype(bf16)
        rows = Exchange("row", row_at, n_row, lambda i: p.snd9.at[i], p.rcv9, p.s9, p.r9, True)
        rows.start_all()
        pending.append(rows.sent)
        p.rcv9[row_at] = p.snd9[row_at]
        cover_rows()
        rows.take_all()
        got = p.rcv9[...].astype(f32)
        own_rows = jnp.concatenate(
            [got[:, :8].reshape(8 * n_row, 128), got[:, 8:].reshape(8 * n_row, 128)], axis=1
        )
        lhs = jnp.transpose(own_rows).astype(bf16)
        cells = Exchange("col", col_at, n_col, lambda i: p.snd10.at[i], p.rcv10, p.s10, p.r10, False)

        def make_cells(d):
            peer = cells.peer(d)
            p.snd10[peer] = dot(lhs, g.ty[peer], NN).astype(bf16)
            cells.start(d)

        each(n_col, make_cells)
        pending.append(cells.sent)
        cover_cells()
        use(col_at, dot(lhs, g.ty[col_at], NN), 0)

        def take(d):
            origin = cells.take(d)
            use(origin, p.rcv10[origin].astype(f32), d)

        each(n_col, take)

    def first_fill(p):
        for copy in p.edge_copies:
            copy.wait_recv()
        fill_wide(p, 0, HALF_FILL)

    def rest_of_conv(p):
        fill_wide(p, HALF_FILL, 17)
        convolve(p)

    def regroup(p):
        def one(x):
            p.raw[pl.ds(aligned(x * 32 + 32, 32), 32), :] = grid_row(x).astype(bf16)

        one(0)
        one(63)
        p.row_copies = send_halo_rows(p)
        loop(62, lambda x: one(x + 1))

    def widen_now(p):
        p.edge_copies = widen(p, p.row_copies)

    def place(slot, value):
        for half in range(2):
            g.stage[pl.ds(aligned(half * 2048 + slot * 256, 256), 256), :] = value[:, 128 * half : 128 * half + 128]

    def placed(slot):
        return jnp.concatenate(
            [g.stage[pl.ds(aligned(half * 2048 + slot * 256, 256), 256), :] for half in range(2)], axis=1
        )

    def grid_row(x):
        return jnp.concatenate([g.stage[pl.ds(2048 * half + x, 32, stride=64), :] for half in range(2)], axis=1)

    def put_grid_row(x, value):
        for half in range(2):
            g.stage[pl.ds(2048 * half + x, 32, stride=64), :] = value[:, 128 * half : 128 * half + 128]

    low = lax.broadcasted_iota(jnp.int32, (16, 128), 1) < 64
    quarter = lax.rem(col_at, 4) * 32
    back_shift = lax.rem(128 - quarter, 128)

    def flatten_modes(p):
        for part in range(2):
            p.flat[32 * part : 32 * part + 32] = jnp.concatenate(
                [p.modes[pl.ds(4 * part + kl, 32, stride=8), :][:, :32] for kl in range(4)], axis=1
            )

    def pack_weight(i):
        for part in range(2):
            g.packed[part, i] = jnp.concatenate([g.weight[kl, part, i].astype(f32) for kl in range(4)], axis=1)

    def spread_mix(parts):
        lane = lax.broadcasted_iota(jnp.int32, (32, 128), 1)
        mine = (lane >= quarter) & (lane < quarter + 32)
        for part, value in enumerate(parts):
            for kl in range(4):
                moved = pltpu.roll(value, (quarter + 128 - 32 * kl) & 127, 1)
                at = 128 * part + 32 * kl
                g.mix[at : at + 32, :] = jnp.where(mine, moved, 0.0)

    def cover_field():
        loads[0].wait()
        for i in range(n_col):
            place(i, g.vbuf[i].astype(f32))

        regroup(first)
        g.cot[...] = cot_ref[...].astype(f32)
        spread_taps(first, False)
        g.bias[...] = column(bias_ref)
        g.proj[...] = column(proj_ref)
        loads[3].wait()
        loop(32, pack_weight)
        loads[1].wait()
        loads[2].wait()

    def column(ref):
        diagonal = lax.broadcasted_iota(jnp.int32, (32, 32), 0) == lax.broadcasted_iota(jnp.int32, (32, 32), 1)
        value = jnp.sum(jnp.where(diagonal, jnp.broadcast_to(ref[...], (32, 32)), 0.0), axis=1, keepdims=True)
        return jnp.broadcast_to(value, (32, 256))

    to_modes(first, lambda i: v_ref.at[i], False, cover_field, lambda: widen_now(first))
    flatten_modes(first)

    def add_channel(i, sums):
        real, imag = sums
        s_re = first.flat[pl.ds(i, 1), :]
        s_im = first.flat[pl.ds(32 + i, 1), :]
        w_re = g.packed[0, i]
        w_im = g.packed[1, i]
        return (real + (w_re * s_re - w_im * s_im), imag + (w_re * s_im + w_im * s_re))

    zero = jnp.zeros((32, 128), f32)
    real, imag = lax.fori_loop(0, 32, add_channel, (zero, zero))
    frequency = row_at * 4 + lax.broadcasted_iota(jnp.int32, (32, 128), 1) // 32
    factor = jnp.where(frequency == 0, 1.0, 2.0) * scale
    spread_mix([value.astype(bf16).astype(f32) * factor for value in (real, imag)])

    back = Exchange("col", col_at, n_col, lambda i: second.snd1.at[i], second.buf1, second.s1, second.r1, False)

    def activate(slot, cells, d):
        conv = placed(slot)
        rounded = []
        for ch in range(4):
            channel = slot * 4 + ch
            rows = slice(64 * ch, 64 * ch + 64)
            bias = jnp.broadcast_to(g.bias[pl.ds(channel, 1), :], (64, 256))
            proj = jnp.broadcast_to(g.proj[pl.ds(channel, 1), :], (64, 256))
            pre = conv[rows] + cells[rows] + bias
            cdf = 0.5 * (1.0 + lax.erf(pre * math.sqrt(0.5)))
            pdf = jnp.exp(-0.5 * pre * pre) * (1.0 / math.sqrt(TWO_PI))
            grad = (proj * g.cot[...]) * (cdf + pre * pdf)
            rounded.append(grad.astype(bf16))
            second.snd1[slot, 64 * ch : 64 * ch + 64] = rounded[ch]
            at = pl.ds(aligned(channel * 8, 8), 8)
            g.bias_rows[at, :] = jnp.sum(grad.reshape(8, 8, 256), axis=0)
            g.proj_rows[at, :] = jnp.sum(((pre * cdf) * g.cot[...]).reshape(8, 8, 256), axis=0)
        if not isinstance(d, int):
            back.start(n_col - d)
        place(slot, jnp.concatenate(rounded, axis=0).astype(f32))

    to_grid(first, lambda: first_fill(first), lambda: rest_of_conv(first), activate)

    piece = 80 // owners

    def cover_grad():
        regroup(second)
        of_channel = (lax.broadcasted_iota(jnp.int32, (32, 256), 1) // 8) == lax.broadcasted_iota(
            jnp.int32, (32, 256), 0
        )
        gather = jnp.where(of_channel, 1.0, 0.0)
        for at, rows in ((0, g.bias_rows), (32, g.proj_rows)):
            g.sums[at : at + 32] = lax.dot_general(
                gather, rows[...], NN, precision=HIGH, preferred_element_type=f32
            )
        g.sums[64:128] = jnp.zeros((64, 256), f32)
        g.outer[...] = jnp.zeros_like(g.outer)

        def block(t):
            rows = first.wide[pl.ds(aligned(t * 768, 16), 960), :]
            grads = second.raw[pl.ds(aligned(t * 256 + 32, 32), 256), :]
            g.outer[...] += dot(rows, grads, NT)

        loop(8, block)
        lane = lax.broadcasted_iota(jnp.int32, (96, 128), 1)
        taps = []
        for a in range(3):
            total = jnp.zeros((96, 128), f32)
            for x in range(8):
                here = g.outer[96 * (x + a) : 96 * (x + a) + 96, 128 * (x // 4) : 128 * (x // 4) + 128]
                total = total + (pltpu.roll(here, 128 - 32 * (x % 4), 1) if x % 4 else here)
            taps.append(jnp.where(lane < 32, total, 0.0))
        taps = jnp.concatenate(taps, axis=0)
        packed = taps[0:72]
        for q in range(1, 4):
            packed = packed + pltpu.roll(taps[72 * q : 72 * q + 72], 32 * q, 1)
        lanes_sum = lax.dot_general(
            jnp.ones((8, 256), f32), g.sums[...], NT, precision=HIGH, preferred_element_type=f32
        )
        g.part[...] = (jnp.concatenate([packed, lanes_sum], axis=0) * scale).reshape(owners, piece, 128)
        for t in range(owners):

            @pl.when(row_at != t)
            def _():
                push(g.part.at[t], g.got_row.at[row_at], g.row_s.at[t], g.row_r, "row", t).start()

        spread_taps(second, True)

    def sum_rows():
        @pl.when(row_at < owners)
        def _():
            g.got_row[row_at] = g.part[row_at]
            Exchange("row", row_at, n_row, None, g.got_row, g.row_s.at[0], g.row_r, True).take_all()
            g.sum_row[...] = jnp.sum(g.got_row[...], axis=0)
            g.got_col[col_at] = g.sum_row[...]
            Exchange("col", col_at, n_col, lambda i: g.sum_row, g.got_col, g.col_s, g.col_r, True).start_all()

    def sum_cols():
        @pl.when(row_at < owners)
        def _():
            sums = Exchange("col", col_at, n_col, lambda i: g.sum_row, g.got_col, g.col_s, g.col_r, True)
            sums.take_all()
            sums.sent()
            g.total[...] = jnp.sum(g.got_col[...], axis=0)
            g.got_all[row_at] = g.total[...]

            def send(d):
                peer = (row_at + d) & (n_row - 1)
                push(g.total, g.got_all.at[row_at], g.all_s, g.all_r.at[row_at], "row", peer).start()

            each(n_row, send)

    def cover_rows_back():
        widen_now(second)
        sum_rows()

    def cover_rows_out():
        first_fill(second)
        sum_cols()

    def write_out(slot, cells, d):
        at = pl.ds(aligned(slot * 256, 256), 256)
        g.out[at, :] = placed(slot) + cells
        pltpu.make_async_copy(g.out.at[at], out_ref.at[at], g.out_s).start()

    to_modes(second, lambda i: second.snd1.at[i], True, cover_grad, cover_rows_back)
    own_mode = lax.broadcasted_iota(jnp.int32, (256, 128), 0) & 3
    second.modes[...] = second.modes[...] * jnp.where(row_at * 4 + own_mode == 0, 1.0, 2.0)
    flatten_modes(second)
    g_re = second.flat[0:32]
    g_im = second.flat[32:64]

    def one_channel(i):
        w_re = g.packed[0, i]
        w_im = g.packed[1, i]
        g.mixed_back[pl.ds(i, 1), :] = jnp.sum(w_re * g_re + w_im * g_im, axis=0, keepdims=True)
        g.mixed_back[pl.ds(32 + i, 1), :] = jnp.sum(w_re * g_im - w_im * g_re, axis=0, keepdims=True)

    loop(32, one_channel)
    spread_mix([g.mixed_back[32 * part : 32 * part + 32].astype(bf16).astype(f32) * scale for part in range(2)])
    to_grid(second, cover_rows_out, lambda: rest_of_conv(second), write_out)

    modes_ref[0] = first.modes[...]
    modes_ref[1] = second.modes[...]
    for t in range(owners):

        @pl.when(row_at != t)
        def _():
            arrived = push(g.part.at[t], g.got_all.at[t], g.row_s.at[t], g.all_r.at[t], "row", t)
            arrived.wait_recv()
            arrived.wait_send()

    @pl.when(row_at < owners)
    def _():
        Exchange("row", row_at, n_row, None, g.got_row, g.all_s, g.row_r, True).sent()

    small_ref[...] = g.got_all[...].reshape(80, 128)
    for wait in pending:
        wait()
    pltpu.make_async_copy(g.out, out_ref, g.out_s).wait()


def outputs_kernel(cells_ref, modes_ref, small_ref, out_ref, gspec_ref, conv_ref, bias_ref, proj_ref, weight, cells, sems):
    copies = []
    loads = []
    parts = [pl.ds(512 * q, 512) for q in range(4)]
    for q, at in enumerate(parts):
        loads.append(pltpu.make_async_copy(cells_ref.at[at], cells.at[at], sems.at[q]))
        loads[q].start()
    for kl in range(4):
        g_re = modes_ref[pl.ds(256 + kl, 32, stride=8), :][:, :32]
        g_im = modes_ref[pl.ds(260 + kl, 32, stride=8), :][:, :32]
        for i in range(32):
            s_re = modes_ref[8 * i + kl : 8 * i + kl + 1, :][:, :32]
            s_im = modes_ref[8 * i + 4 + kl : 8 * i + 5 + kl, :][:, :32]
            weight[kl, 0, i] = g_re * s_re + g_im * s_im
            weight[kl, 1, i] = g_im * s_re - g_re * s_im
        copies.append(pltpu.make_async_copy(weight.at[kl], gspec_ref.at[kl], sems.at[4 + kl]))
        copies[-1].start()
        loads[kl].wait()
        copies.append(pltpu.make_async_copy(cells.at[parts[kl]], out_ref.at[parts[kl]], sems.at[8 + kl]))
        copies[-1].start()
    for q in range(4):
        rows = small_ref[0:72]
        conv_ref[72 * q : 72 * q + 72] = (pltpu.roll(rows, 128 - 32 * q, 1) if q else rows)[:, :32]
    rows = small_ref[72:80]
    bias_ref[...] = rows[0:1, :32]
    proj_ref[...] = pltpu.roll(rows, 96, 1)[0:1, :32]
    for copy in copies:
        copy.wait()


def per_device(n_row, n_col, ocean_field, cotangent, conv_weight, conv_bias, projection, mode_weight):
    chans, rows_dev, cols_dev = ocean_field.shape
    ky_dev = mode_weight.shape[0]
    kx_all = mode_weight.shape[4] * n_col
    owners = min(10, n_row)
    ty, tx = (jnp.asarray(t) for t in tables(n_row, n_col, ky_dev, rows_dev, cols_dev, kx_all))
    vmem = pl.BlockSpec(memory_space=pltpu.VMEM)
    hbm = pl.BlockSpec(memory_space=pl.ANY)
    one = pass_scratch(n_row, n_col)
    scratch = list(one.values()) * 2 + list(common_scratch(n_row, n_col, rows_dev * n_row, owners).values())
    cells, modes, small = pl.pallas_call(
        functools.partial(step_kernel, n_row, n_col, owners),
        out_shape=[
            jax.ShapeDtypeStruct((chans * rows_dev, cols_dev), jnp.float32),
            jax.ShapeDtypeStruct((2, 256, 128), jnp.float32),
            jax.ShapeDtypeStruct((80, 128), jnp.float32),
        ],
        in_specs=[hbm, vmem, vmem, vmem, vmem, hbm, hbm, hbm],
        out_specs=[hbm, vmem, vmem],
        scratch_shapes=scratch,
        compiler_params=pltpu.CompilerParams(
            collective_id=0, has_side_effects=True, vmem_limit_bytes=VMEM_BYTES
        ),
        name="layer_step",
    )(
        ocean_field.reshape(n_col, 256, cols_dev),
        cotangent,
        conv_weight.reshape(9 * chans, chans),
        conv_bias.reshape(1, chans),
        projection.reshape(1, chans),
        mode_weight,
        ty,
        tx,
    )
    grad_input, grad_spec, grad_conv, grad_bias, grad_proj = pl.pallas_call(
        outputs_kernel,
        out_shape=[
            jax.ShapeDtypeStruct((chans * rows_dev, cols_dev), jnp.float32),
            jax.ShapeDtypeStruct(mode_weight.shape, jnp.float32),
            jax.ShapeDtypeStruct((9 * chans, chans), jnp.float32),
            jax.ShapeDtypeStruct((1, chans), jnp.float32),
            jax.ShapeDtypeStruct((1, chans), jnp.float32),
        ],
        in_specs=[hbm, vmem, vmem],
        out_specs=[hbm, hbm, vmem, vmem, vmem],
        scratch_shapes=[
            pltpu.VMEM(mode_weight.shape, jnp.float32),
            pltpu.VMEM((chans * rows_dev, cols_dev), jnp.float32),
            pltpu.SemaphoreType.DMA((12,)),
        ],
        compiler_params=pltpu.CompilerParams(vmem_limit_bytes=VMEM_BYTES),
        name="layer_outputs",
    )(cells, modes.reshape(512, 128), small)
    return (
        grad_input.reshape(ocean_field.shape),
        grad_spec,
        grad_conv.reshape(conv_weight.shape),
        grad_bias.reshape(chans),
        grad_proj.reshape(chans),
    )


def solution(mesh):
    placed = (
        P(None, "row", "col"),
        P("row", "col"),
        P(),
        P(),
        P(),
        P("row", None, None, None, "col"),
    )
    return jax.shard_map(
        functools.partial(per_device, mesh.shape["row"], mesh.shape["col"]),
        mesh=mesh,
        in_specs=placed,
        out_specs=(P(None, "row", "col"), P("row", None, None, None, "col"), P(), P(), P()),
        check_vma=False,
    )
```

```python
import functools
import math

import jax
import jax.numpy as jnp
import ml_dtypes
import numpy as np
from jax import lax
from jax.experimental import pallas as pl
from jax.experimental.pallas import tpu as pltpu
from jax.sharding import PartitionSpec as P

TWO_PI = 2.0 * math.pi
HIGH = lax.Precision.HIGHEST
HALF_FILL = 8
VMEM_BYTES = 56 * 1024 * 1024


def angle_pair(products, period):
    angles = (products % period).astype(np.float32) * np.float32(TWO_PI / period)
    return (np.cos(angles).astype(ml_dtypes.bfloat16), np.sin(angles).astype(ml_dtypes.bfloat16))


def tables(n_row, n_col, ky_dev, rows_dev, cols_dev, kx_all):
    modes, nx, ny = (ky_dev * n_row, rows_dev * n_row, cols_dev * n_col)
    cosine, sine = angle_pair(np.arange(modes)[:, None] * np.arange(ny)[None, :], ny)
    ty = np.stack([cosine.reshape(n_row, ky_dev, ny), -sine.reshape(n_row, ky_dev, ny)], axis=1)
    ty = ty.reshape(2 * modes, n_col, cols_dev).transpose(1, 0, 2)
    ids = np.arange(kx_all)
    freqs = np.where(ids < modes, ids, ids - 2 * modes) % nx
    cosine, sine = angle_pair(freqs[:, None] * np.arange(nx)[None, :], nx)
    return np.ascontiguousarray(ty), np.concatenate([cosine, sine], axis=0)


NT = (((1,), (1,)), ((), ()))
NN = (((1,), (0,)), ((), ()))
TN = (((0,), (0,)), ((), ()))


def dot(a, b, dims):
    return lax.dot_general(a, b, dims, preferred_element_type=jnp.float32)


def push(src, dst, send_sem, recv_sem, axis, peer):
    return pltpu.make_async_remote_copy(
        src_ref=src,
        dst_ref=dst,
        send_sem=send_sem,
        recv_sem=recv_sem,
        device_id={axis: peer},
        device_id_type=pl.DeviceIdType.MESH,
    )


class Exchange:
    def __init__(self, axis, me, size, source, slots, send_sem, recv_sem, shared):
        (self.axis, self.me, self.size, self.source, self.slots) = (axis, me, size, source, slots)
        (self.send_sem, self.recv_sem, self.shared) = (send_sem, recv_sem, shared)

    def peer(self, step):
        return (self.me + step) & (self.size - 1)

    def copy(self, step, src, dst, peer):
        recv_sem = self.recv_sem if self.shared else self.recv_sem.at[step]
        return push(src, dst, self.send_sem, recv_sem, self.axis, peer)

    def start(self, step):
        peer = self.peer(step)
        self.copy(step, self.source(peer), self.slots.at[self.me], peer).start()

    def start_all(self):
        for step in range(1, self.size):
            self.start(step)

    def take(self, step):
        origin = (self.me - step) & (self.size - 1)
        self.copy(step, self.slots.at[origin], self.slots.at[origin], origin).wait_recv()
        return origin

    def every(self):
        rest = self.slots.at[pl.ds(0, self.size - 1)]
        return self.copy(1, rest, rest, self.peer(1))

    def take_all(self):
        self.every().wait_recv()

    def sent(self):
        self.every().wait_send()


def each(size, body):
    def step(index, carry):
        body(index)
        return carry

    lax.fori_loop(1, size, step, 0)


def part_swap(value, sign):
    rows = value.shape[0]
    is_real = (lax.broadcasted_iota(jnp.int32, value.shape, 0) & 4) == 0
    after = pltpu.roll(value, rows - 4, 0)
    before = pltpu.roll(value, 4, 0)
    return jnp.where(is_real, sign * after, -sign * before)


class Group:
    def __init__(self, names, refs):
        for name, ref in zip(names, refs):
            setattr(self, name, ref)


def aligned(value, to):
    return pl.multiple_of(value, to)


def pass_scratch(n_row, n_col):
    bf16, f32 = (jnp.bfloat16, jnp.float32)
    dma = pltpu.SemaphoreType.DMA
    found = dict(
        snd1=pltpu.VMEM((n_col, 256, 256), bf16),
        buf1=pltpu.VMEM((n_col, 256, 256), bf16),
        snd3=pltpu.VMEM((n_row, 16, 128), bf16),
        rcv3=pltpu.VMEM((n_row, 16, 128), bf16),
        snd5=pltpu.VMEM((2, 32, 128), bf16),
        rcv5=pltpu.VMEM((n_col, 32, 128), bf16),
        modes=pltpu.VMEM((256, 128), f32),
        flat=pltpu.VMEM((64, 128), f32),
        snd7=pltpu.VMEM((n_col, 32, 128), bf16),
        rcv7=pltpu.VMEM((n_col, 32, 128), bf16),
        snd9=pltpu.VMEM((n_row, 16, 128), bf16),
        rcv9=pltpu.VMEM((n_row, 16, 128), bf16),
        snd10=pltpu.VMEM((n_col, 256, 256), bf16),
        rcv10=pltpu.VMEM((n_col, 256, 256), bf16),
        raw=pltpu.VMEM((68 * 32, 256), bf16),
        halo=pltpu.VMEM((2, 32, 256), bf16),
        edge_out=pltpu.VMEM((2, 16, 68 * 32), bf16),
        edge_in=pltpu.VMEM((2, 16, 68 * 32), bf16),
        wide=pltpu.VMEM((68 * 96, 256), bf16),
        taps=pltpu.VMEM((256, 1024), bf16),
        own=dma,
        hs=dma((2,)),
        hr=dma((2,)),
        es=dma((2,)),
        er=dma((2,)),
    )
    for step, size in ((1, n_col), (3, n_row), (5, n_col), (7, n_col), (9, n_row), (10, n_col)):
        found["s%d" % step] = dma
        found["r%d" % step] = dma((size,)) if step in (1, 10) else dma
    return found


def common_scratch(n_row, n_col, nx, owners):
    bf16, f32 = (jnp.bfloat16, jnp.float32)
    dma = pltpu.SemaphoreType.DMA
    piece = 80 // owners
    return dict(
        vbuf=pltpu.VMEM((n_col, 256, 256), bf16),
        ty=pltpu.VMEM((n_col, 8 * n_row, 256), bf16),
        tx=pltpu.VMEM((512, nx), bf16),
        weight=pltpu.VMEM((4, 2, 32, 32, 32), bf16),
        stage=pltpu.VMEM((4096, 128), f32),
        bias=pltpu.VMEM((32, 256), f32),
        proj=pltpu.VMEM((32, 256), f32),
        bias_rows=pltpu.VMEM((256, 256), f32),
        proj_rows=pltpu.VMEM((256, 256), f32),
        cot=pltpu.VMEM((64, 256), f32),
        out=pltpu.VMEM((2048, 256), f32),
        out_s=dma,
        acc=pltpu.VMEM((8 * n_row, 256), f32),
        rows_x=pltpu.VMEM((32, nx), bf16),
        mix=pltpu.VMEM((256, 128), f32),
        packed=pltpu.VMEM((2, 32, 32, 128), f32),
        mixed_back=pltpu.VMEM((64, 128), f32),
        outer=pltpu.VMEM((960, 256), f32),
        sums=pltpu.VMEM((128, 256), f32),
        part=pltpu.VMEM((owners, piece, 128), f32),
        got_row=pltpu.VMEM((n_row, piece, 128), f32),
        sum_row=pltpu.VMEM((piece, 128), f32),
        got_col=pltpu.VMEM((n_col, piece, 128), f32),
        total=pltpu.VMEM((piece, 128), f32),
        got_all=pltpu.VMEM((owners, piece, 128), f32),
        load=dma((4,)),
        row_s=dma((owners,)),
        row_r=dma,
        col_s=dma,
        col_r=dma,
        all_s=dma,
        all_r=dma((owners,)),
    )


def step_kernel(n_row, n_col, owners, *refs):
    (v_ref, cot_ref, taps_ref, bias_ref, proj_ref, w_hbm, ty_hbm, tx_hbm, out_ref, modes_ref, small_ref, *rest) = refs
    nx = 64 * n_row
    names = list(pass_scratch(n_row, n_col))
    first = Group(names, rest[: len(names)])
    second = Group(names, rest[len(names) : 2 * len(names)])
    g = Group(list(common_scratch(n_row, n_col, nx, owners)), rest[2 * len(names) :])
    row_at = lax.axis_index("row")
    col_at = lax.axis_index("col")
    pairs = n_row // 2
    scale = 1.0 / math.sqrt((64 * n_row) * (256 * n_col))
    bf16, f32 = (jnp.bfloat16, jnp.float32)
    pending = []

    loads = [
        pltpu.make_async_copy(v_ref, g.vbuf, g.load.at[0]),
        pltpu.make_async_copy(ty_hbm, g.ty, g.load.at[1]),
        pltpu.make_async_copy(tx_hbm, g.tx, g.load.at[2]),
        pltpu.make_async_copy(w_hbm, g.weight, g.load.at[3]),
    ]
    for load in loads:
        load.start()
    barrier = pltpu.get_barrier_semaphore()
    for axis, me, size in (("row", row_at, n_row), ("col", col_at, n_col)):
        for d in range(1, size):
            pl.semaphore_signal(
                barrier, inc=1, device_id={axis: (me + d) & (size - 1)}, device_id_type=pl.DeviceIdType.MESH
            )
    pl.semaphore_wait(barrier, n_col - 1 + n_row - 1)

    def loop(size, body):
        def step(index, carry):
            body(index)
            return carry

        lax.fori_loop(0, size, step, 0)

    def send_halo_rows(p):
        up = lax.rem(row_at + n_row - 1, n_row)
        down = lax.rem(row_at + 1, n_row)
        copies = [
            push(p.raw.at[pl.ds(32, 32)], p.halo.at[1], p.hs.at[0], p.hr.at[0], "row", up),
            push(p.raw.at[pl.ds(64 * 32, 32)], p.halo.at[0], p.hs.at[1], p.hr.at[1], "row", down),
        ]
        for copy in copies:
            copy.start()
            pending.append(copy.wait_send)
        return copies

    def widen(p, row_copies):
        for copy in row_copies:
            copy.wait_recv()
        above = jnp.where(row_at > 0, 1.0, 0.0)
        below = jnp.where(row_at < n_row - 1, 1.0, 0.0)
        p.raw[0:32] = (p.halo[0].astype(f32) * above).astype(bf16)
        p.raw[65 * 32 : 66 * 32] = (p.halo[1].astype(f32) * below).astype(bf16)
        p.raw[66 * 32 : 68 * 32] = jnp.zeros((64, 256), bf16)
        row = lax.broadcasted_iota(jnp.int32, (32, 256), 0)
        lane = lax.broadcasted_iota(jnp.int32, (32, 256), 1)
        pick = ((row == 0) & (lane == 0)) | ((row == 16) & (lane == 255))
        edges = dot(jnp.where(pick, 1.0, 0.0).astype(bf16), p.raw[...], NT)
        p.edge_out[0] = edges[0:16].astype(bf16)
        p.edge_out[1] = edges[16:32].astype(bf16)
        left = lax.rem(col_at + n_col - 1, n_col)
        right = lax.rem(col_at + 1, n_col)
        copies = [
            push(p.edge_out.at[0], p.edge_in.at[1], p.es.at[0], p.er.at[0], "col", left),
            push(p.edge_out.at[1], p.edge_in.at[0], p.es.at[1], p.er.at[1], "col", right),
        ]
        for copy in copies:
            copy.start()
            pending.append(copy.wait_send)
        return copies

    def fill_wide(p, start, stop):
        row = lax.broadcasted_iota(jnp.int32, (16, 128), 0)
        lane = lax.broadcasted_iota(jnp.int32, (16, 128), 1)
        put_left = jnp.where((row == 0) & (lane == 0) & (col_at > 0), 1.0, 0.0).astype(bf16)
        put_right = jnp.where((row == 0) & (lane == 127) & (col_at < n_col - 1), 1.0, 0.0).astype(bf16)
        lanes = lax.broadcasted_iota(jnp.int32, (128, 128), 1)

        def chunk(q):
            here = p.raw[pl.ds(aligned(q * 128, 128), 128), :].astype(f32)
            from_left = dot(p.edge_in[0, :, pl.ds(aligned(q * 128, 128), 128)], put_left, TN)
            from_right = dot(p.edge_in[1, :, pl.ds(aligned(q * 128, 128), 128)], put_right, TN)
            before = pltpu.roll(here, 1, 1)
            after = pltpu.roll(here, 255, 1)
            before = jnp.concatenate([jnp.where(lanes == 0, from_left, before[:, :128]), before[:, 128:]], axis=1)
            after = jnp.concatenate([after[:, :128], jnp.where(lanes == 127, from_right, after[:, 128:])], axis=1)
            for x in range(4):
                for b, value in enumerate((before, here, after)):
                    base = aligned(q * 384 + 96 * x + 32 * b, 32)
                    p.wide[pl.ds(base, 32), :] = value[32 * x : 32 * x + 32].astype(bf16)

        loop(stop - start, lambda q: chunk(q + start))

    def spread_taps(p, turned):
        row = lax.broadcasted_iota(jnp.int32, (32, 1024), 0)
        lane = lax.broadcasted_iota(jnp.int32, (32, 1024), 1)
        padded = jnp.zeros((32, 1024), f32)
        for m in range(9):
            source = 8 - m if turned else m
            spot = jnp.where(lane == row + 32 * m, 1.0, 0.0).astype(bf16)
            padded = padded + dot(taps_ref[32 * source : 32 * source + 32, :], spot, NN if turned else TN)
        for x in range(8):
            p.taps[32 * x : 32 * x + 32, :] = (pltpu.roll(padded, 96 * x, 1) if x else padded).astype(bf16)

    def convolve(p):
        def block(t):
            rows = p.wide[pl.ds(aligned(t * 768, 16), 1024), :]
            result = dot(p.taps[...], rows, NN)
            for x in range(8):
                put_grid_row(8 * t + x, result[32 * x : 32 * x + 32])

        loop(8, block)

    def to_modes(p, source, started, cover, cover_rows):
        own = pltpu.make_async_copy(source(col_at), p.buf1.at[col_at], p.own)
        own.start()
        fields = Exchange("col", col_at, n_col, source, p.buf1, p.s1, p.r1, False)
        if not started:
            fields.start_all()
        pending.append(fields.sent)
        cover()
        own.wait()
        g.acc[...] = dot(g.ty[col_at], p.buf1[col_at], NT)

        def add_block(d):
            origin = fields.take(d)
            g.acc[...] += dot(g.ty[origin], p.buf1[origin], NT)

        each(n_col, add_block)
        whole = g.acc[...]
        upper = whole[:, :128].reshape(n_row, 8, 128)
        lower = whole[:, 128:].reshape(n_row, 8, 128)
        p.snd3[...] = jnp.concatenate([upper, lower], axis=1).astype(bf16)
        rows = Exchange("row", row_at, n_row, lambda i: p.snd3.at[i], p.rcv3, p.s3, p.r3, True)
        rows.start_all()
        pending.append(rows.sent)
        p.rcv3[row_at] = p.snd3[row_at]
        cover_rows()
        rows.take_all()
        for s in range(pairs):
            one = p.rcv3[2 * s].astype(f32)
            two = p.rcv3[2 * s + 1].astype(f32)
            even = jnp.where(low, one, pltpu.roll(two, 64, 1))
            odd = jnp.where(low, pltpu.roll(one, 64, 1), two)
            g.rows_x[0:16, 128 * s : 128 * s + 128] = even.astype(bf16)
            g.rows_x[16:32, 128 * s : 128 * s + 128] = odd.astype(bf16)
        both = dot(g.rows_x[...], g.tx[...], NT)
        coeffs = (both[:, :256] + part_swap(both[:, 256:], 1.0)) * scale
        coeffs = jnp.concatenate([coeffs[0:8], coeffs[16:24], coeffs[8:16], coeffs[24:32]], axis=0)
        p.snd5[0] = coeffs[:, :128].astype(bf16)
        p.snd5[1] = coeffs[:, 128:].astype(bf16)
        parts = Exchange("col", col_at, n_col, lambda i: p.snd5.at[i // 4], p.rcv5, p.s5, p.r5, True)
        parts.start_all()
        pending.append(parts.sent)
        p.rcv5[col_at] = p.snd5[col_at // 4]
        parts.take_all()
        for i in range(n_col):
            p.modes[32 * i : 32 * i + 32] = pltpu.roll(p.rcv5[i].astype(f32), back_shift, 1)

    def to_grid(p, cover_rows, cover_cells, use):
        for i in range(n_col):
            for odd_channel in range(2):
                upper = g.mix[pl.ds(4 * i + odd_channel, 8, stride=32), :]
                lower = g.mix[pl.ds(4 * i + 2 + odd_channel, 8, stride=32), :]
                p.snd7[i, 16 * odd_channel : 16 * odd_channel + 16] = jnp.concatenate(
                    [upper, lower], axis=0
                ).astype(bf16)
        parts = Exchange("col", col_at, n_col, lambda i: p.snd7.at[i], p.rcv7, p.s7, p.r7, True)
        parts.start_all()
        pending.append(parts.sent)
        p.rcv7[col_at] = p.snd7[col_at]
        parts.take_all()
        halves = [sum(p.rcv7[4 * h + q].astype(f32) for q in range(4)) for h in range(2)]
        mixed = jnp.concatenate(halves, axis=1)
        swapped = part_swap(mixed, -1.0)
        operand = jnp.concatenate([mixed, swapped], axis=1).astype(bf16)
        by_rows = dot(operand, g.tx[...], NN)
        for s in range(pairs):
            even = by_rows[0:16, 128 * s : 128 * s + 128]
            odd = by_rows[16:32, 128 * s : 128 * s + 128]
            p.snd9[2 * s] = jnp.where(low, even, pltpu.roll(odd, 64, 1)).astype(bf16)
            p.snd9[2 * s + 1] = jnp.where(low, pltpu.roll(even, 64, 1), odd).astype(bf16)
        rows = Exchange("row", row_at, n_row, lambda i: p.snd9.at[i], p.rcv9, p.s9, p.r9, True)
        rows.start_all()
        pending.append(rows.sent)
        p.rcv9[row_at] = p.snd9[row_at]
        cover_rows()
        rows.take_all()
        got = p.rcv9[...].astype(f32)
        own_rows = jnp.concatenate(
            [got[:, :8].reshape(8 * n_row, 128), got[:, 8:].reshape(8 * n_row, 128)], axis=1
        )
        lhs = jnp.transpose(own_rows).astype(bf16)
        cells = Exchange("col", col_at, n_col, lambda i: p.snd10.at[i], p.rcv10, p.s10, p.r10, False)

        def make_cells(d):
            peer = cells.peer(d)
            p.snd10[peer] = dot(lhs, g.ty[peer], NN).astype(bf16)
            cells.start(d)

        each(n_col, make_cells)
        pending.append(cells.sent)
        cover_cells()
        use(col_at, dot(lhs, g.ty[col_at], NN), 0)

        def take(d):
            origin = cells.take(d)
            use(origin, p.rcv10[origin].astype(f32), d)

        each(n_col, take)

    def first_fill(p):
        for copy in p.edge_copies:
            copy.wait_recv()
        fill_wide(p, 0, HALF_FILL)

    def rest_of_conv(p):
        fill_wide(p, HALF_FILL, 17)
        convolve(p)

    def regroup(p):
        def one(x):
            p.raw[pl.ds(aligned(x * 32 + 32, 32), 32), :] = grid_row(x).astype(bf16)

        one(0)
        one(63)
        p.row_copies = send_halo_rows(p)
        loop(62, lambda x: one(x + 1))

    def widen_now(p):
        p.edge_copies = widen(p, p.row_copies)

    def place(slot, value):
        for half in range(2):
            g.stage[pl.ds(aligned(half * 2048 + slot * 256, 256), 256), :] = value[:, 128 * half : 128 * half + 128]

    def placed(slot):
        return jnp.concatenate(
            [g.stage[pl.ds(aligned(half * 2048 + slot * 256, 256), 256), :] for half in range(2)], axis=1
        )

    def grid_row(x):
        return jnp.concatenate([g.stage[pl.ds(2048 * half + x, 32, stride=64), :] for half in range(2)], axis=1)

    def put_grid_row(x, value):
        for half in range(2):
            g.stage[pl.ds(2048 * half + x, 32, stride=64), :] = value[:, 128 * half : 128 * half + 128]

    low = lax.broadcasted_iota(jnp.int32, (16, 128), 1) < 64
    quarter = lax.rem(col_at, 4) * 32
    back_shift = lax.rem(128 - quarter, 128)

    def flatten_modes(p):
        for part in range(2):
            p.flat[32 * part : 32 * part + 32] = jnp.concatenate(
                [p.modes[pl.ds(4 * part + kl, 32, stride=8), :][:, :32] for kl in range(4)], axis=1
            )

    def pack_weight(i):
        for part in range(2):
            g.packed[part, i] = jnp.concatenate([g.weight[kl, part, i].astype(f32) for kl in range(4)], axis=1)

    def spread_mix(parts):
        lane = lax.broadcasted_iota(jnp.int32, (32, 128), 1)
        mine = (lane >= quarter) & (lane < quarter + 32)
        for part, value in enumerate(parts):
            for kl in range(4):
                moved = pltpu.roll(value, (quarter + 128 - 32 * kl) & 127, 1)
                at = 128 * part + 32 * kl
                g.mix[at : at + 32, :] = jnp.where(mine, moved, 0.0)

    def cover_field():
        loads[0].wait()
        for i in range(n_col):
            place(i, g.vbuf[i].astype(f32))

        regroup(first)
        g.cot[...] = cot_ref[...].astype(f32)
        spread_taps(first, False)
        g.bias[...] = column(bias_ref)
        g.proj[...] = column(proj_ref)
        loads[3].wait()
        loop(32, pack_weight)
        loads[1].wait()
        loads[2].wait()

    def column(ref):
        diagonal = lax.broadcasted_iota(jnp.int32, (32, 32), 0) == lax.broadcasted_iota(jnp.int32, (32, 32), 1)
        value = jnp.sum(jnp.where(diagonal, jnp.broadcast_to(ref[...], (32, 32)), 0.0), axis=1, keepdims=True)
        return jnp.broadcast_to(value, (32, 256))

    to_modes(first, lambda i: v_ref.at[i], False, cover_field, lambda: widen_now(first))
    flatten_modes(first)

    def add_channel(i, sums):
        real, imag = sums
        s_re = first.flat[pl.ds(i, 1), :]
        s_im = first.flat[pl.ds(32 + i, 1), :]
        w_re = g.packed[0, i]
        w_im = g.packed[1, i]
        return (real + (w_re * s_re - w_im * s_im), imag + (w_re * s_im + w_im * s_re))

    zero = jnp.zeros((32, 128), f32)
    real, imag = lax.fori_loop(0, 32, add_channel, (zero, zero))
    frequency = row_at * 4 + lax.broadcasted_iota(jnp.int32, (32, 128), 1) // 32
    factor = jnp.where(frequency == 0, 1.0, 2.0) * scale
    spread_mix([value.astype(bf16).astype(f32) * factor for value in (real, imag)])

    back = Exchange("col", col_at, n_col, lambda i: second.snd1.at[i], second.buf1, second.s1, second.r1, False)

    def activate(slot, cells, d):
        conv = placed(slot)
        rounded = []
        for ch in range(4):
            channel = slot * 4 + ch
            rows = slice(64 * ch, 64 * ch + 64)
            bias = jnp.broadcast_to(g.bias[pl.ds(channel, 1), :], (64, 256))
            proj = jnp.broadcast_to(g.proj[pl.ds(channel, 1), :], (64, 256))
            pre = conv[rows] + cells[rows] + bias
            cdf = 0.5 * (1.0 + lax.erf(pre * math.sqrt(0.5)))
            pdf = jnp.exp(-0.5 * pre * pre) * (1.0 / math.sqrt(TWO_PI))
            grad = (proj * g.cot[...]) * (cdf + pre * pdf)
            rounded.append(grad.astype(bf16))
            second.snd1[slot, 64 * ch : 64 * ch + 64] = rounded[ch]
            at = pl.ds(aligned(channel * 8, 8), 8)
            g.bias_rows[at, :] = jnp.sum(grad.reshape(8, 8, 256), axis=0)
            g.proj_rows[at, :] = jnp.sum(((pre * cdf) * g.cot[...]).reshape(8, 8, 256), axis=0)
        if not isinstance(d, int):
            back.start(n_col - d)
        place(slot, jnp.concatenate(rounded, axis=0).astype(f32))

    to_grid(first, lambda: first_fill(first), lambda: rest_of_conv(first), activate)

    piece = 80 // owners

    def cover_grad():
        regroup(second)
        of_channel = (lax.broadcasted_iota(jnp.int32, (32, 256), 1) // 8) == lax.broadcasted_iota(
            jnp.int32, (32, 256), 0
        )
        gather = jnp.where(of_channel, 1.0, 0.0)
        for at, rows in ((0, g.bias_rows), (32, g.proj_rows)):
            g.sums[at : at + 32] = lax.dot_general(
                gather, rows[...], NN, precision=HIGH, preferred_element_type=f32
            )
        g.sums[64:128] = jnp.zeros((64, 256), f32)
        g.outer[...] = jnp.zeros_like(g.outer)

        def block(t):
            rows = first.wide[pl.ds(aligned(t * 768, 16), 960), :]
            grads = second.raw[pl.ds(aligned(t * 256 + 32, 32), 256), :]
            g.outer[...] += dot(rows, grads, NT)

        loop(8, block)
        lane = lax.broadcasted_iota(jnp.int32, (96, 128), 1)
        taps = []
        for a in range(3):
            total = jnp.zeros((96, 128), f32)
            for x in range(8):
                here = g.outer[96 * (x + a) : 96 * (x + a) + 96, 128 * (x // 4) : 128 * (x // 4) + 128]
                total = total + (pltpu.roll(here, 128 - 32 * (x % 4), 1) if x % 4 else here)
            taps.append(jnp.where(lane < 32, total, 0.0))
        taps = jnp.concatenate(taps, axis=0)
        packed = taps[0:72]
        for q in range(1, 4):
            packed = packed + pltpu.roll(taps[72 * q : 72 * q + 72], 32 * q, 1)
        lanes_sum = lax.dot_general(
            jnp.ones((8, 256), f32), g.sums[...], NT, precision=HIGH, preferred_element_type=f32
        )
        g.part[...] = (jnp.concatenate([packed, lanes_sum], axis=0) * scale).reshape(owners, piece, 128)
        for t in range(owners):

            @pl.when(row_at != t)
            def _():
                push(g.part.at[t], g.got_row.at[row_at], g.row_s.at[t], g.row_r, "row", t).start()

        spread_taps(second, True)

    def sum_rows():
        @pl.when(row_at < owners)
        def _():
            g.got_row[row_at] = g.part[row_at]
            Exchange("row", row_at, n_row, None, g.got_row, g.row_s.at[0], g.row_r, True).take_all()
            g.sum_row[...] = jnp.sum(g.got_row[...], axis=0)
            g.got_col[col_at] = g.sum_row[...]
            Exchange("col", col_at, n_col, lambda i: g.sum_row, g.got_col, g.col_s, g.col_r, True).start_all()

    def sum_cols():
        @pl.when(row_at < owners)
        def _():
            sums = Exchange("col", col_at, n_col, lambda i: g.sum_row, g.got_col, g.col_s, g.col_r, True)
            sums.take_all()
            sums.sent()
            g.total[...] = jnp.sum(g.got_col[...], axis=0)
            g.got_all[row_at] = g.total[...]

            def send(d):
                peer = (row_at + d) & (n_row - 1)
                push(g.total, g.got_all.at[row_at], g.all_s, g.all_r.at[row_at], "row", peer).start()

            each(n_row, send)

    def cover_rows_back():
        widen_now(second)
        sum_rows()

    def cover_rows_out():
        first_fill(second)
        sum_cols()

    def write_out(slot, cells, d):
        at = pl.ds(aligned(slot * 256, 256), 256)
        g.out[at, :] = placed(slot) + cells
        pltpu.make_async_copy(g.out.at[at], out_ref.at[at], g.out_s).start()

    to_modes(second, lambda i: second.snd1.at[i], True, cover_grad, cover_rows_back)
    own_mode = lax.broadcasted_iota(jnp.int32, (256, 128), 0) & 3
    second.modes[...] = second.modes[...] * jnp.where(row_at * 4 + own_mode == 0, 1.0, 2.0)
    flatten_modes(second)
    g_re = second.flat[0:32]
    g_im = second.flat[32:64]

    def one_channel(i):
        w_re = g.packed[0, i]
        w_im = g.packed[1, i]
        g.mixed_back[pl.ds(i, 1), :] = jnp.sum(w_re * g_re + w_im * g_im, axis=0, keepdims=True)
        g.mixed_back[pl.ds(32 + i, 1), :] = jnp.sum(w_re * g_im - w_im * g_re, axis=0, keepdims=True)

    loop(32, one_channel)
    spread_mix([g.mixed_back[32 * part : 32 * part + 32].astype(bf16).astype(f32) * scale for part in range(2)])
    to_grid(second, cover_rows_out, lambda: rest_of_conv(second), write_out)

    modes_ref[0] = first.modes[...]
    modes_ref[1] = second.modes[...]
    for t in range(owners):

        @pl.when(row_at != t)
        def _():
            arrived = push(g.part.at[t], g.got_all.at[t], g.row_s.at[t], g.all_r.at[t], "row", t)
            arrived.wait_recv()
            arrived.wait_send()

    @pl.when(row_at < owners)
    def _():
        Exchange("row", row_at, n_row, None, g.got_row, g.all_s, g.row_r, True).sent()

    small_ref[...] = g.got_all[...].reshape(80, 128)
    for wait in pending:
        wait()
    pltpu.make_async_copy(g.out, out_ref, g.out_s).wait()


def outputs_kernel(cells_ref, modes_ref, small_ref, out_ref, gspec_ref, conv_ref, bias_ref, proj_ref, weight, cells, sems):
    copies = []
    loads = []
    parts = [pl.ds(512 * q, 512) for q in range(4)]
    for q, at in enumerate(parts):
        loads.append(pltpu.make_async_copy(cells_ref.at[at], cells.at[at], sems.at[q]))
        loads[q].start()
    for kl in range(4):
        g_re = modes_ref[pl.ds(256 + kl, 32, stride=8), :][:, :32]
        g_im = modes_ref[pl.ds(260 + kl, 32, stride=8), :][:, :32]
        for i in range(32):
            s_re = modes_ref[8 * i + kl : 8 * i + kl + 1, :][:, :32]
            s_im = modes_ref[8 * i + 4 + kl : 8 * i + 5 + kl, :][:, :32]
            weight[kl, 0, i] = g_re * s_re + g_im * s_im
            weight[kl, 1, i] = g_im * s_re - g_re * s_im
        copies.append(pltpu.make_async_copy(weight.at[kl], gspec_ref.at[kl], sems.at[4 + kl]))
        copies[-1].start()
        loads[kl].wait()
        copies.append(pltpu.make_async_copy(cells.at[parts[kl]], out_ref.at[parts[kl]], sems.at[8 + kl]))
        copies[-1].start()
    for q in range(4):
        rows = small_ref[0:72]
        conv_ref[72 * q : 72 * q + 72] = (pltpu.roll(rows, 128 - 32 * q, 1) if q else rows)[:, :32]
    rows = small_ref[72:80]
    bias_ref[...] = rows[0:1, :32]
    proj_ref[...] = pltpu.roll(rows, 96, 1)[0:1, :32]
    for copy in copies:
        copy.wait()


def per_device(n_row, n_col, ocean_field, cotangent, conv_weight, conv_bias, projection, mode_weight):
    chans, rows_dev, cols_dev = ocean_field.shape
    ky_dev = mode_weight.shape[0]
    kx_all = mode_weight.shape[4] * n_col
    owners = min(10, n_row)
    ty, tx = (jnp.asarray(t) for t in tables(n_row, n_col, ky_dev, rows_dev, cols_dev, kx_all))
    vmem = pl.BlockSpec(memory_space=pltpu.VMEM)
    hbm = pl.BlockSpec(memory_space=pl.ANY)
    one = pass_scratch(n_row, n_col)
    scratch = list(one.values()) * 2 + list(common_scratch(n_row, n_col, rows_dev * n_row, owners).values())
    cells, modes, small = pl.pallas_call(
        functools.partial(step_kernel, n_row, n_col, owners),
        out_shape=[
            jax.ShapeDtypeStruct((chans * rows_dev, cols_dev), jnp.float32),
            jax.ShapeDtypeStruct((2, 256, 128), jnp.float32),
            jax.ShapeDtypeStruct((80, 128), jnp.float32),
        ],
        in_specs=[hbm, vmem, vmem, vmem, vmem, hbm, hbm, hbm],
        out_specs=[hbm, vmem, vmem],
        scratch_shapes=scratch,
        compiler_params=pltpu.CompilerParams(
            collective_id=0, has_side_effects=True, vmem_limit_bytes=VMEM_BYTES
        ),
        name="layer_step",
    )(
        ocean_field.reshape(n_col, 256, cols_dev),
        cotangent,
        conv_weight.reshape(9 * chans, chans),
        conv_bias.reshape(1, chans),
        projection.reshape(1, chans),
        mode_weight,
        ty,
        tx,
    )
    grad_input, grad_spec, grad_conv, grad_bias, grad_proj = pl.pallas_call(
        outputs_kernel,
        out_shape=[
            jax.ShapeDtypeStruct((chans * rows_dev, cols_dev), jnp.float32),
            jax.ShapeDtypeStruct(mode_weight.shape, jnp.float32),
            jax.ShapeDtypeStruct((9 * chans, chans), jnp.float32),
            jax.ShapeDtypeStruct((1, chans), jnp.float32),
            jax.ShapeDtypeStruct((1, chans), jnp.float32),
        ],
        in_specs=[hbm, vmem, vmem],
        out_specs=[hbm, hbm, vmem, vmem, vmem],
        scratch_shapes=[
            pltpu.VMEM(mode_weight.shape, jnp.float32),
            pltpu.VMEM((chans * rows_dev, cols_dev), jnp.float32),
            pltpu.SemaphoreType.DMA((12,)),
        ],
        compiler_params=pltpu.CompilerParams(vmem_limit_bytes=VMEM_BYTES),
        name="layer_outputs",
    )(cells, modes.reshape(512, 128), small)
    return (
        grad_input.reshape(ocean_field.shape),
        grad_spec,
        grad_conv.reshape(conv_weight.shape),
        grad_bias.reshape(chans),
        grad_proj.reshape(chans),
    )


def solution(mesh):
    placed = (
        P(None, "row", "col"),
        P("row", "col"),
        P(),
        P(),
        P(),
        P("row", None, None, None, "col"),
    )
    return jax.shard_map(
        functools.partial(per_device, mesh.shape["row"], mesh.shape["col"]),
        mesh=mesh,
        in_specs=placed,
        out_specs=(P(None, "row", "col"), P("row", None, None, None, "col"), P(), P(), P()),
        check_vma=False,
    )
```

```python
import functools
import math

import jax
import jax.numpy as jnp
import ml_dtypes
import numpy as np
from jax import lax
from jax.experimental import pallas as pl
from jax.experimental.pallas import tpu as pltpu
from jax.sharding import PartitionSpec as P

TWO_PI = 2.0 * math.pi
HIGH = lax.Precision.HIGHEST
HALF_FILL = 8
VMEM_BYTES = 56 * 1024 * 1024


def angle_pair(products, period):
    angles = (products % period).astype(np.float32) * np.float32(TWO_PI / period)
    return (np.cos(angles).astype(ml_dtypes.bfloat16), np.sin(angles).astype(ml_dtypes.bfloat16))


def tables(n_row, n_col, ky_dev, rows_dev, cols_dev, kx_all):
    modes, nx, ny = (ky_dev * n_row, rows_dev * n_row, cols_dev * n_col)
    cosine, sine = angle_pair(np.arange(modes)[:, None] * np.arange(ny)[None, :], ny)
    ty = np.stack([cosine.reshape(n_row, ky_dev, ny), -sine.reshape(n_row, ky_dev, ny)], axis=1)
    ty = ty.reshape(2 * modes, n_col, cols_dev).transpose(1, 0, 2)
    ids = np.arange(kx_all)
    freqs = np.where(ids < modes, ids, ids - 2 * modes) % nx
    cosine, sine = angle_pair(freqs[:, None] * np.arange(nx)[None, :], nx)
    return np.ascontiguousarray(ty), np.concatenate([cosine, sine], axis=0)


NT = (((1,), (1,)), ((), ()))
NN = (((1,), (0,)), ((), ()))
TN = (((0,), (0,)), ((), ()))


def dot(a, b, dims):
    return lax.dot_general(a, b, dims, preferred_element_type=jnp.float32)


def push(src, dst, send_sem, recv_sem, axis, peer):
    return pltpu.make_async_remote_copy(
        src_ref=src,
        dst_ref=dst,
        send_sem=send_sem,
        recv_sem=recv_sem,
        device_id={axis: peer},
        device_id_type=pl.DeviceIdType.MESH,
    )


class Exchange:
    def __init__(self, axis, me, size, source, slots, send_sem, recv_sem, shared):
        (self.axis, self.me, self.size, self.source, self.slots) = (axis, me, size, source, slots)
        (self.send_sem, self.recv_sem, self.shared) = (send_sem, recv_sem, shared)

    def peer(self, step):
        return (self.me + step) & (self.size - 1)

    def copy(self, step, src, dst, peer):
        recv_sem = self.recv_sem if self.shared else self.recv_sem.at[step]
        return push(src, dst, self.send_sem, recv_sem, self.axis, peer)

    def start(self, step):
        peer = self.peer(step)
        self.copy(step, self.source(peer), self.slots.at[self.me], peer).start()

    def start_all(self):
        each(self.size, self.start)

    def take(self, step):
        origin = (self.me - step) & (self.size - 1)
        self.copy(step, self.slots.at[origin], self.slots.at[origin], origin).wait_recv()
        return origin

    def every(self):
        rest = self.slots.at[pl.ds(0, self.size - 1)]
        return self.copy(1, rest, rest, self.peer(1))

    def take_all(self):
        self.every().wait_recv()

    def sent(self):
        self.every().wait_send()


def each(size, body):
    def step(index, carry):
        body(index)
        return carry

    lax.fori_loop(1, size, step, 0)


def part_swap(value, sign):
    rows = value.shape[0]
    is_real = (lax.broadcasted_iota(jnp.int32, value.shape, 0) & 4) == 0
    after = pltpu.roll(value, rows - 4, 0)
    before = pltpu.roll(value, 4, 0)
    return jnp.where(is_real, sign * after, -sign * before)


class Group:
    def __init__(self, names, refs):
        for name, ref in zip(names, refs):
            setattr(self, name, ref)


def aligned(value, to):
    return pl.multiple_of(value, to)


def pass_scratch(n_row, n_col):
    bf16, f32 = (jnp.bfloat16, jnp.float32)
    dma = pltpu.SemaphoreType.DMA
    found = dict(
        snd1=pltpu.VMEM((n_col, 256, 256), bf16),
        buf1=pltpu.VMEM((n_col, 256, 256), bf16),
        snd3=pltpu.VMEM((n_row, 16, 128), bf16),
        rcv3=pltpu.VMEM((n_row, 16, 128), bf16),
        snd5=pltpu.VMEM((2, 32, 128), bf16),
        rcv5=pltpu.VMEM((n_col, 32, 128), bf16),
        modes=pltpu.VMEM((256, 128), f32),
        flat=pltpu.VMEM((64, 128), f32),
        snd7=pltpu.VMEM((n_col, 32, 128), bf16),
        rcv7=pltpu.VMEM((n_col, 32, 128), bf16),
        snd9=pltpu.VMEM((n_row, 16, 128), bf16),
        rcv9=pltpu.VMEM((n_row, 16, 128), bf16),
        rcv10=pltpu.VMEM((n_col, 256, 256), bf16),
        raw=pltpu.VMEM((68 * 32, 256), bf16),
        halo=pltpu.VMEM((2, 32, 256), bf16),
        edge_out=pltpu.VMEM((2, 16, 68 * 32), bf16),
        edge_in=pltpu.VMEM((2, 16, 68 * 32), bf16),
        wide=pltpu.VMEM((68 * 96, 256), bf16),
        taps=pltpu.VMEM((256, 1024), bf16),
        own=dma,
        hs=dma((2,)),
        hr=dma((2,)),
        es=dma((2,)),
        er=dma((2,)),
    )
    for step, size in ((1, n_col), (3, n_row), (5, n_col), (7, n_col), (9, n_row), (10, n_col)):
        found["s%d" % step] = dma((9,)) if step == 10 else dma
        found["r%d" % step] = dma((9,)) if step == 10 else dma((size,)) if step == 1 else dma
    return found


def common_scratch(n_row, n_col, nx, owners):
    bf16, f32 = (jnp.bfloat16, jnp.float32)
    dma = pltpu.SemaphoreType.DMA
    piece = 80 // owners
    return dict(
        vbuf=pltpu.VMEM((n_col, 256, 256), bf16),
        ty=pltpu.VMEM((n_col, 8 * n_row, 256), bf16),
        tx=pltpu.VMEM((512, nx), bf16),
        weight=pltpu.VMEM((4, 2, 32, 32, 32), bf16),
        stage=pltpu.VMEM((4096, 128), f32),
        bias=pltpu.VMEM((32, 256), f32),
        proj=pltpu.VMEM((32, 256), f32),
        bias_rows=pltpu.VMEM((256, 256), f32),
        proj_rows=pltpu.VMEM((256, 256), f32),
        cot=pltpu.VMEM((64, 256), f32),
        out=pltpu.VMEM((2048, 256), f32),
        out_s=dma,
        acc=pltpu.VMEM((8 * n_row, 256), f32),
        rows_x=pltpu.VMEM((32, nx), bf16),
        mix=pltpu.VMEM((256, 128), f32),
        packed=pltpu.VMEM((2, 32, 32, 128), f32),
        mixed_back=pltpu.VMEM((64, 128), f32),
        outer=pltpu.VMEM((960, 256), f32),
        sums=pltpu.VMEM((128, 256), f32),
        part=pltpu.VMEM((owners, piece, 128), f32),
        got_row=pltpu.VMEM((n_row, piece, 128), f32),
        sum_row=pltpu.VMEM((piece, 128), f32),
        got_col=pltpu.VMEM((n_col, piece, 128), f32),
        total=pltpu.VMEM((piece, 128), f32),
        got_all=pltpu.VMEM((owners, piece, 128), f32),
        load=dma((4,)),
        row_s=dma((owners,)),
        row_r=dma,
        col_s=dma,
        col_r=dma,
        all_s=dma,
        all_r=dma((owners,)),
    )


def step_kernel(n_row, n_col, owners, *refs):
    (v_ref, cot_ref, taps_ref, bias_ref, proj_ref, w_hbm, ty_hbm, tx_hbm, out_ref, modes_ref, small_ref, *rest) = refs
    nx = 64 * n_row
    names = list(pass_scratch(n_row, n_col))
    first = Group(names, rest[: len(names)])
    second = Group(names, rest[len(names) : 2 * len(names)])
    g = Group(list(common_scratch(n_row, n_col, nx, owners)), rest[2 * len(names) :])
    row_at = lax.axis_index("row")
    col_at = lax.axis_index("col")
    pairs = n_row // 2
    scale = 1.0 / math.sqrt((64 * n_row) * (256 * n_col))
    bf16, f32 = (jnp.bfloat16, jnp.float32)
    pending = []

    loads = [
        pltpu.make_async_copy(v_ref, g.vbuf, g.load.at[0]),
        pltpu.make_async_copy(ty_hbm, g.ty, g.load.at[1]),
        pltpu.make_async_copy(tx_hbm, g.tx, g.load.at[2]),
        pltpu.make_async_copy(w_hbm, g.weight, g.load.at[3]),
    ]
    for load in loads:
        load.start()
    barrier = pltpu.get_barrier_semaphore()
    each(n_col, lambda d: pl.semaphore_signal(
        barrier, inc=1, device_id={"col": (col_at + d) & (n_col - 1)}, device_id_type=pl.DeviceIdType.MESH))
    each(n_row, lambda d: pl.semaphore_signal(
        barrier, inc=1, device_id={"row": (row_at + d) & (n_row - 1)}, device_id_type=pl.DeviceIdType.MESH))
    pl.semaphore_wait(barrier, n_col - 1 + n_row - 1)

    def loop(size, body):
        def step(index, carry):
            body(index)
            return carry

        lax.fori_loop(0, size, step, 0)

    def send_halo_rows(p):
        up = lax.rem(row_at + n_row - 1, n_row)
        down = lax.rem(row_at + 1, n_row)
        copies = [
            push(p.raw.at[pl.ds(32, 32)], p.halo.at[1], p.hs.at[0], p.hr.at[0], "row", up),
            push(p.raw.at[pl.ds(64 * 32, 32)], p.halo.at[0], p.hs.at[1], p.hr.at[1], "row", down),
        ]
        for copy in copies:
            copy.start()
            pending.append(copy.wait_send)
        return copies

    def widen(p, row_copies):
        for copy in row_copies:
            copy.wait_recv()
        above = jnp.where(row_at > 0, 1.0, 0.0)
        below = jnp.where(row_at < n_row - 1, 1.0, 0.0)
        p.raw[0:32] = (p.halo[0].astype(f32) * above).astype(bf16)
        p.raw[65 * 32 : 66 * 32] = (p.halo[1].astype(f32) * below).astype(bf16)
        p.raw[66 * 32 : 68 * 32] = jnp.zeros((64, 256), bf16)
        row = lax.broadcasted_iota(jnp.int32, (32, 256), 0)
        lane = lax.broadcasted_iota(jnp.int32, (32, 256), 1)
        pick = ((row == 0) & (lane == 0)) | ((row == 16) & (lane == 255))
        edges = dot(jnp.where(pick, 1.0, 0.0).astype(bf16), p.raw[...], NT)
        p.edge_out[0] = edges[0:16].astype(bf16)
        p.edge_out[1] = edges[16:32].astype(bf16)
        left = lax.rem(col_at + n_col - 1, n_col)
        right = lax.rem(col_at + 1, n_col)
        copies = [
            push(p.edge_out.at[0], p.edge_in.at[1], p.es.at[0], p.er.at[0], "col", left),
            push(p.edge_out.at[1], p.edge_in.at[0], p.es.at[1], p.er.at[1], "col", right),
        ]
        for copy in copies:
            copy.start()
            pending.append(copy.wait_send)
        return copies

    def fill_wide(p, start, stop):
        row = lax.broadcasted_iota(jnp.int32, (16, 128), 0)
        lane = lax.broadcasted_iota(jnp.int32, (16, 128), 1)
        put_left = jnp.where((row == 0) & (lane == 0) & (col_at > 0), 1.0, 0.0).astype(bf16)
        put_right = jnp.where((row == 0) & (lane == 127) & (col_at < n_col - 1), 1.0, 0.0).astype(bf16)
        lanes = lax.broadcasted_iota(jnp.int32, (128, 128), 1)

        def chunk(q):
            here = p.raw[pl.ds(aligned(q * 128, 128), 128), :].astype(f32)
            from_left = dot(p.edge_in[0, :, pl.ds(aligned(q * 128, 128), 128)], put_left, TN)
            from_right = dot(p.edge_in[1, :, pl.ds(aligned(q * 128, 128), 128)], put_right, TN)
            before = pltpu.roll(here, 1, 1)
            after = pltpu.roll(here, 255, 1)
            before = jnp.concatenate([jnp.where(lanes == 0, from_left, before[:, :128]), before[:, 128:]], axis=1)
            after = jnp.concatenate([after[:, :128], jnp.where(lanes == 127, from_right, after[:, 128:])], axis=1)
            for x in range(4):
                for b, value in enumerate((before, here, after)):
                    base = aligned(q * 384 + 96 * x + 32 * b, 32)
                    p.wide[pl.ds(base, 32), :] = value[32 * x : 32 * x + 32].astype(bf16)

        loop(stop - start, lambda q: chunk(q + start))

    def spread_taps(p, turned):
        row = lax.broadcasted_iota(jnp.int32, (32, 1024), 0)
        lane = lax.broadcasted_iota(jnp.int32, (32, 1024), 1)
        padded = jnp.zeros((32, 1024), f32)
        for m in range(9):
            source = 8 - m if turned else m
            spot = jnp.where(lane == row + 32 * m, 1.0, 0.0).astype(bf16)
            padded = padded + dot(taps_ref[32 * source : 32 * source + 32, :], spot, NN if turned else TN)
        for x in range(8):
            p.taps[32 * x : 32 * x + 32, :] = (pltpu.roll(padded, 96 * x, 1) if x else padded).astype(bf16)

    def convolve(p, start, stop):
        def block(t):
            rows = p.wide[pl.ds(aligned(t * 768, 16), 1024), :]
            result = dot(p.taps[...], rows, NN)
            for x in range(8):
                put_grid_row(8 * t + x, result[32 * x : 32 * x + 32])

        loop(stop - start, lambda t: block(t + start))

    def to_modes(p, source, started, cover, cover_rows):
        own = pltpu.make_async_copy(source(col_at), p.buf1.at[col_at], p.own)
        own.start()
        fields = Exchange("col", col_at, n_col, source, p.buf1, p.s1, p.r1, False)
        if not started:
            fields.start_all()
        pending.append(fields.sent)
        cover()
        own.wait()
        g.acc[...] = dot(g.ty[col_at], p.buf1[col_at], NT)

        def add_block(d):
            origin = fields.take(d)
            g.acc[...] += dot(g.ty[origin], p.buf1[origin], NT)

        each(n_col, add_block)
        whole = g.acc[...]
        upper = whole[:, :128].reshape(n_row, 8, 128)
        lower = whole[:, 128:].reshape(n_row, 8, 128)
        p.snd3[...] = jnp.concatenate([upper, lower], axis=1).astype(bf16)
        rows = Exchange("row", row_at, n_row, lambda i: p.snd3.at[i], p.rcv3, p.s3, p.r3, True)
        rows.start_all()
        pending.append(rows.sent)
        p.rcv3[row_at] = p.snd3[row_at]
        cover_rows()
        rows.take_all()
        for s in range(pairs):
            one = p.rcv3[2 * s].astype(f32)
            two = p.rcv3[2 * s + 1].astype(f32)
            even = jnp.where(low, one, pltpu.roll(two, 64, 1))
            odd = jnp.where(low, pltpu.roll(one, 64, 1), two)
            g.rows_x[0:16, 128 * s : 128 * s + 128] = even.astype(bf16)
            g.rows_x[16:32, 128 * s : 128 * s + 128] = odd.astype(bf16)
        both = dot(g.rows_x[...], g.tx[...], NT)
        coeffs = (both[:, :256] + part_swap(both[:, 256:], 1.0)) * scale
        coeffs = jnp.concatenate([coeffs[0:8], coeffs[16:24], coeffs[8:16], coeffs[24:32]], axis=0)
        p.snd5[0] = coeffs[:, :128].astype(bf16)
        p.snd5[1] = coeffs[:, 128:].astype(bf16)
        parts = Exchange("col", col_at, n_col, lambda i: p.snd5.at[i // 4], p.rcv5, p.s5, p.r5, True)
        parts.start_all()
        pending.append(parts.sent)
        p.rcv5[col_at] = p.snd5[col_at // 4]
        parts.take_all()
        for i in range(n_col):
            p.modes[32 * i : 32 * i + 32] = pltpu.roll(p.rcv5[i].astype(f32), back_shift, 1)

    def to_grid(p, cover_rows, cover_cells, use):
        for i in range(n_col):
            for odd_channel in range(2):
                upper = g.mix[pl.ds(4 * i + odd_channel, 8, stride=32), :]
                lower = g.mix[pl.ds(4 * i + 2 + odd_channel, 8, stride=32), :]
                p.snd7[i, 16 * odd_channel : 16 * odd_channel + 16] = jnp.concatenate(
                    [upper, lower], axis=0
                ).astype(bf16)
        parts = Exchange("col", col_at, n_col, lambda i: p.snd7.at[i], p.rcv7, p.s7, p.r7, True)
        parts.start_all()
        pending.append(parts.sent)
        p.rcv7[col_at] = p.snd7[col_at]
        parts.take_all()
        halves = [sum(p.rcv7[4 * h + q].astype(f32) for q in range(4)) for h in range(2)]
        mixed = jnp.concatenate(halves, axis=1)
        swapped = part_swap(mixed, -1.0)
        operand = jnp.concatenate([mixed, swapped], axis=1).astype(bf16)
        by_rows = dot(operand, g.tx[...], NN)
        for s in range(pairs):
            even = by_rows[0:16, 128 * s : 128 * s + 128]
            odd = by_rows[16:32, 128 * s : 128 * s + 128]
            p.snd9[2 * s] = jnp.where(low, even, pltpu.roll(odd, 64, 1)).astype(bf16)
            p.snd9[2 * s + 1] = jnp.where(low, pltpu.roll(even, 64, 1), odd).astype(bf16)
        rows = Exchange("row", row_at, n_row, lambda i: p.snd9.at[i], p.rcv9, p.s9, p.r9, True)
        rows.start_all()
        pending.append(rows.sent)
        p.rcv9[row_at] = p.snd9[row_at]
        cover_rows()
        rows.take_all()
        got = p.rcv9[...].astype(f32)
        own_rows = jnp.concatenate(
            [got[:, :8].reshape(8 * n_row, 128), got[:, 8:].reshape(8 * n_row, 128)], axis=1
        )
        lhs = jnp.transpose(own_rows).astype(bf16)
        def at(dy, dz):
            return ((((col_at >> 1) + dy) & (n_col // 2 - 1)) << 1) | ((col_at + dz) & 1)

        ahead, behind, beside, far = (at(1, 0), at(n_col // 2 - 1, 0), at(0, 1), at(2, 0))
        behind_beside, ahead_beside, far_beside = (at(n_col // 2 - 1, 1), at(1, 1), at(2, 1))

        def send(kind, block, to, rows=None):
            ref = p.rcv10.at[block] if rows is None else p.rcv10.at[block, pl.ds(128 * rows, 128)]
            copy = push(ref, ref, p.s10.at[kind], p.r10.at[kind], "col", to)
            copy.start()
            pending.append(copy.wait_send)

        def arrived(kind, block, rows=None):
            ref = p.rcv10.at[block] if rows is None else p.rcv10.at[block, pl.ds(128 * rows, 128)]
            push(ref, ref, p.s10.at[kind], p.r10.at[kind], "col", beside).wait_recv()

        def give(block):
            use(block, dot(p.rcv10[block], g.ty[col_at], NN), (col_at - block) & (n_col - 1))

        p.rcv10[col_at] = lhs
        send(0, col_at, ahead)
        send(1, col_at, behind)
        send(2, col_at, beside)
        cover_cells[0]()
        arrived(2, beside)
        send(3, beside, ahead)
        send(4, beside, behind)
        arrived(0, behind)
        send(5, behind, ahead, 0)
        arrived(1, ahead)
        send(6, ahead, behind, 1)
        cover_cells[1]()
        arrived(3, behind_beside)
        send(7, behind_beside, ahead, 0)
        arrived(4, ahead_beside)
        send(8, ahead_beside, behind, 1)
        cover_cells[2]()
        use(col_at, dot(lhs, g.ty[col_at], NN), 0)
        ready = [beside, behind, ahead, behind_beside, ahead_beside]
        for block in ready:
            give(block)
        arrived(5, far, 0)
        arrived(6, far, 1)
        give(far)
        arrived(7, far_beside, 0)
        arrived(8, far_beside, 1)
        give(far_beside)

    def first_fill(p):
        for copy in p.edge_copies:
            copy.wait_recv()
        fill_wide(p, 0, HALF_FILL)

    def rest_of_conv(p):
        return (lambda: fill_wide(p, HALF_FILL, 17), lambda: convolve(p, 0, 5), lambda: convolve(p, 5, 8))

    def regroup(p):
        def one(x):
            p.raw[pl.ds(aligned(x * 32 + 32, 32), 32), :] = grid_row(x).astype(bf16)

        one(0)
        one(63)
        p.row_copies = send_halo_rows(p)
        loop(62, lambda x: one(x + 1))

    def widen_now(p):
        p.edge_copies = widen(p, p.row_copies)

    def place(slot, value):
        for half in range(2):
            g.stage[pl.ds(aligned(half * 2048 + slot * 256, 256), 256), :] = value[:, 128 * half : 128 * half + 128]

    def placed(slot):
        return jnp.concatenate(
            [g.stage[pl.ds(aligned(half * 2048 + slot * 256, 256), 256), :] for half in range(2)], axis=1
        )

    def grid_row(x):
        return jnp.concatenate([g.stage[pl.ds(2048 * half + x, 32, stride=64), :] for half in range(2)], axis=1)

    def put_grid_row(x, value):
        for half in range(2):
            g.stage[pl.ds(2048 * half + x, 32, stride=64), :] = value[:, 128 * half : 128 * half + 128]

    low = lax.broadcasted_iota(jnp.int32, (16, 128), 1) < 64
    quarter = lax.rem(col_at, 4) * 32
    back_shift = lax.rem(128 - quarter, 128)

    def flatten_modes(p):
        for part in range(2):
            p.flat[32 * part : 32 * part + 32] = jnp.concatenate(
                [p.modes[pl.ds(4 * part + kl, 32, stride=8), :][:, :32] for kl in range(4)], axis=1
            )

    def pack_weight(i):
        for part in range(2):
            g.packed[part, i] = jnp.concatenate([g.weight[kl, part, i].astype(f32) for kl in range(4)], axis=1)

    def spread_mix(parts):
        lane = lax.broadcasted_iota(jnp.int32, (32, 128), 1)
        mine = (lane >= quarter) & (lane < quarter + 32)
        for part, value in enumerate(parts):
            for kl in range(4):
                moved = pltpu.roll(value, (quarter + 128 - 32 * kl) & 127, 1)
                at = 128 * part + 32 * kl
                g.mix[at : at + 32, :] = jnp.where(mine, moved, 0.0)

    def cover_field():
        loads[0].wait()
        for i in range(n_col):
            place(i, g.vbuf[i].astype(f32))

        regroup(first)
        g.cot[...] = cot_ref[...].astype(f32)
        spread_taps(first, False)
        g.bias[...] = column(bias_ref)
        g.proj[...] = column(proj_ref)
        loads[3].wait()
        loop(32, pack_weight)
        loads[1].wait()
        loads[2].wait()

    def column(ref):
        diagonal = lax.broadcasted_iota(jnp.int32, (32, 32), 0) == lax.broadcasted_iota(jnp.int32, (32, 32), 1)
        value = jnp.sum(jnp.where(diagonal, jnp.broadcast_to(ref[...], (32, 32)), 0.0), axis=1, keepdims=True)
        return jnp.broadcast_to(value, (32, 256))

    to_modes(first, lambda i: v_ref.at[i], False, cover_field, lambda: widen_now(first))
    flatten_modes(first)

    def add_channel(i, sums):
        real, imag = sums
        s_re = first.flat[pl.ds(i, 1), :]
        s_im = first.flat[pl.ds(32 + i, 1), :]
        w_re = g.packed[0, i]
        w_im = g.packed[1, i]
        return (real + (w_re * s_re - w_im * s_im), imag + (w_re * s_im + w_im * s_re))

    zero = jnp.zeros((32, 128), f32)
    real, imag = lax.fori_loop(0, 32, add_channel, (zero, zero))
    frequency = row_at * 4 + lax.broadcasted_iota(jnp.int32, (32, 128), 1) // 32
    factor = jnp.where(frequency == 0, 1.0, 2.0) * scale
    spread_mix([value.astype(bf16).astype(f32) * factor for value in (real, imag)])

    back = Exchange("col", col_at, n_col, lambda i: second.snd1.at[i], second.buf1, second.s1, second.r1, False)

    def activate(slot, cells, d):
        conv = placed(slot)
        rounded = []
        for ch in range(4):
            channel = slot * 4 + ch
            rows = slice(64 * ch, 64 * ch + 64)
            bias = jnp.broadcast_to(g.bias[pl.ds(channel, 1), :], (64, 256))
            proj = jnp.broadcast_to(g.proj[pl.ds(channel, 1), :], (64, 256))
            pre = conv[rows] + cells[rows] + bias
            cdf = 0.5 * (1.0 + lax.erf(pre * math.sqrt(0.5)))
            pdf = jnp.exp(-0.5 * pre * pre) * (1.0 / math.sqrt(TWO_PI))
            grad = (proj * g.cot[...]) * (cdf + pre * pdf)
            rounded.append(grad.astype(bf16))
            second.snd1[slot, 64 * ch : 64 * ch + 64] = rounded[ch]
            at = pl.ds(aligned(channel * 8, 8), 8)
            g.bias_rows[at, :] = jnp.sum(grad.reshape(8, 8, 256), axis=0)
            g.proj_rows[at, :] = jnp.sum(((pre * cdf) * g.cot[...]).reshape(8, 8, 256), axis=0)
        if not isinstance(d, int):
            back.start(n_col - d)
        place(slot, jnp.concatenate(rounded, axis=0).astype(f32))

    to_grid(first, lambda: first_fill(first), rest_of_conv(first), activate)

    piece = 80 // owners

    def cover_grad():
        regroup(second)
        of_channel = (lax.broadcasted_iota(jnp.int32, (32, 256), 1) // 8) == lax.broadcasted_iota(
            jnp.int32, (32, 256), 0
        )
        gather = jnp.where(of_channel, 1.0, 0.0)
        for at, rows in ((0, g.bias_rows), (32, g.proj_rows)):
            g.sums[at : at + 32] = lax.dot_general(
                gather, rows[...], NN, precision=HIGH, preferred_element_type=f32
            )
        g.sums[64:128] = jnp.zeros((64, 256), f32)
        g.outer[...] = jnp.zeros_like(g.outer)

        def block(t):
            rows = first.wide[pl.ds(aligned(t * 768, 16), 960), :]
            grads = second.raw[pl.ds(aligned(t * 256 + 32, 32), 256), :]
            g.outer[...] += dot(rows, grads, NT)

        loop(8, block)
        lane = lax.broadcasted_iota(jnp.int32, (96, 128), 1)
        taps = []
        for a in range(3):
            total = jnp.zeros((96, 128), f32)
            for x in range(8):
                here = g.outer[96 * (x + a) : 96 * (x + a) + 96, 128 * (x // 4) : 128 * (x // 4) + 128]
                total = total + (pltpu.roll(here, 128 - 32 * (x % 4), 1) if x % 4 else here)
            taps.append(jnp.where(lane < 32, total, 0.0))
        taps = jnp.concatenate(taps, axis=0)
        packed = taps[0:72]
        for q in range(1, 4):
            packed = packed + pltpu.roll(taps[72 * q : 72 * q + 72], 32 * q, 1)
        lanes_sum = lax.dot_general(
            jnp.ones((8, 256), f32), g.sums[...], NT, precision=HIGH, preferred_element_type=f32
        )
        g.part[...] = (jnp.concatenate([packed, lanes_sum], axis=0) * scale).reshape(owners, piece, 128)
        for t in range(owners):

            @pl.when(row_at != t)
            def _():
                push(g.part.at[t], g.got_row.at[row_at], g.row_s.at[t], g.row_r, "row", t).start()

        spread_taps(second, True)

    def sum_rows():
        @pl.when(row_at < owners)
        def _():
            g.got_row[row_at] = g.part[row_at]
            Exchange("row", row_at, n_row, None, g.got_row, g.row_s.at[0], g.row_r, True).take_all()
            g.sum_row[...] = jnp.sum(g.got_row[...], axis=0)
            g.got_col[col_at] = g.sum_row[...]
            Exchange("col", col_at, n_col, lambda i: g.sum_row, g.got_col, g.col_s, g.col_r, True).start_all()

    def sum_cols():
        @pl.when(row_at < owners)
        def _():
            sums = Exchange("col", col_at, n_col, lambda i: g.sum_row, g.got_col, g.col_s, g.col_r, True)
            sums.take_all()
            sums.sent()
            g.total[...] = jnp.sum(g.got_col[...], axis=0)
            g.got_all[row_at] = g.total[...]

            def send(d):
                peer = (row_at + d) & (n_row - 1)
                push(g.total, g.got_all.at[row_at], g.all_s, g.all_r.at[row_at], "row", peer).start()

            each(n_row, send)

    def cover_rows_back():
        widen_now(second)
        sum_rows()

    def cover_rows_out():
        first_fill(second)
        sum_cols()

    def write_out(slot, cells, d):
        at = pl.ds(aligned(slot * 256, 256), 256)
        g.out[at, :] = placed(slot) + cells
        pltpu.make_async_copy(g.out.at[at], out_ref.at[at], g.out_s).start()

    to_modes(second, lambda i: second.snd1.at[i], True, cover_grad, cover_rows_back)
    own_mode = lax.broadcasted_iota(jnp.int32, (256, 128), 0) & 3
    second.modes[...] = second.modes[...] * jnp.where(row_at * 4 + own_mode == 0, 1.0, 2.0)
    flatten_modes(second)
    g_re = second.flat[0:32]
    g_im = second.flat[32:64]

    def one_channel(i):
        w_re = g.packed[0, i]
        w_im = g.packed[1, i]
        g.mixed_back[pl.ds(i, 1), :] = jnp.sum(w_re * g_re + w_im * g_im, axis=0, keepdims=True)
        g.mixed_back[pl.ds(32 + i, 1), :] = jnp.sum(w_re * g_im - w_im * g_re, axis=0, keepdims=True)

    loop(32, one_channel)
    spread_mix([g.mixed_back[32 * part : 32 * part + 32].astype(bf16).astype(f32) * scale for part in range(2)])
    to_grid(second, cover_rows_out, rest_of_conv(second), write_out)

    modes_ref[0] = first.modes[...]
    modes_ref[1] = second.modes[...]
    for t in range(owners):

        @pl.when(row_at != t)
        def _():
            arrived = push(g.part.at[t], g.got_all.at[t], g.row_s.at[t], g.all_r.at[t], "row", t)
            arrived.wait_recv()
            arrived.wait_send()

    @pl.when(row_at < owners)
    def _():
        Exchange("row", row_at, n_row, None, g.got_row, g.all_s, g.row_r, True).sent()

    small_ref[...] = g.got_all[...].reshape(80, 128)
    for wait in pending:
        wait()
    pltpu.make_async_copy(g.out, out_ref, g.out_s).wait()


def outputs_kernel(cells_ref, modes_ref, small_ref, out_ref, gspec_ref, conv_ref, bias_ref, proj_ref, weight, cells, sems):
    copies = []
    loads = []
    parts = [pl.ds(512 * q, 512) for q in range(4)]
    for q, at in enumerate(parts):
        loads.append(pltpu.make_async_copy(cells_ref.at[at], cells.at[at], sems.at[q]))
        loads[q].start()
    for kl in range(4):
        g_re = modes_ref[pl.ds(256 + kl, 32, stride=8), :][:, :32]
        g_im = modes_ref[pl.ds(260 + kl, 32, stride=8), :][:, :32]
        for i in range(32):
            s_re = modes_ref[8 * i + kl : 8 * i + kl + 1, :][:, :32]
            s_im = modes_ref[8 * i + 4 + kl : 8 * i + 5 + kl, :][:, :32]
            weight[kl, 0, i] = g_re * s_re + g_im * s_im
            weight[kl, 1, i] = g_im * s_re - g_re * s_im
        copies.append(pltpu.make_async_copy(weight.at[kl], gspec_ref.at[kl], sems.at[4 + kl]))
        copies[-1].start()
        loads[kl].wait()
        copies.append(pltpu.make_async_copy(cells.at[parts[kl]], out_ref.at[parts[kl]], sems.at[8 + kl]))
        copies[-1].start()
    for q in range(4):
        rows = small_ref[0:72]
        conv_ref[72 * q : 72 * q + 72] = (pltpu.roll(rows, 128 - 32 * q, 1) if q else rows)[:, :32]
    rows = small_ref[72:80]
    bias_ref[...] = rows[0:1, :32]
    proj_ref[...] = pltpu.roll(rows, 96, 1)[0:1, :32]
    for copy in copies:
        copy.wait()


def per_device(n_row, n_col, ocean_field, cotangent, conv_weight, conv_bias, projection, mode_weight):
    chans, rows_dev, cols_dev = ocean_field.shape
    ky_dev = mode_weight.shape[0]
    kx_all = mode_weight.shape[4] * n_col
    owners = min(10, n_row)
    ty, tx = (jnp.asarray(t) for t in tables(n_row, n_col, ky_dev, rows_dev, cols_dev, kx_all))
    vmem = pl.BlockSpec(memory_space=pltpu.VMEM)
    hbm = pl.BlockSpec(memory_space=pl.ANY)
    one = pass_scratch(n_row, n_col)
    scratch = list(one.values()) * 2 + list(common_scratch(n_row, n_col, rows_dev * n_row, owners).values())
    cells, modes, small = pl.pallas_call(
        functools.partial(step_kernel, n_row, n_col, owners),
        out_shape=[
            jax.ShapeDtypeStruct((chans * rows_dev, cols_dev), jnp.float32),
            jax.ShapeDtypeStruct((2, 256, 128), jnp.float32),
            jax.ShapeDtypeStruct((80, 128), jnp.float32),
        ],
        in_specs=[hbm, vmem, vmem, vmem, vmem, hbm, hbm, hbm],
        out_specs=[hbm, vmem, vmem],
        scratch_shapes=scratch,
        compiler_params=pltpu.CompilerParams(
            collective_id=0, has_side_effects=True, vmem_limit_bytes=VMEM_BYTES
        ),
        name="layer_step",
    )(
        ocean_field.reshape(n_col, 256, cols_dev),
        cotangent,
        conv_weight.reshape(9 * chans, chans),
        conv_bias.reshape(1, chans),
        projection.reshape(1, chans),
        mode_weight,
        ty,
        tx,
    )
    grad_input, grad_spec, grad_conv, grad_bias, grad_proj = pl.pallas_call(
        outputs_kernel,
        out_shape=[
            jax.ShapeDtypeStruct((chans * rows_dev, cols_dev), jnp.float32),
            jax.ShapeDtypeStruct(mode_weight.shape, jnp.float32),
            jax.ShapeDtypeStruct((9 * chans, chans), jnp.float32),
            jax.ShapeDtypeStruct((1, chans), jnp.float32),
            jax.ShapeDtypeStruct((1, chans), jnp.float32),
        ],
        in_specs=[hbm, vmem, vmem],
        out_specs=[hbm, hbm, vmem, vmem, vmem],
        scratch_shapes=[
            pltpu.VMEM(mode_weight.shape, jnp.float32),
            pltpu.VMEM((chans * rows_dev, cols_dev), jnp.float32),
            pltpu.SemaphoreType.DMA((12,)),
        ],
        compiler_params=pltpu.CompilerParams(vmem_limit_bytes=VMEM_BYTES),
        name="layer_outputs",
    )(cells, modes.reshape(512, 128), small)
    return (
        grad_input.reshape(ocean_field.shape),
        grad_spec,
        grad_conv.reshape(conv_weight.shape),
        grad_bias.reshape(chans),
        grad_proj.reshape(chans),
    )


def solution(mesh):
    placed = (
        P(None, "row", "col"),
        P("row", "col"),
        P(),
        P(),
        P(),
        P("row", None, None, None, "col"),
    )
    return jax.shard_map(
        functools.partial(per_device, mesh.shape["row"], mesh.shape["col"]),
        mesh=mesh,
        in_specs=placed,
        out_specs=(P(None, "row", "col"), P("row", None, None, None, "col"), P(), P(), P()),
        check_vma=False,
    )
```

```python
import functools
import math

import jax
import jax.numpy as jnp
import ml_dtypes
import numpy as np
from jax import lax
from jax.experimental import pallas as pl
from jax.experimental.pallas import tpu as pltpu
from jax.sharding import PartitionSpec as P

TWO_PI = 2.0 * math.pi
HIGH = lax.Precision.HIGHEST
VMEM_BYTES = 56 * 1024 * 1024


def angle_pair(products, period):
    angles = (products % period).astype(np.float32) * np.float32(TWO_PI / period)
    return (np.cos(angles).astype(ml_dtypes.bfloat16), np.sin(angles).astype(ml_dtypes.bfloat16))


def tables(n_row, n_col, ky_dev, rows_dev, cols_dev, kx_all):
    modes, nx, ny = (ky_dev * n_row, rows_dev * n_row, cols_dev * n_col)
    cosine, sine = angle_pair(np.arange(modes)[:, None] * np.arange(ny)[None, :], ny)
    ty = np.stack([cosine.reshape(n_row, ky_dev, ny), -sine.reshape(n_row, ky_dev, ny)], axis=1)
    ty = ty.reshape(2 * modes, n_col, cols_dev).transpose(1, 0, 2)
    ids = np.arange(kx_all)
    freqs = np.where(ids < modes, ids, ids - 2 * modes) % nx
    cosine, sine = angle_pair(freqs[:, None] * np.arange(nx)[None, :], nx)
    return np.ascontiguousarray(ty), np.concatenate([cosine, sine], axis=0)


NT = (((1,), (1,)), ((), ()))
NN = (((1,), (0,)), ((), ()))
TN = (((0,), (0,)), ((), ()))


def dot(a, b, dims):
    return lax.dot_general(a, b, dims, preferred_element_type=jnp.float32)


def push(src, dst, send_sem, recv_sem, axis, peer):
    return pltpu.make_async_remote_copy(
        src_ref=src,
        dst_ref=dst,
        send_sem=send_sem,
        recv_sem=recv_sem,
        device_id={axis: peer},
        device_id_type=pl.DeviceIdType.MESH,
    )


class Exchange:
    def __init__(self, axis, me, size, source, slots, send_sem, recv_sem, shared):
        (self.axis, self.me, self.size, self.source, self.slots) = (axis, me, size, source, slots)
        (self.send_sem, self.recv_sem, self.shared) = (send_sem, recv_sem, shared)

    def peer(self, step):
        return (self.me + step) & (self.size - 1)

    def copy(self, step, src, dst, peer):
        recv_sem = self.recv_sem if self.shared else self.recv_sem.at[step]
        return push(src, dst, self.send_sem, recv_sem, self.axis, peer)

    def start(self, step):
        peer = self.peer(step)
        self.copy(step, self.source(peer), self.slots.at[self.me], peer).start()

    def start_all(self):
        each(self.size, self.start)

    def take(self, step):
        origin = (self.me - step) & (self.size - 1)
        self.copy(step, self.slots.at[origin], self.slots.at[origin], origin).wait_recv()
        return origin

    def every(self):
        rest = self.slots.at[pl.ds(0, self.size - 1)]
        return self.copy(1, rest, rest, self.peer(1))

    def take_all(self):
        self.every().wait_recv()

    def sent(self):
        self.every().wait_send()


def each(size, body):
    def step(index, carry):
        body(index)
        return carry

    lax.fori_loop(1, size, step, 0)


def part_swap(value, sign):
    rows = value.shape[0]
    is_real = (lax.broadcasted_iota(jnp.int32, value.shape, 0) & 4) == 0
    after = pltpu.roll(value, rows - 4, 0)
    before = pltpu.roll(value, 4, 0)
    return jnp.where(is_real, sign * after, -sign * before)


class Group:
    def __init__(self, names, refs):
        for name, ref in zip(names, refs):
            setattr(self, name, ref)


def aligned(value, to):
    return pl.multiple_of(value, to)


def pass_scratch(n_row, n_col):
    bf16, f32 = (jnp.bfloat16, jnp.float32)
    dma = pltpu.SemaphoreType.DMA
    found = dict(
        snd1=pltpu.VMEM((n_col, 256, 256), bf16),
        buf1=pltpu.VMEM((n_col, 256, 256), bf16),
        snd3=pltpu.VMEM((n_row, 16, 128), bf16),
        rcv3=pltpu.VMEM((n_row, 16, 128), bf16),
        snd5=pltpu.VMEM((2, 32, 128), bf16),
        rcv5=pltpu.VMEM((n_col, 32, 128), bf16),
        modes=pltpu.VMEM((256, 128), f32),
        flat=pltpu.VMEM((64, 128), f32),
        snd7=pltpu.VMEM((n_col, 32, 128), bf16),
        rcv7=pltpu.VMEM((n_col, 32, 128), bf16),
        snd9=pltpu.VMEM((n_row, 16, 128), bf16),
        rcv9=pltpu.VMEM((n_row, 16, 128), bf16),
        rcv10=pltpu.VMEM((n_col, 256, 256), bf16),
        raw=pltpu.VMEM((68 * 32, 256), bf16),
        halo=pltpu.VMEM((2, 32, 256), bf16),
        edge_out=pltpu.VMEM((2, 16, 68 * 32), bf16),
        edge_in=pltpu.VMEM((2, 16, 68 * 32), bf16),
        wide=pltpu.VMEM((68 * 96, 256), bf16),
        taps=pltpu.VMEM((256, 1024), bf16),
        own=dma,
        hs=dma((2,)),
        hr=dma((2,)),
        es=dma((2,)),
        er=dma((2,)),
    )
    for step, size in ((1, n_col), (3, n_row), (5, n_col), (7, n_col), (9, n_row), (10, n_col)):
        found["s%d" % step] = dma((9,)) if step == 10 else dma
        found["r%d" % step] = dma((9,)) if step == 10 else dma((size,)) if step == 1 else dma
    return found


def common_scratch(n_row, n_col, nx, owners):
    bf16, f32 = (jnp.bfloat16, jnp.float32)
    dma = pltpu.SemaphoreType.DMA
    piece = 80 // owners
    return dict(
        vbuf=pltpu.VMEM((n_col, 256, 256), bf16),
        ty=pltpu.VMEM((n_col, 8 * n_row, 256), bf16),
        tx=pltpu.VMEM((512, nx), bf16),
        weight=pltpu.VMEM((4, 2, 32, 32, 32), bf16),
        stage=pltpu.VMEM((4096, 128), f32),
        bias=pltpu.VMEM((32, 256), f32),
        proj=pltpu.VMEM((32, 256), f32),
        bias_rows=pltpu.VMEM((256, 256), f32),
        proj_rows=pltpu.VMEM((256, 256), f32),
        cot=pltpu.VMEM((64, 256), f32),
        out=pltpu.VMEM((2048, 256), f32),
        out_s=dma,
        acc=pltpu.VMEM((8 * n_row, 256), f32),
        rows_x=pltpu.VMEM((32, nx), bf16),
        mix=pltpu.VMEM((256, 128), f32),
        packed=pltpu.VMEM((2, 32, 32, 128), f32),
        mixed_back=pltpu.VMEM((64, 128), f32),
        outer=pltpu.VMEM((960, 256), f32),
        sums=pltpu.VMEM((128, 256), f32),
        part=pltpu.VMEM((owners, piece, 128), f32),
        got_row=pltpu.VMEM((n_row, piece, 128), f32),
        sum_row=pltpu.VMEM((piece, 128), f32),
        got_col=pltpu.VMEM((n_col, piece, 128), f32),
        total=pltpu.VMEM((piece, 128), f32),
        got_all=pltpu.VMEM((owners, piece, 128), f32),
        load=dma((4,)),
        row_s=dma((owners,)),
        row_r=dma,
        col_s=dma,
        col_r=dma,
        all_s=dma,
        all_r=dma((owners,)),
    )


def step_kernel(n_row, n_col, owners, *refs):
    (v_ref, cot_ref, taps_ref, bias_ref, proj_ref, w_hbm, ty_hbm, tx_hbm, out_ref, modes_ref, small_ref, *rest) = refs
    nx = 64 * n_row
    names = list(pass_scratch(n_row, n_col))
    first = Group(names, rest[: len(names)])
    second = Group(names, rest[len(names) : 2 * len(names)])
    g = Group(list(common_scratch(n_row, n_col, nx, owners)), rest[2 * len(names) :])
    row_at = lax.axis_index("row")
    col_at = lax.axis_index("col")
    pairs = n_row // 2
    scale = 1.0 / math.sqrt((64 * n_row) * (256 * n_col))
    bf16, f32 = (jnp.bfloat16, jnp.float32)
    pending = []

    loads = [
        pltpu.make_async_copy(v_ref, g.vbuf, g.load.at[0]),
        pltpu.make_async_copy(ty_hbm, g.ty, g.load.at[1]),
        pltpu.make_async_copy(tx_hbm, g.tx, g.load.at[2]),
        pltpu.make_async_copy(w_hbm, g.weight, g.load.at[3]),
    ]
    for load in loads:
        load.start()
    barrier = pltpu.get_barrier_semaphore()
    each(n_col, lambda d: pl.semaphore_signal(
        barrier, inc=1, device_id={"col": (col_at + d) & (n_col - 1)}, device_id_type=pl.DeviceIdType.MESH))
    each(n_row, lambda d: pl.semaphore_signal(
        barrier, inc=1, device_id={"row": (row_at + d) & (n_row - 1)}, device_id_type=pl.DeviceIdType.MESH))
    pl.semaphore_wait(barrier, n_col - 1 + n_row - 1)

    def loop(size, body):
        def step(index, carry):
            body(index)
            return carry

        lax.fori_loop(0, size, step, 0)

    def send_halo_rows(p):
        up = lax.rem(row_at + n_row - 1, n_row)
        down = lax.rem(row_at + 1, n_row)
        copies = [
            push(p.raw.at[pl.ds(32, 32)], p.halo.at[1], p.hs.at[0], p.hr.at[0], "row", up),
            push(p.raw.at[pl.ds(64 * 32, 32)], p.halo.at[0], p.hs.at[1], p.hr.at[1], "row", down),
        ]
        for copy in copies:
            copy.start()
            pending.append(copy.wait_send)
        return copies

    def widen(p, row_copies):
        for copy in row_copies:
            copy.wait_recv()
        above = jnp.where(row_at > 0, 1.0, 0.0)
        below = jnp.where(row_at < n_row - 1, 1.0, 0.0)
        p.raw[0:32] = (p.halo[0].astype(f32) * above).astype(bf16)
        p.raw[65 * 32 : 66 * 32] = (p.halo[1].astype(f32) * below).astype(bf16)
        p.raw[66 * 32 : 68 * 32] = jnp.zeros((64, 256), bf16)
        row = lax.broadcasted_iota(jnp.int32, (32, 256), 0)
        lane = lax.broadcasted_iota(jnp.int32, (32, 256), 1)
        pick = ((row == 0) & (lane == 0)) | ((row == 16) & (lane == 255))
        edges = dot(jnp.where(pick, 1.0, 0.0).astype(bf16), p.raw[...], NT)
        p.edge_out[0] = edges[0:16].astype(bf16)
        p.edge_out[1] = edges[16:32].astype(bf16)
        left = lax.rem(col_at + n_col - 1, n_col)
        right = lax.rem(col_at + 1, n_col)
        copies = [
            push(p.edge_out.at[0], p.edge_in.at[1], p.es.at[0], p.er.at[0], "col", left),
            push(p.edge_out.at[1], p.edge_in.at[0], p.es.at[1], p.er.at[1], "col", right),
        ]
        for copy in copies:
            copy.start()
            pending.append(copy.wait_send)
        return copies

    def fill_wide(p, start, stop):
        row = lax.broadcasted_iota(jnp.int32, (16, 128), 0)
        lane = lax.broadcasted_iota(jnp.int32, (16, 128), 1)
        put_left = jnp.where((row == 0) & (lane == 0) & (col_at > 0), 1.0, 0.0).astype(bf16)
        put_right = jnp.where((row == 0) & (lane == 127) & (col_at < n_col - 1), 1.0, 0.0).astype(bf16)
        lanes = lax.broadcasted_iota(jnp.int32, (128, 128), 1)

        def chunk(q):
            here = p.raw[pl.ds(aligned(q * 128, 128), 128), :].astype(f32)
            from_left = dot(p.edge_in[0, :, pl.ds(aligned(q * 128, 128), 128)], put_left, TN)
            from_right = dot(p.edge_in[1, :, pl.ds(aligned(q * 128, 128), 128)], put_right, TN)
            before = pltpu.roll(here, 1, 1)
            after = pltpu.roll(here, 255, 1)
            before = jnp.concatenate([jnp.where(lanes == 0, from_left, before[:, :128]), before[:, 128:]], axis=1)
            after = jnp.concatenate([after[:, :128], jnp.where(lanes == 127, from_right, after[:, 128:])], axis=1)
            for x in range(4):
                for b, value in enumerate((before, here, after)):
                    base = aligned(q * 384 + 96 * x + 32 * b, 32)
                    p.wide[pl.ds(base, 32), :] = value[32 * x : 32 * x + 32].astype(bf16)

        loop(stop - start, lambda q: chunk(q + start))

    def spread_taps(p, turned):
        row = lax.broadcasted_iota(jnp.int32, (32, 1024), 0)
        lane = lax.broadcasted_iota(jnp.int32, (32, 1024), 1)
        padded = jnp.zeros((32, 1024), f32)
        for m in range(9):
            source = 8 - m if turned else m
            spot = jnp.where(lane == row + 32 * m, 1.0, 0.0).astype(bf16)
            padded = padded + dot(taps_ref[32 * source : 32 * source + 32, :], spot, NN if turned else TN)
        for x in range(8):
            p.taps[32 * x : 32 * x + 32, :] = (pltpu.roll(padded, 96 * x, 1) if x else padded).astype(bf16)

    def convolve(p, start, stop):
        def block(t):
            rows = p.wide[pl.ds(aligned(t * 768, 16), 1024), :]
            result = dot(p.taps[...], rows, NN)
            for x in range(8):
                put_grid_row(8 * t + x, result[32 * x : 32 * x + 32])

        loop(stop - start, lambda t: block(t + start))

    def to_modes(p, source, started, cover, cover_rows):
        own = pltpu.make_async_copy(source(col_at), p.buf1.at[col_at], p.own)
        own.start()
        fields = Exchange("col", col_at, n_col, source, p.buf1, p.s1, p.r1, False)
        if not started:
            fields.start_all()
        pending.append(fields.sent)
        cover()
        own.wait()
        g.acc[...] = dot(g.ty[col_at], p.buf1[col_at], NT)

        def add_block(d):
            origin = fields.take(d)
            g.acc[...] += dot(g.ty[origin], p.buf1[origin], NT)

        each(n_col, add_block)
        whole = g.acc[...]
        upper = whole[:, :128].reshape(n_row, 8, 128)
        lower = whole[:, 128:].reshape(n_row, 8, 128)
        p.snd3[...] = jnp.concatenate([upper, lower], axis=1).astype(bf16)
        rows = Exchange("row", row_at, n_row, lambda i: p.snd3.at[i], p.rcv3, p.s3, p.r3, True)
        rows.start_all()
        pending.append(rows.sent)
        p.rcv3[row_at] = p.snd3[row_at]
        cover_rows()
        rows.take_all()
        for s in range(pairs):
            one = p.rcv3[2 * s].astype(f32)
            two = p.rcv3[2 * s + 1].astype(f32)
            even = jnp.where(low, one, pltpu.roll(two, 64, 1))
            odd = jnp.where(low, pltpu.roll(one, 64, 1), two)
            g.rows_x[0:16, 128 * s : 128 * s + 128] = even.astype(bf16)
            g.rows_x[16:32, 128 * s : 128 * s + 128] = odd.astype(bf16)
        both = dot(g.rows_x[...], g.tx[...], NT)
        coeffs = (both[:, :256] + part_swap(both[:, 256:], 1.0)) * scale
        coeffs = jnp.concatenate([coeffs[0:8], coeffs[16:24], coeffs[8:16], coeffs[24:32]], axis=0)
        p.snd5[0] = coeffs[:, :128].astype(bf16)
        p.snd5[1] = coeffs[:, 128:].astype(bf16)
        parts = Exchange("col", col_at, n_col, lambda i: p.snd5.at[i // 4], p.rcv5, p.s5, p.r5, True)
        parts.start_all()
        pending.append(parts.sent)
        p.rcv5[col_at] = p.snd5[col_at // 4]
        parts.take_all()
        for i in range(n_col):
            p.modes[32 * i : 32 * i + 32] = pltpu.roll(p.rcv5[i].astype(f32), back_shift, 1)

    def to_grid(p, cover_rows, cover_cells, use):
        for i in range(n_col):
            for odd_channel in range(2):
                upper = g.mix[pl.ds(4 * i + odd_channel, 8, stride=32), :]
                lower = g.mix[pl.ds(4 * i + 2 + odd_channel, 8, stride=32), :]
                p.snd7[i, 16 * odd_channel : 16 * odd_channel + 16] = jnp.concatenate(
                    [upper, lower], axis=0
                ).astype(bf16)
        parts = Exchange("col", col_at, n_col, lambda i: p.snd7.at[i], p.rcv7, p.s7, p.r7, True)
        parts.start_all()
        pending.append(parts.sent)
        p.rcv7[col_at] = p.snd7[col_at]
        parts.take_all()
        halves = [sum(p.rcv7[4 * h + q].astype(f32) for q in range(4)) for h in range(2)]
        mixed = jnp.concatenate(halves, axis=1)
        swapped = part_swap(mixed, -1.0)
        operand = jnp.concatenate([mixed, swapped], axis=1).astype(bf16)
        by_rows = dot(operand, g.tx[...], NN)
        for s in range(pairs):
            even = by_rows[0:16, 128 * s : 128 * s + 128]
            odd = by_rows[16:32, 128 * s : 128 * s + 128]
            p.snd9[2 * s] = jnp.where(low, even, pltpu.roll(odd, 64, 1)).astype(bf16)
            p.snd9[2 * s + 1] = jnp.where(low, pltpu.roll(even, 64, 1), odd).astype(bf16)
        rows = Exchange("row", row_at, n_row, lambda i: p.snd9.at[i], p.rcv9, p.s9, p.r9, True)
        rows.start_all()
        pending.append(rows.sent)
        p.rcv9[row_at] = p.snd9[row_at]
        cover_rows()
        rows.take_all()
        got = p.rcv9[...].astype(f32)
        own_rows = jnp.concatenate(
            [got[:, :8].reshape(8 * n_row, 128), got[:, 8:].reshape(8 * n_row, 128)], axis=1
        )
        lhs = jnp.transpose(own_rows).astype(bf16)
        def at(dy, dz):
            return ((((col_at >> 1) + dy) & (n_col // 2 - 1)) << 1) | ((col_at + dz) & 1)

        ahead, behind, beside, far = (at(1, 0), at(n_col // 2 - 1, 0), at(0, 1), at(2, 0))
        behind_beside, ahead_beside, far_beside = (at(n_col // 2 - 1, 1), at(1, 1), at(2, 1))

        def send(kind, block, to, rows=None):
            ref = p.rcv10.at[block] if rows is None else p.rcv10.at[block, pl.ds(128 * rows, 128)]
            copy = push(ref, ref, p.s10.at[kind], p.r10.at[kind], "col", to)
            copy.start()
            pending.append(copy.wait_send)

        def arrived(kind, block, rows=None):
            ref = p.rcv10.at[block] if rows is None else p.rcv10.at[block, pl.ds(128 * rows, 128)]
            push(ref, ref, p.s10.at[kind], p.r10.at[kind], "col", beside).wait_recv()

        def give(block):
            use(block, dot(p.rcv10[block], g.ty[col_at], NN), (col_at - block) & (n_col - 1))

        p.rcv10[col_at] = lhs
        send(2, col_at, beside)
        send(0, col_at, ahead)
        send(1, col_at, behind)
        cover_cells[0]()
        arrived(2, beside)
        send(3, beside, ahead)
        send(4, beside, behind)
        arrived(0, behind)
        send(5, behind, ahead, 0)
        arrived(1, ahead)
        send(6, ahead, behind, 1)
        cover_cells[1]()
        arrived(3, behind_beside)
        send(7, behind_beside, ahead, 0)
        arrived(4, ahead_beside)
        send(8, ahead_beside, behind, 1)
        use(col_at, dot(lhs, g.ty[col_at], NN), 0)
        ready = [beside, behind, ahead, behind_beside, ahead_beside]
        for block in ready:
            give(block)
        arrived(5, far, 0)
        arrived(6, far, 1)
        give(far)
        arrived(7, far_beside, 0)
        arrived(8, far_beside, 1)
        give(far_beside)

    def first_fill(p):
        for copy in p.edge_copies:
            copy.wait_recv()
        fill_wide(p, 0, 17)

    def rest_of_conv(p):
        return (lambda: convolve(p, 0, 5), lambda: convolve(p, 5, 8))

    def regroup(p):
        def one(x):
            p.raw[pl.ds(aligned(x * 32 + 32, 32), 32), :] = grid_row(x).astype(bf16)

        one(0)
        one(63)
        p.row_copies = send_halo_rows(p)
        loop(62, lambda x: one(x + 1))

    def widen_now(p):
        p.edge_copies = widen(p, p.row_copies)

    def place(slot, value):
        for half in range(2):
            g.stage[pl.ds(aligned(half * 2048 + slot * 256, 256), 256), :] = value[:, 128 * half : 128 * half + 128]

    def placed(slot):
        return jnp.concatenate(
            [g.stage[pl.ds(aligned(half * 2048 + slot * 256, 256), 256), :] for half in range(2)], axis=1
        )

    def grid_row(x):
        return jnp.concatenate([g.stage[pl.ds(2048 * half + x, 32, stride=64), :] for half in range(2)], axis=1)

    def put_grid_row(x, value):
        for half in range(2):
            g.stage[pl.ds(2048 * half + x, 32, stride=64), :] = value[:, 128 * half : 128 * half + 128]

    low = lax.broadcasted_iota(jnp.int32, (16, 128), 1) < 64
    quarter = lax.rem(col_at, 4) * 32
    back_shift = lax.rem(128 - quarter, 128)

    def flatten_modes(p):
        for part in range(2):
            p.flat[32 * part : 32 * part + 32] = jnp.concatenate(
                [p.modes[pl.ds(4 * part + kl, 32, stride=8), :][:, :32] for kl in range(4)], axis=1
            )

    def pack_weight(i):
        for part in range(2):
            g.packed[part, i] = jnp.concatenate([g.weight[kl, part, i].astype(f32) for kl in range(4)], axis=1)

    def spread_mix(parts):
        lane = lax.broadcasted_iota(jnp.int32, (32, 128), 1)
        mine = (lane >= quarter) & (lane < quarter + 32)
        for part, value in enumerate(parts):
            for kl in range(4):
                moved = pltpu.roll(value, (quarter + 128 - 32 * kl) & 127, 1)
                at = 128 * part + 32 * kl
                g.mix[at : at + 32, :] = jnp.where(mine, moved, 0.0)

    def cover_field():
        loads[0].wait()
        for i in range(n_col):
            place(i, g.vbuf[i].astype(f32))

        regroup(first)
        g.cot[...] = cot_ref[...].astype(f32)
        spread_taps(first, False)
        g.bias[...] = column(bias_ref)
        g.proj[...] = column(proj_ref)
        loads[3].wait()
        loop(32, pack_weight)
        loads[1].wait()
        loads[2].wait()

    def column(ref):
        diagonal = lax.broadcasted_iota(jnp.int32, (32, 32), 0) == lax.broadcasted_iota(jnp.int32, (32, 32), 1)
        value = jnp.sum(jnp.where(diagonal, jnp.broadcast_to(ref[...], (32, 32)), 0.0), axis=1, keepdims=True)
        return jnp.broadcast_to(value, (32, 256))

    to_modes(first, lambda i: v_ref.at[i], False, cover_field, lambda: widen_now(first))
    flatten_modes(first)

    def add_channel(i, sums):
        real, imag = sums
        s_re = first.flat[pl.ds(i, 1), :]
        s_im = first.flat[pl.ds(32 + i, 1), :]
        w_re = g.packed[0, i]
        w_im = g.packed[1, i]
        return (real + (w_re * s_re - w_im * s_im), imag + (w_re * s_im + w_im * s_re))

    zero = jnp.zeros((32, 128), f32)
    real, imag = lax.fori_loop(0, 32, add_channel, (zero, zero))
    frequency = row_at * 4 + lax.broadcasted_iota(jnp.int32, (32, 128), 1) // 32
    factor = jnp.where(frequency == 0, 1.0, 2.0) * scale
    spread_mix([value.astype(bf16).astype(f32) * factor for value in (real, imag)])

    back = Exchange("col", col_at, n_col, lambda i: second.snd1.at[i], second.buf1, second.s1, second.r1, False)

    def activate(slot, cells, d):
        conv = placed(slot)
        rounded = []
        for ch in range(4):
            channel = slot * 4 + ch
            rows = slice(64 * ch, 64 * ch + 64)
            bias = jnp.broadcast_to(g.bias[pl.ds(channel, 1), :], (64, 256))
            proj = jnp.broadcast_to(g.proj[pl.ds(channel, 1), :], (64, 256))
            pre = conv[rows] + cells[rows] + bias
            cdf = 0.5 * (1.0 + lax.erf(pre * math.sqrt(0.5)))
            pdf = jnp.exp(-0.5 * pre * pre) * (1.0 / math.sqrt(TWO_PI))
            grad = (proj * g.cot[...]) * (cdf + pre * pdf)
            rounded.append(grad.astype(bf16))
            second.snd1[slot, 64 * ch : 64 * ch + 64] = rounded[ch]
            at = pl.ds(aligned(channel * 8, 8), 8)
            g.bias_rows[at, :] = jnp.sum(grad.reshape(8, 8, 256), axis=0)
            g.proj_rows[at, :] = jnp.sum(((pre * cdf) * g.cot[...]).reshape(8, 8, 256), axis=0)
        if not isinstance(d, int):
            back.start(n_col - d)
        place(slot, jnp.concatenate(rounded, axis=0).astype(f32))

    to_grid(first, lambda: first_fill(first), rest_of_conv(first), activate)

    piece = 80 // owners

    def cover_grad():
        regroup(second)
        of_channel = (lax.broadcasted_iota(jnp.int32, (32, 256), 1) // 8) == lax.broadcasted_iota(
            jnp.int32, (32, 256), 0
        )
        gather = jnp.where(of_channel, 1.0, 0.0)
        for at, rows in ((0, g.bias_rows), (32, g.proj_rows)):
            g.sums[at : at + 32] = lax.dot_general(
                gather, rows[...], NN, precision=HIGH, preferred_element_type=f32
            )
        g.sums[64:128] = jnp.zeros((64, 256), f32)
        g.outer[...] = jnp.zeros_like(g.outer)

        def block(t):
            rows = first.wide[pl.ds(aligned(t * 768, 16), 960), :]
            grads = second.raw[pl.ds(aligned(t * 256 + 32, 32), 256), :]
            g.outer[...] += dot(rows, grads, NT)

        loop(8, block)
        lane = lax.broadcasted_iota(jnp.int32, (96, 128), 1)
        taps = []
        for a in range(3):
            total = jnp.zeros((96, 128), f32)
            for x in range(8):
                here = g.outer[96 * (x + a) : 96 * (x + a) + 96, 128 * (x // 4) : 128 * (x // 4) + 128]
                total = total + (pltpu.roll(here, 128 - 32 * (x % 4), 1) if x % 4 else here)
            taps.append(jnp.where(lane < 32, total, 0.0))
        taps = jnp.concatenate(taps, axis=0)
        packed = taps[0:72]
        for q in range(1, 4):
            packed = packed + pltpu.roll(taps[72 * q : 72 * q + 72], 32 * q, 1)
        lanes_sum = lax.dot_general(
            jnp.ones((8, 256), f32), g.sums[...], NT, precision=HIGH, preferred_element_type=f32
        )
        g.part[...] = (jnp.concatenate([packed, lanes_sum], axis=0) * scale).reshape(owners, piece, 128)
        for t in range(owners):

            @pl.when(row_at != t)
            def _():
                push(g.part.at[t], g.got_row.at[row_at], g.row_s.at[t], g.row_r, "row", t).start()

        spread_taps(second, True)

    def sum_rows():
        @pl.when(row_at < owners)
        def _():
            g.got_row[row_at] = g.part[row_at]
            Exchange("row", row_at, n_row, None, g.got_row, g.row_s.at[0], g.row_r, True).take_all()
            g.sum_row[...] = jnp.sum(g.got_row[...], axis=0)
            g.got_col[col_at] = g.sum_row[...]
            Exchange("col", col_at, n_col, lambda i: g.sum_row, g.got_col, g.col_s, g.col_r, True).start_all()

    def sum_cols():
        @pl.when(row_at < owners)
        def _():
            sums = Exchange("col", col_at, n_col, lambda i: g.sum_row, g.got_col, g.col_s, g.col_r, True)
            sums.take_all()
            sums.sent()
            g.total[...] = jnp.sum(g.got_col[...], axis=0)
            g.got_all[row_at] = g.total[...]

            def send(d):
                peer = (row_at + d) & (n_row - 1)
                push(g.total, g.got_all.at[row_at], g.all_s, g.all_r.at[row_at], "row", peer).start()

            each(n_row, send)

    def cover_rows_back():
        widen_now(second)
        sum_rows()

    def cover_rows_out():
        first_fill(second)
        sum_cols()

    def write_out(slot, cells, d):
        at = pl.ds(aligned(slot * 256, 256), 256)
        g.out[at, :] = placed(slot) + cells
        pltpu.make_async_copy(g.out.at[at], out_ref.at[at], g.out_s).start()

    to_modes(second, lambda i: second.snd1.at[i], True, cover_grad, cover_rows_back)
    own_mode = lax.broadcasted_iota(jnp.int32, (256, 128), 0) & 3
    second.modes[...] = second.modes[...] * jnp.where(row_at * 4 + own_mode == 0, 1.0, 2.0)
    flatten_modes(second)
    g_re = second.flat[0:32]
    g_im = second.flat[32:64]

    def one_channel(i):
        w_re = g.packed[0, i]
        w_im = g.packed[1, i]
        g.mixed_back[pl.ds(i, 1), :] = jnp.sum(w_re * g_re + w_im * g_im, axis=0, keepdims=True)
        g.mixed_back[pl.ds(32 + i, 1), :] = jnp.sum(w_re * g_im - w_im * g_re, axis=0, keepdims=True)

    loop(32, one_channel)
    spread_mix([g.mixed_back[32 * part : 32 * part + 32].astype(bf16).astype(f32) * scale for part in range(2)])
    to_grid(second, cover_rows_out, rest_of_conv(second), write_out)

    modes_ref[0] = first.modes[...]
    modes_ref[1] = second.modes[...]
    for t in range(owners):

        @pl.when(row_at != t)
        def _():
            arrived = push(g.part.at[t], g.got_all.at[t], g.row_s.at[t], g.all_r.at[t], "row", t)
            arrived.wait_recv()
            arrived.wait_send()

    @pl.when(row_at < owners)
    def _():
        Exchange("row", row_at, n_row, None, g.got_row, g.all_s, g.row_r, True).sent()

    small_ref[...] = g.got_all[...].reshape(80, 128)
    for wait in pending:
        wait()
    pltpu.make_async_copy(g.out, out_ref, g.out_s).wait()


def outputs_kernel(cells_ref, modes_ref, small_ref, out_ref, gspec_ref, conv_ref, bias_ref, proj_ref, weight, cells, sems):
    copies = []
    loads = []
    parts = [pl.ds(512 * q, 512) for q in range(4)]
    for q, at in enumerate(parts):
        loads.append(pltpu.make_async_copy(cells_ref.at[at], cells.at[at], sems.at[q]))
        loads[q].start()
    for kl in range(4):
        g_re = modes_ref[pl.ds(256 + kl, 32, stride=8), :][:, :32]
        g_im = modes_ref[pl.ds(260 + kl, 32, stride=8), :][:, :32]
        for i in range(32):
            s_re = modes_ref[8 * i + kl : 8 * i + kl + 1, :][:, :32]
            s_im = modes_ref[8 * i + 4 + kl : 8 * i + 5 + kl, :][:, :32]
            weight[kl, 0, i] = g_re * s_re + g_im * s_im
            weight[kl, 1, i] = g_im * s_re - g_re * s_im
        copies.append(pltpu.make_async_copy(weight.at[kl], gspec_ref.at[kl], sems.at[4 + kl]))
        copies[-1].start()
        loads[kl].wait()
        copies.append(pltpu.make_async_copy(cells.at[parts[kl]], out_ref.at[parts[kl]], sems.at[8 + kl]))
        copies[-1].start()
    for q in range(4):
        rows = small_ref[0:72]
        conv_ref[72 * q : 72 * q + 72] = (pltpu.roll(rows, 128 - 32 * q, 1) if q else rows)[:, :32]
    rows = small_ref[72:80]
    bias_ref[...] = rows[0:1, :32]
    proj_ref[...] = pltpu.roll(rows, 96, 1)[0:1, :32]
    for copy in copies:
        copy.wait()


def per_device(n_row, n_col, ocean_field, cotangent, conv_weight, conv_bias, projection, mode_weight):
    chans, rows_dev, cols_dev = ocean_field.shape
    ky_dev = mode_weight.shape[0]
    kx_all = mode_weight.shape[4] * n_col
    owners = min(10, n_row)
    ty, tx = (jnp.asarray(t) for t in tables(n_row, n_col, ky_dev, rows_dev, cols_dev, kx_all))
    vmem = pl.BlockSpec(memory_space=pltpu.VMEM)
    hbm = pl.BlockSpec(memory_space=pl.ANY)
    one = pass_scratch(n_row, n_col)
    scratch = list(one.values()) * 2 + list(common_scratch(n_row, n_col, rows_dev * n_row, owners).values())
    cells, modes, small = pl.pallas_call(
        functools.partial(step_kernel, n_row, n_col, owners),
        out_shape=[
            jax.ShapeDtypeStruct((chans * rows_dev, cols_dev), jnp.float32),
            jax.ShapeDtypeStruct((2, 256, 128), jnp.float32),
            jax.ShapeDtypeStruct((80, 128), jnp.float32),
        ],
        in_specs=[hbm, vmem, vmem, vmem, vmem, hbm, hbm, hbm],
        out_specs=[hbm, vmem, vmem],
        scratch_shapes=scratch,
        compiler_params=pltpu.CompilerParams(
            collective_id=0, has_side_effects=True, vmem_limit_bytes=VMEM_BYTES
        ),
        name="layer_step",
    )(
        ocean_field.reshape(n_col, 256, cols_dev),
        cotangent,
        conv_weight.reshape(9 * chans, chans),
        conv_bias.reshape(1, chans),
        projection.reshape(1, chans),
        mode_weight,
        ty,
        tx,
    )
    grad_input, grad_spec, grad_conv, grad_bias, grad_proj = pl.pallas_call(
        outputs_kernel,
        out_shape=[
            jax.ShapeDtypeStruct((chans * rows_dev, cols_dev), jnp.float32),
            jax.ShapeDtypeStruct(mode_weight.shape, jnp.float32),
            jax.ShapeDtypeStruct((9 * chans, chans), jnp.float32),
            jax.ShapeDtypeStruct((1, chans), jnp.float32),
            jax.ShapeDtypeStruct((1, chans), jnp.float32),
        ],
        in_specs=[hbm, vmem, vmem],
        out_specs=[hbm, hbm, vmem, vmem, vmem],
        scratch_shapes=[
            pltpu.VMEM(mode_weight.shape, jnp.float32),
            pltpu.VMEM((chans * rows_dev, cols_dev), jnp.float32),
            pltpu.SemaphoreType.DMA((12,)),
        ],
        compiler_params=pltpu.CompilerParams(vmem_limit_bytes=VMEM_BYTES),
        name="layer_outputs",
    )(cells, modes.reshape(512, 128), small)
    return (
        grad_input.reshape(ocean_field.shape),
        grad_spec,
        grad_conv.reshape(conv_weight.shape),
        grad_bias.reshape(chans),
        grad_proj.reshape(chans),
    )


def solution(mesh):
    placed = (
        P(None, "row", "col"),
        P("row", "col"),
        P(),
        P(),
        P(),
        P("row", None, None, None, "col"),
    )
    return jax.shard_map(
        functools.partial(per_device, mesh.shape["row"], mesh.shape["col"]),
        mesh=mesh,
        in_specs=placed,
        out_specs=(P(None, "row", "col"), P("row", None, None, None, "col"), P(), P(), P()),
        check_vma=False,
    )
```
